32 devices in a mesh: dp: 8 (over z, y), tp: 4 (over x, core).
Axes of the slice: x: 2, y: 2, z: 4, core: 2. Of those that a mesh axis runs over, the one named last changes fastest.
Arguments:
- hidden: bfloat16 [16, 4096], P('dp'), may hold values from -6 to 6
- attention_norm_gain: bfloat16 [4096], replicated, may hold values from 0.5 to 1.5
- query_key_value_weight: bfloat16 [4096, 4, 1280], P('dp', 'tp'), may hold values from -0.09375 to 0.09375
- key_value_cache: bfloat16 [16, 2048, 4, 256], P('dp', None, 'tp'), may hold values from -6 to 6
- cache_fill_lengths: int32 [16], P('dp'), may hold values from 2 to 2048
- output_weight_frozen: bfloat16 [4, 1024, 4096], P('tp', None, 'dp'), may hold values from -0.09375 to 0.09375
- adapter_down_transposed: bfloat16 [64, 4, 1024], P(None, 'tp', 'dp'), may hold values from -0.09375 to 0.09375
- adapter_up_matrix: bfloat16 [64, 4, 1024], P(None, 'tp', 'dp'), may hold values from -0.75 to 0.75
- attention_rows: bfloat16 [4096, 4096], P('dp', 'tp'), may hold values from -6 to 6
- upstream: bfloat16 [4096, 4096], P('dp', 'tp'), may hold values from -6 to 6
- rewards: float32 [16], P('dp'), may hold values from 0 to 2
- prompt_group_index: int32 [16], P('dp'), may hold values from 0 to 3, as said below
- completion_live_lengths: int32 [16], P('dp'), may hold values from 1 to 256
Outputs:
- decoded: float32 [16, 4096], P('dp')
- adapted_output_rows: float32 [4096, 4096], P('dp', 'tp')
- grad_lora_a_t: float32 [64, 4, 1024], P(None, 'tp', 'dp')
- grad_lora_b: float32 [64, 4, 1024], P(None, 'tp', 'dp')
The draws below stay inside these ranges and needn't reach their ends.
Inputs may be any that keep to these rules, and one draw needn't show every extreme that they name: `prompt_group_index`: each prompt holds exactly 4 rollouts.
All inputs are finite; a program needn't handle non-finite values.
Results may differ from the reference program's by a relative error of at most 0.0041.
Values may be sent and summed in bfloat16 or wider, within the bound.
A program may use at most 128 MiB of HBM per device.

```python
import math
import jax
import jax.numpy as jnp
from jax import lax

MODEL_WIDTH = 4096
HD = 128
HEADS_TP = 8
ADAPTER_RANK = 64
CTX = 2048
GROUP = 4
COMP = 256
ROLLOUTS = 16
GROUP_QUERY_DIMS = 1024
QKV_TP = 1280
SHARD_WIDTH = 1024
ROWS = 4096
N_TP = 4


def draw_prompt_group_index(key, part):
    order = jax.random.permutation(key, ROLLOUTS)
    return (order // GROUP).astype(jnp.int32)


def draw_query_key_value_weight(key, part):
    noise_key = jax.random.fold_in(key, 101)
    weight = jax.random.truncated_normal(noise_key, -6.0, 6.0, (MODEL_WIDTH, N_TP, QKV_TP), jnp.float32) / math.sqrt(MODEL_WIDTH)
    return weight.astype(jnp.bfloat16)


def draw_key_value_cache(key, part):
    cache = jax.random.truncated_normal(jax.random.fold_in(key, 202), -6.0, 6.0, (ROLLOUTS, CTX, N_TP, 2 * HD), jnp.float32)
    return cache.astype(jnp.bfloat16)


def set_ends(entries, rng, low, high):
    place = [jax.random.randint(jax.random.fold_in(rng, axis), (), 0, length) for axis, length in enumerate(entries.shape)]
    main_axis = entries.shape.index(max(entries.shape))
    neighbour = place[:main_axis] + [(place[main_axis] + 1) % entries.shape[main_axis]] + place[main_axis + 1:]
    return entries.at[tuple(place)].set(low).at[tuple(neighbour)].set(high)


def shard_levels(key, extent, cuts, least, high):
    def one(dim, shards_of):
        steps = jax.random.uniform(jax.random.fold_in(jax.random.fold_in(key, 6), dim), (shards_of,), jnp.float32, least / len(cuts), high / len(cuts))
        return jnp.repeat(jnp.exp(steps), extent[dim] // shards_of).reshape((-1,) + (1,) * (len(extent) - dim - 1))

    level = one(*cuts[0])
    for cut in cuts[1:]:
        level = level * one(*cut)
    return level


def gaussian(stream_key, shape, spread, bound, cuts=(), held_as=jnp.bfloat16):
    level = shard_levels(stream_key, shape, cuts, -0.22, 0.18) if cuts else 1.0
    array = jax.random.normal(stream_key, shape, jnp.float32) * spread * level
    return jnp.minimum(jnp.maximum(array, -bound), bound).astype(held_as)


def setup_inputs(seed: int = 0) -> dict:
    seeds = jax.random.split(jax.random.key(seed), 14)
    hidden = gaussian(seeds[0], (ROLLOUTS, MODEL_WIDTH), 1.0, 6.0, ((0, 8),))
    attention_norm_gain = jnp.clip(1.0 + 0.1 * jax.random.normal(seeds[1], (MODEL_WIDTH,), jnp.float32), 0.5, 1.5).astype(jnp.bfloat16)
    query_key_value_weight = draw_query_key_value_weight(jax.random.fold_in(seeds[13], 71), 0)
    key_value_cache = draw_key_value_cache(jax.random.fold_in(seeds[13], 71), 0)
    cache_fill_lengths = set_ends(jax.random.randint(seeds[4], (ROLLOUTS,), 2, CTX + 1), jax.random.fold_in(seeds[4], 1), 2, CTX).astype(jnp.int32)
    output_weight_frozen = gaussian(seeds[5], (N_TP, GROUP_QUERY_DIMS, MODEL_WIDTH), (GROUP_QUERY_DIMS * N_TP) ** -0.5, 0.09375, ((0, 4), (2, 8)))
    adapter_down_transposed = gaussian(seeds[6], (ADAPTER_RANK, N_TP, GROUP_QUERY_DIMS), (GROUP_QUERY_DIMS * N_TP) ** -0.5, 0.09375, ((1, 4), (2, 8)))
    adapter_up_matrix = gaussian(seeds[7], (ADAPTER_RANK, N_TP, SHARD_WIDTH), ADAPTER_RANK ** -0.5, 0.75, ((1, 4), (2, 8)))
    attention_rows = gaussian(seeds[8], (ROWS, GROUP_QUERY_DIMS * N_TP), 1.0, 6.0, ((0, 8), (1, 4)))
    upstream = gaussian(seeds[9], (ROWS, MODEL_WIDTH), 1.0, 6.0, ((0, 8), (1, 4)))
    rewards = jnp.clip(2.0 * jax.random.uniform(seeds[10], (ROLLOUTS,), jnp.float32) ** shard_levels(seeds[10], (ROLLOUTS,), ((0, 8),), -0.2, 0.2), 0.0, 2.0)
    prompt_group_index = draw_prompt_group_index(jax.random.fold_in(seeds[13], 71), 0)
    completion_live_lengths = set_ends(jax.random.randint(seeds[12], (ROLLOUTS,), 1, COMP + 1), jax.random.fold_in(seeds[12], 1), 1, COMP).astype(jnp.int32)
    return {"hidden": hidden, "attention_norm_gain": attention_norm_gain, "query_key_value_weight": query_key_value_weight, "key_value_cache": key_value_cache, "cache_fill_lengths": cache_fill_lengths, "output_weight_frozen": output_weight_frozen, "adapter_down_transposed": adapter_down_transposed, "adapter_up_matrix": adapter_up_matrix, "attention_rows": attention_rows, "upstream": upstream, "rewards": rewards, "prompt_group_index": prompt_group_index, "completion_live_lengths": completion_live_lengths}


adapter_scale = 2.0

def rms_norm(decode_state, gain):
    scale = lax.rsqrt(lax.optimization_barrier(jnp.mean(decode_state * decode_state, axis=-1, keepdims=True)) + 1e-05)
    return decode_state * scale * gain.astype(jnp.float32)

def one_rollout(packed):
    query, cache, length, new_keys, new_values = packed
    head = query.shape[-1]
    slots = cache.shape[0]
    factor = 1.0 / math.sqrt(head)
    q32 = query.astype(jnp.float32)
    keys = cache[:, :, :head].astype(jnp.float32)
    values = cache[:, :, head:].astype(jnp.float32)
    scores = jnp.einsum('thd,ctd->thc', q32, keys, precision=lax.Precision.HIGHEST) * factor
    valid = jnp.arange(slots) < length
    scores = jnp.where(valid[None, None, :], scores, -1e+30)
    extra = jnp.einsum('thd,etd->the', q32, new_keys.astype(jnp.float32), precision=lax.Precision.HIGHEST) * factor
    joined = jnp.concatenate([scores, extra], axis=-1)
    top = lax.optimization_barrier(jnp.max(joined, axis=-1, keepdims=True))
    expo = jnp.exp(joined - top)
    probs = (expo / lax.optimization_barrier(jnp.sum(expo, axis=-1, keepdims=True))).astype(jnp.bfloat16).astype(jnp.float32)
    out = jnp.einsum('thc,ctd->thd', probs[..., :slots], values, precision=lax.Precision.HIGHEST)
    out = out + jnp.einsum('the,etd->thd', probs[..., slots:], new_values.astype(jnp.float32), precision=lax.Precision.HIGHEST)
    return out.astype(jnp.bfloat16)

def reference(hidden, attention_norm_gain, query_key_value_weight, key_value_cache, cache_fill_lengths, output_weight_frozen, adapter_down_transposed, adapter_up_matrix, attention_rows, upstream, rewards, prompt_group_index, completion_live_lengths):
    rollouts = hidden.shape[0]
    w_qkv = query_key_value_weight.reshape(MODEL_WIDTH, N_TP * QKV_TP).astype(jnp.float32)
    w_out = output_weight_frozen.reshape(N_TP * GROUP_QUERY_DIMS, MODEL_WIDTH)
    down_matrix_full = adapter_down_transposed.reshape(ADAPTER_RANK, N_TP * GROUP_QUERY_DIMS)
    up_matrix_full = adapter_up_matrix.reshape(ADAPTER_RANK, MODEL_WIDTH)
    decode_state = hidden.astype(jnp.float32)
    keys_new = []
    values_new = []
    for step in range(2):
        normed = rms_norm(decode_state, attention_norm_gain)
        qkv = jnp.dot(normed, w_qkv, precision=lax.Precision.HIGHEST)
        qkv = qkv.reshape(rollouts, N_TP, QKV_TP)
        query = qkv[:, :, :GROUP_QUERY_DIMS].reshape(rollouts, N_TP, HEADS_TP, HD)
        keys_new.append(qkv[:, :, GROUP_QUERY_DIMS:GROUP_QUERY_DIMS + HD])
        values_new.append(qkv[:, :, GROUP_QUERY_DIMS + HD:])
        stacked_k = jnp.stack(keys_new, axis=1)
        stacked_v = jnp.stack(values_new, axis=1)
        attended = lax.map(one_rollout, (query, key_value_cache, cache_fill_lengths, stacked_k, stacked_v))
        attended = attended.reshape(rollouts, N_TP * GROUP_QUERY_DIMS)
        frozen_output = jnp.dot(attended, w_out, preferred_element_type=jnp.float32)
        low_rank_decode = jnp.dot(attended, down_matrix_full.T, preferred_element_type=jnp.float32)
        decode_state = decode_state + frozen_output + adapter_scale * jnp.dot(low_rank_decode, up_matrix_full.astype(jnp.float32), precision=lax.Precision.HIGHEST)
    decoded = decode_state
    groups = rollouts // GROUP
    onehot = (prompt_group_index[:, None] == jnp.arange(groups, dtype=jnp.int32)[None, :]).astype(jnp.float32)
    totals = lax.optimization_barrier(jnp.sum(onehot * rewards[:, None], axis=0))
    squares = lax.optimization_barrier(jnp.sum(onehot * (rewards * rewards)[:, None], axis=0))
    mean = totals / GROUP
    std = jnp.sqrt(jnp.maximum(squares / GROUP - mean * mean, 0.09))
    advantage = (rewards - lax.optimization_barrier(jnp.sum(onehot * mean[None, :], axis=1))) / lax.optimization_barrier(jnp.sum(onehot * std[None, :], axis=1))
    per_roll = advantage / completion_live_lengths.astype(jnp.float32)
    rows = attention_rows.shape[0]
    slot = jnp.arange(rows, dtype=jnp.int32) % COMP
    limit = jnp.repeat(completion_live_lengths, COMP)
    row_w = jnp.where(slot < limit, jnp.repeat(per_roll, COMP), 0.0)
    low_rank_rows = jnp.dot(attention_rows, down_matrix_full.T, preferred_element_type=jnp.float32).astype(jnp.bfloat16)
    frozen_output_rows = jnp.dot(attention_rows, w_out, preferred_element_type=jnp.float32)
    adapted_output_rows = frozen_output_rows + adapter_scale * jnp.dot(low_rank_rows, up_matrix_full, preferred_element_type=jnp.float32)
    advantage_weighted = (row_w[:, None] * upstream.astype(jnp.float32)).astype(jnp.bfloat16)
    backward_result = jnp.dot(advantage_weighted, up_matrix_full.T, preferred_element_type=jnp.float32).astype(jnp.bfloat16)
    down_gradient = adapter_scale * lax.dot_general(backward_result, attention_rows, (((0,), (0,)), ((), ())), preferred_element_type=jnp.float32)
    up_gradient = adapter_scale * lax.dot_general(low_rank_rows, advantage_weighted, (((0,), (0,)), ((), ())), preferred_element_type=jnp.float32)
    return (decoded, adapted_output_rows, down_gradient.reshape(ADAPTER_RANK, N_TP, GROUP_QUERY_DIMS), up_gradient.reshape(ADAPTER_RANK, N_TP, MODEL_WIDTH // N_TP))
```

```python
import math

import jax
import jax.numpy as jnp
from jax import lax
from jax.experimental import pallas as pl
from jax.experimental.pallas import tpu as pltpu
from jax.sharding import PartitionSpec as P

HD = 128
HEADS_TP = 8
GROUP = 4
COMP = 256


adapter_scale = 2.0


def rms_norm(decode_state, gain):
    scale = lax.rsqrt(jnp.mean(decode_state * decode_state, axis=-1, keepdims=True) + 1e-05)
    return decode_state * scale * gain.astype(jnp.float32)


def attend(query, cache, lengths, new_keys, new_values):
    head = query.shape[-1]
    slots = cache.shape[1]
    factor = 1.0 / math.sqrt(head)
    keys = cache[:, :, :head].astype(jnp.float32)
    values = cache[:, :, head:]
    scores = jnp.einsum("bhd,bcd->bhc", query, keys, precision=lax.Precision.HIGHEST) * factor
    valid = jnp.arange(slots, dtype=jnp.int32)[None, None, :] < lengths[:, None, None]
    scores = jnp.where(valid, scores, -1e30)
    extra = jnp.einsum("bhd,bed->bhe", query, new_keys, precision=lax.Precision.HIGHEST) * factor
    joined = jnp.concatenate([scores, extra], axis=-1)
    top = jnp.max(joined, axis=-1, keepdims=True)
    expo = jnp.exp(joined - top)
    probs = (expo / jnp.sum(expo, axis=-1, keepdims=True)).astype(jnp.bfloat16)
    out = jnp.einsum("bhc,bcd->bhd", probs[..., :slots], values, preferred_element_type=jnp.float32)
    out = out + jnp.einsum(
        "bhe,bed->bhd",
        probs[..., slots:].astype(jnp.float32),
        new_values,
        precision=lax.Precision.HIGHEST,
    )
    return out.astype(jnp.bfloat16).reshape(query.shape[0], -1)


MESH = pl.DeviceIdType.MESH
F32 = jnp.float32
BF16 = jnp.bfloat16
NT = (((1,), (1,)), ((), ()))
TN = (((0,), (0,)), ((), ()))
CHUNK = 256
SEGS = 4
ROW_PARTS = 8


def split3(v):
    hi = v.astype(BF16)
    rest = v - hi.astype(F32)
    mid = rest.astype(BF16)
    lo = (rest - mid.astype(F32)).astype(BF16)
    return jnp.concatenate([hi, mid, lo], axis=0)


def exact_dot(v, w, dims=(((1,), (0,)), ((), ()))):
    n = v.shape[0]
    r = lax.dot_general(split3(v), w, dims, preferred_element_type=F32)
    return r[:n] + r[n : 2 * n] + r[2 * n :]


def rows_of(ref, n):
    return jnp.concatenate([ref[i] for i in range(n)], axis=0)


def lanes_of(ref, n):
    return jnp.concatenate([ref[i] for i in range(n)], axis=1)


def fused_kernel(
    ndp,
    ntp,
    h_ref,
    gain_ref,
    wqkv_ref,
    cache_ref,
    lens_ref,
    wo_ref,
    a_ref,
    b_ref,
    x_ref,
    up_ref,
    rew_ref,
    idx_ref,
    live_ref,
    dec_ref,
    out_ref,
    ga_ref,
    gb_ref,
    hsend,
    stats_ref,
    hbuf,
    abuf,
    bbuf,
    bdbuf,
    statbuf,
    qsend,
    qrecv,
    asend,
    arecv,
    usend,
    urecv,
    fsend,
    frecv,
    lbsend,
    lbrecv,
    gown,
    gsend,
    grecv,
    gzsend,
    gzrecv,
    wt_ref,
    xbuf,
    wbuf,
    pbuf,
    prcv,
    ds_s,
    ds_r,
    ts_s,
    ts_r,
    bd_s,
    bd_r,
    xs_s,
    xs_r,
    wl_s,
    wl_r,
    ps_s,
    ps_r,
    gy_s,
    gy_r,
    gz_s,
    gz_r,
):
    d = lax.axis_index("dp")
    t = lax.axis_index("tp")
    z, y = d // 2, d % 2
    x, c = t // 2, t % 2
    nz = ndp // 2
    rolls, model = h_ref.shape
    width = model // ndp
    rank = a_ref.shape[0]
    piece = a_ref.shape[1]
    chunks = wo_ref.shape[1] // CHUNK
    qkvw = wqkv_ref.shape[1]
    rows = x_ref.shape[0]

    barrier = pltpu.get_barrier_semaphore()
    for i in range(ndp):
        for j in range(ntp):
            if i or j:
                pl.semaphore_signal(
                    barrier,
                    inc=1,
                    device_id=((d + i) % ndp, (t + j) % ntp),
                    device_id_type=MESH,
                )
    pl.semaphore_wait(barrier, ndp * ntp - 1)

    sent = []

    def send(src, dst, s, r, dev):
        cp = pltpu.make_async_remote_copy(
            src_ref=src, dst_ref=dst, send_sem=s, recv_sem=r, device_id=dev, device_id_type=MESH
        )
        return cp

    def dp_start(e, src, dst):
        for off in range(1, ndp):
            peer = (d + off) % ndp
            cp = send(src(peer), dst.at[d], ds_s.at[e, off], ds_r.at[e, off], (peer, t))
            cp.start()
            sent.append(cp)

    def dp_wait(e, src, dst):
        for off in range(1, ndp):
            frm = (d + ndp - off) % ndp
            send(src(d), dst.at[frm], ds_s.at[e, off], ds_r.at[e, off], (frm, t)).wait_recv()

    def tp_start(e, src, dst):
        for off in range(1, ntp):
            peer = (t + off) % ntp
            cp = send(src, dst.at[t], ts_s.at[e, off], ts_r.at[e, off], (d, peer))
            cp.start()
            sent.append(cp)

    def tp_wait(e, src, dst):
        for off in range(1, ntp):
            frm = (t + ntp - off) % ntp
            send(src, dst.at[frm], ts_s.at[e, off], ts_r.at[e, off], (d, frm)).wait_recv()

    hidden = h_ref[...].astype(F32)
    for i in range(ndp):
        hsend[i] = hidden[:, i * width : (i + 1) * width]
    lane = lax.broadcasted_iota(jnp.int32, (1, 128), 1)
    ones = [jnp.where(lane == idx_ref[r], 1.0, 0.0) for r in range(rolls)]
    stats_ref[...] = jnp.zeros_like(stats_ref)
    for r in range(rolls):
        stats_ref[0:1] += ones[r] * rew_ref[r]
        stats_ref[1:2] += ones[r] * (rew_ref[r] * rew_ref[r])

    dp_start(0, lambda p: hsend.at[p], hbuf)
    hbuf[d] = hsend[d]
    dp_start(1, lambda p: a_ref, abuf)
    abuf[d] = a_ref[...]
    dp_start(2, lambda p: b_ref, bbuf)
    bbuf[d] = b_ref[...]
    dp_start(3, lambda p: stats_ref, statbuf)
    statbuf[d] = stats_ref[...]
    per = width // piece
    half = ndp // per
    bdst = t * half + d // per
    bslot = d % per
    for j in range(ntp):
        tj = (t + j) % ntp
        if j == 0:
            here = bdst == d

            @pl.when(here)
            def _():
                bdbuf[bslot] = b_ref[...]

            @pl.when(jnp.logical_not(here))
            def _():
                send(b_ref, bdbuf.at[bslot], bd_s.at[0], bd_r.at[bslot], (bdst, tj)).start()

        else:
            cp = send(b_ref, bdbuf.at[bslot], bd_s.at[j], bd_r.at[bslot], (bdst, tj))
            cp.start()
            sent.append(cp)
    mate = 2 * x + (1 - c)
    other_y = 2 * z + (1 - y)
    xcp = send(x_ref, xbuf.at[y, c], xs_s.at[0], xs_r.at[0], (d, mate))
    xcp.start()
    sent.append(xcp)
    xbuf[y, c] = x_ref[...]

    def row_send(k):
        part = rows // ROW_PARTS
        if k >= ROW_PARTS:
            return
        seg = pl.ds(k * part, part)
        send(
            x_ref.at[seg], xbuf.at[y, c, seg], xs_s.at[1], xs_r.at[1], (other_y, t)
        ).start()

    def rows_whole():
        return send(x_ref, xbuf.at[1 - y, c], xs_s.at[1], xs_r.at[1], (other_y, t))

    def relay(dst_core):
        return send(
            xbuf.at[1 - y, c], xbuf.at[1 - y, dst_core], xs_s.at[2], xs_r.at[2], (d, mate)
        )

    feats = wo_ref.shape[0]
    pieces = chunks * SEGS
    near, far = z // 2, 1 - z // 2
    end = jnp.logical_or(z == 0, z == nz - 1)
    role_m = jnp.logical_and(jnp.logical_not(end), c == z // 2)
    role_2 = jnp.logical_and(jnp.logical_not(end), c != z // 2)
    z_up, z_dn = jnp.minimum(z + 1, nz - 1), jnp.maximum(z - 1, 0)
    z_in = jnp.where(z < 2, z_up, z_dn)
    z_out = jnp.where(z < 2, z_dn, z_up)

    def seg_of(k):
        size = feats // SEGS
        return k // SEGS, pl.ds((k % SEGS) * size, size)

    def own(k, which, zt):
        ch, seg = seg_of(k)
        return send(
            wo_ref.at[seg, pl.ds(ch * CHUNK, CHUNK)],
            wbuf.at[z // 2, c, ch, seg],
            wl_s.at[which],
            wl_r.at[z // 2, c, k],
            (2 * zt + y, 2 * x + z % 2),
        )

    def hop(blk, j, which, zt):
        k, cc = j // 2, j % 2
        ch, seg = seg_of(k)
        ref = wbuf.at[blk, cc, ch, seg]
        return send(ref, ref, wl_s.at[which], wl_r.at[blk, cc, k], (2 * zt + y, t))

    def own_tick(k):
        @pl.when(z < nz - 1)
        def _():
            own(k, 0, z_up).start()

        @pl.when(z > 0)
        def _():
            own(k, 1, z_dn).start()

        @pl.when(z % 2 != c)
        def _():
            own(k, 2, z).start()

    waited = {"near": 0, "far_m": 0, "far_2": 0}

    def arrive(name, blk, upto):
        for j in range(waited[name], upto):
            hop(blk, j, 3, z_in).wait_recv()
        waited[name] = max(waited[name], upto)

    def relay_tick(name, blk, lo, hi, which, zt):
        hi = min(hi, 2 * pieces)
        arrive(name, blk, hi)
        for j in range(lo, hi):
            hop(blk, j, which, zt).start()

    clock = [0]
    ticks = pieces + 2 + 2 * pieces

    def tick():
        n = clock[0]
        if n >= ticks:
            return
        clock[0] += 1
        if n < pieces:
            own_tick(n)
            row_send(n)
            return
        m = n - pieces

        @pl.when(role_m)
        def _():
            if m < pieces:
                relay_tick("near", near, 2 * m, 2 * m + 2, 3, z_in)
            if m < 2:
                relay_tick("far_m", far, 2 * m, 2 * m + 2, 4, z_out)
            elif m + 2 < 2 * pieces:
                relay_tick("far_m", far, m + 2, m + 3, 4, z_out)

        if m >= 2:

            @pl.when(role_2)
            def _():
                relay_tick("far_2", far, m - 2, m - 1, 4, z_out)

    def pump(n):
        for _ in range(n):
            tick()

    pump(2)

    @pl.when(z % 2 == c)
    def _():
        for ch in range(chunks):
            wbuf[z // 2, c, ch] = wo_ref[:, ch * CHUNK : (ch + 1) * CHUNK]

    def g_side():
        return send(gsend.at[1 - y], grecv, gy_s, gy_r, (other_y, t))

    def g_line(off):
        zt = (z + off) % nz
        return send(gzsend.at[zt], gzrecv.at[z], gz_s.at[off], gz_r.at[off], (2 * zt + y, t))

    def share(dx, dy, ch):
        zz = jnp.where(dx == 1, 1 - x, x)
        yy = jnp.where(dy == 1, 1 - y, y)
        return send(
            pbuf.at[dx, dy, ch],
            prcv.at[dx, dy, ch],
            ps_s.at[dx, dy, ch],
            ps_r.at[dx, dy, ch],
            (2 * z + yy, 2 * zz + c),
        )

    def rows_in():
        rows_whole().wait_recv()
        relay(c).start()

    def rows_ready():
        send(x_ref, xbuf.at[y, 1 - c], xs_s.at[0], xs_r.at[0], (d, mate)).wait_recv()
        relay(1 - c).wait_recv()

    def unit(blk, ch):
        is_near = blk is near
        upto = 2 * (ch + 1) * SEGS
        if is_near:

            @pl.when(role_m)
            def _():
                arrive("near", blk, upto)

            others = jnp.logical_not(role_m)
        else:

            @pl.when(role_m)
            def _():
                arrive("far_m", blk, upto)

            @pl.when(role_2)
            def _():
                arrive("far_2", blk, upto)

            others = end
        for cc in range(2):
            mine = jnp.logical_and(c + 2 * blk == z, c == cc)

            @pl.when(jnp.logical_and(others, jnp.logical_not(mine)))
            def _():
                for k in range(ch * SEGS, (ch + 1) * SEGS):
                    hop(blk, 2 * k + cc, 3, z_in).wait_recv()

        dx = jnp.where(blk == x, 0, 1)
        for dy in (1, 0):
            yy = (y + dy) % 2
            p = jnp.dot(xbuf[yy, 0], wbuf[blk, 0, ch], preferred_element_type=F32)
            p = p + jnp.dot(xbuf[yy, 1], wbuf[blk, 1, ch], preferred_element_type=F32)
            if dy == 1:
                pbuf[dx, 1, ch] = p.astype(BF16)
                share(dx, 1, ch).start()
            else:

                @pl.when(dx == 1)
                def _():
                    pbuf[1, 0, ch] = p.astype(BF16)
                    share(1, 0, ch).start()

                @pl.when(dx == 0)
                def _():
                    cols = pl.ds(pl.multiple_of((y * chunks + ch) * CHUNK, CHUNK), CHUNK)
                    out_ref[:, cols] += p

    dp_wait(0, lambda p: hsend.at[p], hbuf)
    state = rows_of(hbuf, ndp)
    gain = gain_ref[:, pl.ds(pl.multiple_of(d * width, width), width)].astype(F32)
    new_k, new_v = [], []
    factor = 1.0 / math.sqrt(HD)

    for step in range(2):
        squares = jnp.sum(state * state, axis=-1, keepdims=True)
        part = exact_dot(state * gain, wqkv_ref[...])
        both = jnp.concatenate([part, jnp.broadcast_to(squares, (ndp * rolls, 128))], axis=1)
        for i in range(ndp):
            qsend[step, i] = both[i * rolls : (i + 1) * rolls]
        dp_start(4 + 2 * step, lambda p: qsend.at[step, p], qrecv.at[step])
        pump(2)
        qrecv[step, d] = qsend[step, d]
        if step == 0:
            dp_wait(1, lambda p: a_ref, abuf)
            at = lanes_of(abuf, ndp)
            dp_wait(2, lambda p: b_ref, bbuf)
            bt = lanes_of(bbuf, ndp)
            dp_wait(3, lambda p: stats_ref, statbuf)
            tot = statbuf[0]
            for i in range(1, ndp):
                tot = tot + statbuf[i]
            mean = tot[0:1] / GROUP
            std = jnp.sqrt(jnp.maximum(tot[1:2] / GROUP - mean * mean, 0.09))
            for r in range(rolls):
                one, rew = ones[r], rew_ref[r]
                live = live_ref[r].astype(F32)
                adv = (rew - jnp.sum(one * mean, axis=1, keepdims=True)) / jnp.sum(
                    one * std, axis=1, keepdims=True
                )
                slot = lax.broadcasted_iota(jnp.int32, (COMP, 1), 0).astype(F32)
                row_w = jnp.where(slot < live, adv / live, 0.0)
                seg = pl.ds(r * COMP, COMP)
                wt_ref[seg, :] = (row_w * up_ref[seg, :].astype(F32)).astype(BF16)
            lbsend[0] = lax.dot_general(at, x_ref[...], NT, preferred_element_type=F32).astype(BF16)
            lbsend[1] = lax.dot_general(bt, wt_ref[...], NT, preferred_element_type=F32).astype(BF16)
        dp_wait(4 + 2 * step, lambda p: qsend.at[step, p], qrecv.at[step])
        total = qrecv[step, 0]
        for i in range(1, ndp):
            total = total + qrecv[step, i]
        qkv = total[:, :qkvw] * lax.rsqrt(total[:, qkvw : qkvw + 1] / model + 1e-05)
        new_k.append(qkv[:, HEADS_TP * HD : HEADS_TP * HD + HD])
        new_v.append(qkv[:, HEADS_TP * HD + HD :])
        for b in range(rolls):
            q = jnp.concatenate(
                [qkv[b : b + 1, h * HD : (h + 1) * HD] for h in range(HEADS_TP)], axis=0
            )
            scores = exact_dot(q, cache_ref[b, :, :HD], NT) * factor
            pos = lax.broadcasted_iota(jnp.int32, scores.shape, 1)
            scores = jnp.where(pos < lens_ref[b], scores, -1e30)
            extra = [
                jnp.sum(q * k[b : b + 1], axis=-1, keepdims=True) * factor for k in new_k
            ]
            top = jnp.max(scores, axis=-1, keepdims=True)
            for e in extra:
                top = jnp.maximum(top, e)
            expo = jnp.exp(scores - top)
            ee = [jnp.exp(e - top) for e in extra]
            den = jnp.sum(expo, axis=-1, keepdims=True)
            for e in ee:
                den = den + e
            att = jnp.dot(
                (expo / den).astype(BF16), cache_ref[b, :, HD:], preferred_element_type=F32
            )
            for e, v in zip(ee, new_v):
                att = att + (e / den).astype(BF16).astype(F32) * v[b : b + 1]
            att = att.astype(BF16).astype(F32)
            asend[step, b : b + 1, :] = jnp.concatenate(
                [att[h : h + 1] for h in range(HEADS_TP)], axis=1
            )
        dp_start(5 + 2 * step, lambda p: asend.at[step], arecv.at[step])
        pump(2)
        arecv[step, d] = asend[step]
        if step == 0:
            tp_start(2, lbsend, lbrecv)
            lbrecv[t] = lbsend[...]
        else:
            tp_wait(2, lbsend, lbrecv)
            lb = lbrecv[0].astype(F32)
            for i in range(1, ntp):
                lb = lb + lbrecv[i].astype(F32)
            lb = lb.astype(BF16)
            low_t, back_t = lb[0], lb[1]
            ga = adapter_scale * jnp.dot(back_t, x_ref[...], preferred_element_type=F32)
            gb = adapter_scale * jnp.dot(low_t, wt_ref[...], preferred_element_type=F32)
            for i in range(ndp):
                for k, g in enumerate((ga, gb)):
                    part = g[:, i * piece : (i + 1) * piece]
                    gown[i % 2, i // 2, k] = part
                    gsend[i % 2, i // 2, k] = part.astype(BF16)
            g_side().start()
            out_ref[...] = adapter_scale * lax.dot_general(
                low_t, bt, TN, preferred_element_type=F32
            )
        dp_wait(5 + 2 * step, lambda p: asend.at[step], arecv.at[step])
        attended = rows_of(arecv.at[step], ndp).astype(BF16)
        usend[step, :, :width] = jnp.dot(attended, wo_ref[...], preferred_element_type=F32)
        usend[step, :, width:] = jnp.concatenate(
            [
                lax.dot_general(attended, at, NT, preferred_element_type=F32),
                jnp.zeros((ndp * rolls, 128 - rank), F32),
            ],
            axis=1,
        )
        tp_start(step, usend.at[step], urecv.at[step])
        pump(2)
        urecv[step, t] = usend[step]
        if step == 0:
            src_t = d // half
            for j in range(per):
                frm = (d % half) * per + j
                same = jnp.logical_and(src_t == t, frm == d)

                @pl.when(jnp.logical_not(same))
                def _():
                    send(b_ref, bdbuf.at[j], bd_s.at[0], bd_r.at[j], (frm, src_t)).wait_recv()

            bd = lanes_of(bdbuf, per)
        tp_wait(step, usend.at[step], urecv.at[step])
        upd = urecv[step, 0]
        for i in range(1, ntp):
            upd = upd + urecv[step, i]
        state = state + (
            upd[:, :width] + adapter_scale * exact_dot(upd[:, width : width + rank], bd)
        )

    for i in range(ndp):
        fsend[i] = state[i * rolls : (i + 1) * rolls]
    dp_start(8, lambda p: fsend.at[p], frecv)
    frecv[d] = fsend[d]
    rows_in()
    g_side().wait_recv()
    for i in range(nz):
        gzsend[i] = (gown[y, i] + grecv[i].astype(F32)).astype(BF16)
    for off in range(1, nz):
        g_line(off).start()
    pump(2)
    rows_ready()
    unit(near, 0)
    pump(2)
    unit(near, 1)
    pump(2)
    dp_wait(8, lambda p: fsend.at[p], frecv)
    for i in range(ndp):
        dec_ref[:, i * width : (i + 1) * width] = frecv[i]
    while waited["far_2"] < pieces or clock[0] < pieces + 2 + pieces:
        pump(1)
    unit(far, 0)
    pump(ticks)
    unit(far, 1)

    g = gown[y, z] + grecv[z].astype(F32)
    for off in range(1, nz):
        g_line(off).wait_recv()
        g = g + gzrecv[(z + nz - off) % nz].astype(F32)
    ga_ref[...] = g[0]
    gb_ref[...] = g[1]
    for ch in range(chunks):
        for dx, dy in ((1, 0), (0, 1), (1, 1)):
            share(dx, dy, ch).wait_recv()
            yy = (y + dy) % 2
            cols = pl.ds(pl.multiple_of((yy * chunks + ch) * CHUNK, CHUNK), CHUNK)
            out_ref[:, cols] += prcv[dx, dy, ch].astype(F32)

    def drain(which, full):
        send(full, full, wl_s.at[which], wl_r.at[0, 0, 0], (d, mate)).wait_send()

    @pl.when(z < nz - 1)
    def _():
        drain(0, wbuf.at[0, 0])

    @pl.when(z > 0)
    def _():
        drain(1, wbuf.at[0, 0])

    @pl.when(z % 2 != c)
    def _():
        drain(2, wbuf.at[0, 0])

    @pl.when(role_m)
    def _():
        drain(3, wbuf.at[0])

    @pl.when(jnp.logical_not(end))
    def _():
        drain(4, wbuf.at[0])

    for ch in range(chunks):
        for dx, dy in ((1, 0), (0, 1), (1, 1)):
            share(dx, dy, ch).wait_send()
    rows_whole().wait_send()
    relay(c).wait_send()
    g_side().wait_send()
    for off in range(1, nz):
        g_line(off).wait_send()

    @pl.when(bdst != d)
    def _():
        send(b_ref, bdbuf.at[bslot], bd_s.at[0], bd_r.at[bslot], (bdst, t)).wait_send()

    for cp in sent:
        cp.wait_send()


def fused_shards(
    ndp,
    ntp,
    hidden,
    attention_norm_gain,
    query_key_value_weight,
    key_value_cache,
    cache_fill_lengths,
    output_weight_frozen,
    adapter_down_transposed,
    adapter_up_matrix,
    attention_rows,
    upstream,
    rewards,
    prompt_group_index,
    completion_live_lengths,
):
    rolls, model = hidden.shape
    width = model // ndp
    rank, _, piece = adapter_down_transposed.shape
    rows, shard = attention_rows.shape
    qkvw = query_key_value_weight.shape[2]
    feats = output_weight_frozen.shape[1]
    chunks = width // CHUNK
    vm = pl.BlockSpec(memory_space=pltpu.VMEM)
    sm = pl.BlockSpec(memory_space=pltpu.SMEM)
    dma = pltpu.SemaphoreType.DMA
    V = pltpu.VMEM
    dec, out, ga, gb = pl.pallas_call(
        lambda *refs: fused_kernel(ndp, ntp, *refs),
        out_shape=(
            jax.ShapeDtypeStruct((rolls, model), F32),
            jax.ShapeDtypeStruct((rows, shard), F32),
            jax.ShapeDtypeStruct((rank, piece), F32),
            jax.ShapeDtypeStruct((rank, piece), F32),
        ),
        in_specs=[vm, vm, vm, vm, sm, vm, vm, vm, vm, vm, sm, sm, sm],
        out_specs=(vm, vm, vm, vm),
        scratch_shapes=[
            V((ndp, rolls, width), F32),
            V((8, 128), F32),
            V((ndp, rolls, width), F32),
            V((ndp, rank, piece), BF16),
            V((ndp, rank, piece), BF16),
            V((width // piece, rank, piece), BF16),
            V((ndp, 8, 128), F32),
            V((2, ndp, rolls, qkvw + 128), F32),
            V((2, ndp, rolls, qkvw + 128), F32),
            V((2, rolls, feats), F32),
            V((2, ndp, rolls, feats), F32),
            V((2, ndp * rolls, width + 128), F32),
            V((2, ntp, ndp * rolls, width + 128), F32),
            V((ndp, rolls, width), F32),
            V((ndp, rolls, width), F32),
            V((2, rank, rows), BF16),
            V((ntp, 2, rank, rows), BF16),
            V((2, ndp // 2, 2, rank, piece), F32),
            V((2, ndp // 2, 2, rank, piece), BF16),
            V((ndp // 2, 2, rank, piece), BF16),
            V((ndp // 2, 2, rank, piece), BF16),
            V((ndp // 2, 2, rank, piece), BF16),
            V((rows, shard), BF16),
            V((2, 2, rows, shard), BF16),
            V((2, 2, chunks, feats, CHUNK), BF16),
            V((2, 2, chunks, rows, CHUNK), BF16),
            V((2, 2, chunks, rows, CHUNK), BF16),
            dma((10, ndp)),
            dma((10, ndp)),
            dma((3, ntp)),
            dma((3, ntp)),
            dma((ntp,)),
            dma((width // piece,)),
            dma((3,)),
            dma((3,)),
            dma((5,)),
            dma((2, 2, chunks * SEGS)),
            dma((2, 2, chunks)),
            dma((2, 2, chunks)),
            dma,
            dma,
            dma((ndp // 2,)),
            dma((ndp // 2,)),
        ],
        compiler_params=pltpu.CompilerParams(
            collective_id=0, has_side_effects=True, vmem_limit_bytes=60 * 2**20
        ),
    )(
        hidden,
        attention_norm_gain.reshape(1, model),
        query_key_value_weight[:, 0, :],
        key_value_cache[:, :, 0, :],
        cache_fill_lengths,
        output_weight_frozen[0],
        adapter_down_transposed[:, 0, :],
        adapter_up_matrix[:, 0, :],
        attention_rows,
        upstream,
        rewards,
        prompt_group_index,
        completion_live_lengths,
    )
    return dec, out, ga[:, None, :], gb[:, None, :]


def shards(
    hidden,
    attention_norm_gain,
    query_key_value_weight,
    key_value_cache,
    cache_fill_lengths,
    output_weight_frozen,
    adapter_down_transposed,
    adapter_up_matrix,
    attention_rows,
    upstream,
    rewards,
    prompt_group_index,
    completion_live_lengths,
):
    a_piece, b_piece = (
        lax.all_gather(adapter_down_transposed, "dp", axis=2, tiled=True),
        lax.all_gather(adapter_up_matrix, "dp", axis=2, tiled=True),
    )
    b_whole = lax.all_gather(b_piece, "tp", axis=1, tiled=True)
    up_matrix_flat = b_whole.reshape(b_whole.shape[0], -1).astype(jnp.float32)
    a_local = a_piece[:, 0, :]
    up_matrix_columns = b_piece[:, 0, :]
    w_rows = query_key_value_weight[:, 0, :].astype(jnp.float32)
    w_cols = output_weight_frozen[0]
    query_width = HEADS_TP * HD
    local_rolls = hidden.shape[0]
    decode_state = hidden.astype(jnp.float32)
    keys_new = []
    values_new = []
    for step in range(2):
        normed = rms_norm(decode_state, attention_norm_gain)
        spread = lax.all_to_all(normed, "dp", split_axis=1, concat_axis=0, tiled=True)
        partial_value = jnp.dot(spread, w_rows, precision=lax.Precision.HIGHEST)
        qkv = lax.psum_scatter(partial_value, "dp", scatter_dimension=0, tiled=True)
        query = qkv[:, :query_width].reshape(local_rolls, HEADS_TP, HD)
        keys_new.append(qkv[:, query_width : query_width + HD])
        values_new.append(qkv[:, query_width + HD :])
        attended = attend(
            query,
            key_value_cache[:, :, 0, :],
            cache_fill_lengths,
            jnp.stack(keys_new, axis=1),
            jnp.stack(values_new, axis=1),
        )
        columns = jnp.dot(
            lax.all_gather(attended, "dp", axis=0, tiled=True),
            w_cols,
            preferred_element_type=jnp.float32,
        )
        returned_values = lax.all_to_all(columns, "dp", split_axis=0, concat_axis=1, tiled=True)
        low_rank_decode = jnp.dot(attended, a_local.T, preferred_element_type=jnp.float32)
        state_update = returned_values + adapter_scale * jnp.dot(
            low_rank_decode, up_matrix_flat, precision=lax.Precision.HIGHEST
        )
        decode_state = decode_state + lax.psum(state_update, "tp")
    groups = local_rolls * lax.axis_size("dp") // GROUP
    onehot = (prompt_group_index[:, None] == jnp.arange(groups, dtype=jnp.int32)[None, :]).astype(
        jnp.float32
    )
    totals, squares = lax.psum(
        (
            jnp.sum(onehot * rewards[:, None], axis=0),
            jnp.sum(onehot * (rewards * rewards)[:, None], axis=0),
        ),
        "dp",
    )
    mean = totals / GROUP
    std = jnp.sqrt(jnp.maximum(squares / GROUP - mean * mean, 0.09))
    advantage = (rewards - jnp.sum(onehot * mean[None, :], axis=1)) / jnp.sum(
        onehot * std[None, :], axis=1
    )
    per_roll = advantage / completion_live_lengths.astype(jnp.float32)
    rows = attention_rows.shape[0]
    slot = jnp.arange(rows, dtype=jnp.int32) % COMP
    limit = jnp.repeat(completion_live_lengths, COMP)
    row_w = jnp.where(slot < limit, jnp.repeat(per_roll, COMP), 0.0)
    whole_rows = jnp.dot(
        attention_rows,
        lax.all_gather(output_weight_frozen, "dp", axis=2, tiled=True)[0],
        preferred_element_type=jnp.float32,
    )
    frozen_output_rows = lax.psum_scatter(whole_rows, "tp", scatter_dimension=1, tiled=True)
    low_sum = lax.psum(jnp.dot(attention_rows, a_local.T, preferred_element_type=jnp.float32), "tp")
    low_rank_rows = low_sum.astype(jnp.bfloat16)
    adapted_output_rows = frozen_output_rows + adapter_scale * jnp.dot(
        low_rank_rows, up_matrix_columns, preferred_element_type=jnp.float32
    )
    advantage_weighted = (row_w[:, None] * upstream.astype(jnp.float32)).astype(jnp.bfloat16)
    backward_result = lax.psum(
        jnp.dot(advantage_weighted, up_matrix_columns.T, preferred_element_type=jnp.float32), "tp"
    ).astype(jnp.bfloat16)
    down_gradient = adapter_scale * lax.dot_general(
        backward_result,
        attention_rows,
        (((0,), (0,)), ((), ())),
        preferred_element_type=jnp.float32,
    )
    up_gradient = adapter_scale * lax.dot_general(
        low_rank_rows,
        advantage_weighted,
        (((0,), (0,)), ((), ())),
        preferred_element_type=jnp.float32,
    )
    grad_a_part, grad_b_part = (
        lax.psum_scatter(down_gradient[:, None, :], "dp", scatter_dimension=2, tiled=True),
        lax.psum_scatter(up_gradient[:, None, :], "dp", scatter_dimension=2, tiled=True),
    )
    return (decode_state, adapted_output_rows, grad_a_part, grad_b_part)


def solution(mesh):
    placed = (
        P("dp", None),
        P(),
        P("dp", "tp", None),
        P("dp", None, "tp", None),
        P("dp"),
        P("tp", None, "dp"),
        P(None, "tp", "dp"),
        P(None, "tp", "dp"),
        P("dp", "tp"),
        P("dp", "tp"),
        P("dp"),
        P("dp"),
        P("dp"),
    )
    ndp, ntp = mesh.shape["dp"], mesh.shape["tp"]

    def body(*args):
        width = args[5].shape[2]
        piece = args[6].shape[2]
        if ntp == 4 and ndp == 8 and piece % 128 == 0 and width % CHUNK == 0:
            return fused_shards(ndp, ntp, *args)
        return shards(*args)

    return jax.shard_map(
        body,
        mesh=mesh,
        in_specs=placed,
        out_specs=(P("dp", None), P("dp", "tp"), P(None, "tp", "dp"), P(None, "tp", "dp")),
        check_vma=False,
    )
```

```python
import math

import jax
import jax.numpy as jnp
from jax import lax
from jax.experimental import pallas as pl
from jax.experimental.pallas import tpu as pltpu
from jax.sharding import PartitionSpec as P

HD = 128
HEADS_TP = 8
GROUP = 4
COMP = 256


adapter_scale = 2.0


def rms_norm(decode_state, gain):
    scale = lax.rsqrt(jnp.mean(decode_state * decode_state, axis=-1, keepdims=True) + 1e-05)
    return decode_state * scale * gain.astype(jnp.float32)


def attend(query, cache, lengths, new_keys, new_values):
    head = query.shape[-1]
    slots = cache.shape[1]
    factor = 1.0 / math.sqrt(head)
    keys = cache[:, :, :head].astype(jnp.float32)
    values = cache[:, :, head:]
    scores = jnp.einsum("bhd,bcd->bhc", query, keys, precision=lax.Precision.HIGHEST) * factor
    valid = jnp.arange(slots, dtype=jnp.int32)[None, None, :] < lengths[:, None, None]
    scores = jnp.where(valid, scores, -1e30)
    extra = jnp.einsum("bhd,bed->bhe", query, new_keys, precision=lax.Precision.HIGHEST) * factor
    joined = jnp.concatenate([scores, extra], axis=-1)
    top = jnp.max(joined, axis=-1, keepdims=True)
    expo = jnp.exp(joined - top)
    probs = (expo / jnp.sum(expo, axis=-1, keepdims=True)).astype(jnp.bfloat16)
    out = jnp.einsum("bhc,bcd->bhd", probs[..., :slots], values, preferred_element_type=jnp.float32)
    out = out + jnp.einsum(
        "bhe,bed->bhd",
        probs[..., slots:].astype(jnp.float32),
        new_values,
        precision=lax.Precision.HIGHEST,
    )
    return out.astype(jnp.bfloat16).reshape(query.shape[0], -1)


MESH = pl.DeviceIdType.MESH
F32 = jnp.float32
BF16 = jnp.bfloat16
NT = (((1,), (1,)), ((), ()))
TN = (((0,), (0,)), ((), ()))
CHUNK = 256
SEGS = 4
ROW_PARTS = 8


def split3(v):
    hi = v.astype(BF16)
    rest = v - hi.astype(F32)
    mid = rest.astype(BF16)
    lo = (rest - mid.astype(F32)).astype(BF16)
    return jnp.concatenate([hi, mid, lo], axis=0)


def exact_dot(v, w, dims=(((1,), (0,)), ((), ()))):
    n = v.shape[0]
    r = lax.dot_general(split3(v), w, dims, preferred_element_type=F32)
    return r[:n] + r[n : 2 * n] + r[2 * n :]


def rows_of(ref, n):
    return jnp.concatenate([ref[i] for i in range(n)], axis=0)


def lanes_of(ref, n):
    return jnp.concatenate([ref[i] for i in range(n)], axis=1)


def fused_kernel(
    ndp,
    ntp,
    h_ref,
    gain_ref,
    wqkv_in,
    cache_in,
    lens_ref,
    wo_in,
    a_ref,
    b_ref,
    x_in,
    up_in,
    rew_ref,
    idx_ref,
    live_ref,
    dec_ref,
    out_ref,
    ga_ref,
    gb_ref,
    hsend,
    stats_ref,
    hbuf,
    abuf,
    bdbuf,
    statbuf,
    qsend,
    qrecv,
    asend,
    arecv,
    usend,
    urecv,
    fsend,
    frecv,
    lbsend,
    lbhalf,
    lbfull,
    gown,
    gsend,
    grecv,
    gzsend,
    gzrecv,
    wt_ref,
    xbuf,
    wbuf,
    pbuf,
    prcv,
    ds_s,
    ds_r,
    ts_s,
    ts_r,
    bd_s,
    bd_r,
    xs_s,
    xs_r,
    wl_s,
    wl_r,
    ps_s,
    ps_r,
    gy_s,
    gy_r,
    gz_s,
    gz_r,
    lb_s,
    lb_r,
    ab_s,
    ab_r,
    wo_ref,
    x_ref,
    wqkv_ref,
    cache_ref,
    up_ref,
    in_s,
):
    d = lax.axis_index("dp")
    t = lax.axis_index("tp")
    z, y = d // 2, d % 2
    x, c = t // 2, t % 2
    nz = ndp // 2
    rolls, model = h_ref.shape
    width = model // ndp
    rank = a_ref.shape[0]
    piece = a_ref.shape[1]
    chunks = wo_ref.shape[1] // CHUNK
    qkvw = wqkv_ref.shape[1]
    rows = x_ref.shape[0]

    def fetch(k):
        src, dst = (
            (wo_in, wo_ref),
            (x_in, x_ref),
            (wqkv_in, wqkv_ref),
            (cache_in, cache_ref),
            (up_in, up_ref),
        )[k]
        return pltpu.make_async_copy(src, dst, in_s.at[k])

    for k in range(5):
        fetch(k).start()
    barrier = pltpu.get_barrier_semaphore()
    for i in range(ndp):
        for j in range(ntp):
            if i or j:
                pl.semaphore_signal(
                    barrier,
                    inc=1,
                    device_id=((d + i) % ndp, (t + j) % ntp),
                    device_id_type=MESH,
                )
    pl.semaphore_wait(barrier, ndp * ntp - 1)

    sent = []

    def send(src, dst, s, r, dev):
        cp = pltpu.make_async_remote_copy(
            src_ref=src, dst_ref=dst, send_sem=s, recv_sem=r, device_id=dev, device_id_type=MESH
        )
        return cp

    def dp_start(e, src, dst):
        for off in range(1, ndp):
            peer = (d + off) % ndp
            cp = send(src(peer), dst.at[d], ds_s.at[e, off], ds_r.at[e, off], (peer, t))
            cp.start()
            sent.append(cp)

    def dp_wait(e, src, dst):
        for off in range(1, ndp):
            frm = (d + ndp - off) % ndp
            send(src(d), dst.at[frm], ds_s.at[e, off], ds_r.at[e, off], (frm, t)).wait_recv()

    def tp_start(e, src, dst):
        for off in range(1, ntp):
            peer = (t + off) % ntp
            cp = send(src, dst.at[t], ts_s.at[e, off], ts_r.at[e, off], (d, peer))
            cp.start()
            sent.append(cp)

    def tp_wait(e, src, dst):
        for off in range(1, ntp):
            frm = (t + ntp - off) % ntp
            send(src, dst.at[frm], ts_s.at[e, off], ts_r.at[e, off], (d, frm)).wait_recv()

    hidden = h_ref[...].astype(F32)
    for i in range(ndp):
        hsend[i] = hidden[:, i * width : (i + 1) * width]
    lane = lax.broadcasted_iota(jnp.int32, (1, 128), 1)
    ones = [jnp.where(lane == idx_ref[r], 1.0, 0.0) for r in range(rolls)]
    stats_ref[...] = jnp.zeros_like(stats_ref)
    for r in range(rolls):
        stats_ref[0:1] += ones[r] * rew_ref[r]
        stats_ref[1:2] += ones[r] * (rew_ref[r] * rew_ref[r])

    dp_start(0, lambda p: hsend.at[p], hbuf)
    hbuf[d] = hsend[d]
    abuf[y, z, 0] = a_ref[...]
    abuf[y, z, 1] = b_ref[...]
    for k, ref in enumerate((a_ref, b_ref)):
        for off in range(1, nz):
            peer = 2 * ((z + off) % nz) + y
            cp = send(ref, abuf.at[y, z, k], ab_s.at[k, off], ab_r.at[k, off], (peer, t))
            cp.start()
            sent.append(cp)
    dp_start(3, lambda p: stats_ref, statbuf)
    statbuf[d] = stats_ref[...]
    per = width // piece
    half = ndp // per
    bdst = t * half + d // per
    bslot = d % per
    for j in range(ntp):
        tj = (t + j) % ntp
        if j == 0:
            here = bdst == d

            @pl.when(here)
            def _():
                bdbuf[bslot] = b_ref[...]

            @pl.when(jnp.logical_not(here))
            def _():
                send(b_ref, bdbuf.at[bslot], bd_s.at[0], bd_r.at[bslot], (bdst, tj)).start()

        else:
            cp = send(b_ref, bdbuf.at[bslot], bd_s.at[j], bd_r.at[bslot], (bdst, tj))
            cp.start()
            sent.append(cp)
    mate = 2 * x + (1 - c)
    other_y = 2 * z + (1 - y)
    fetch(0).wait()
    fetch(1).wait()
    xcp = send(x_ref, xbuf.at[y, c], xs_s.at[0], xs_r.at[0], (d, mate))
    xcp.start()
    sent.append(xcp)
    xbuf[y, c] = x_ref[...]

    def row_send(k):
        part = rows // ROW_PARTS
        if k >= ROW_PARTS:
            return
        seg = pl.ds(k * part, part)
        send(
            x_ref.at[seg], xbuf.at[y, c, seg], xs_s.at[1], xs_r.at[1], (other_y, t)
        ).start()

    def rows_whole():
        return send(x_ref, xbuf.at[1 - y, c], xs_s.at[1], xs_r.at[1], (other_y, t))

    def relay(dst_core):
        return send(
            xbuf.at[1 - y, c], xbuf.at[1 - y, dst_core], xs_s.at[2], xs_r.at[2], (d, mate)
        )

    feats = wo_ref.shape[0]
    pieces = chunks * SEGS
    near, far = z // 2, 1 - z // 2
    end = jnp.logical_or(z == 0, z == nz - 1)
    role_m = jnp.logical_and(jnp.logical_not(end), c == z // 2)
    role_2 = jnp.logical_and(jnp.logical_not(end), c != z // 2)
    z_up, z_dn = jnp.minimum(z + 1, nz - 1), jnp.maximum(z - 1, 0)
    z_in = jnp.where(z < 2, z_up, z_dn)
    z_out = jnp.where(z < 2, z_dn, z_up)

    def seg_of(k):
        size = feats // SEGS
        return k // SEGS, pl.ds((k % SEGS) * size, size)

    def own(k, which, zt):
        ch, seg = seg_of(k)
        return send(
            wo_ref.at[seg, pl.ds(ch * CHUNK, CHUNK)],
            wbuf.at[z // 2, c, ch, seg],
            wl_s.at[which],
            wl_r.at[z // 2, c, k],
            (2 * zt + y, 2 * x + z % 2),
        )

    def hop(blk, j, which, zt):
        k, cc = j // 2, j % 2
        ch, seg = seg_of(k)
        ref = wbuf.at[blk, cc, ch, seg]
        return send(ref, ref, wl_s.at[which], wl_r.at[blk, cc, k], (2 * zt + y, t))

    def own_tick(k):
        @pl.when(z < nz - 1)
        def _():
            own(k, 0, z_up).start()

        @pl.when(z > 0)
        def _():
            own(k, 1, z_dn).start()

        @pl.when(z % 2 != c)
        def _():
            own(k, 2, z).start()

    waited = {"near": 0, "far_m": 0, "far_2": 0}

    def arrive(name, blk, upto):
        for j in range(waited[name], upto):
            hop(blk, j, 3, z_in).wait_recv()
        waited[name] = max(waited[name], upto)

    def relay_tick(name, blk, lo, hi, which, zt):
        hi = min(hi, 2 * pieces)
        arrive(name, blk, hi)
        for j in range(lo, hi):
            hop(blk, j, which, zt).start()

    clock = [0]
    ticks = pieces + 2 + 2 * pieces

    def tick():
        n = clock[0]
        if n >= ticks:
            return
        clock[0] += 1
        if n < pieces:
            own_tick(n)
            row_send(n)
            return
        m = n - pieces

        @pl.when(role_m)
        def _():
            if m < pieces:
                relay_tick("near", near, 2 * m, 2 * m + 2, 3, z_in)
            if m < 2:
                relay_tick("far_m", far, 2 * m, 2 * m + 2, 4, z_out)
            elif m + 2 < 2 * pieces:
                relay_tick("far_m", far, m + 2, m + 3, 4, z_out)

        if m >= 2:

            @pl.when(role_2)
            def _():
                relay_tick("far_2", far, m - 2, m - 1, 4, z_out)

    def pump(n):
        for _ in range(n):
            tick()

    pump(2)

    @pl.when(z % 2 == c)
    def _():
        for ch in range(chunks):
            wbuf[z // 2, c, ch] = wo_ref[:, ch * CHUNK : (ch + 1) * CHUNK]

    def ab_side(yy):
        return send(abuf.at[yy], abuf.at[yy], ab_s.at[0, 0], ab_r.at[0, 0], (other_y, t))

    def lb_core():
        return send(lbsend.at[1 - c], lbhalf.at[2], lb_s.at[0], lb_r.at[0], (d, mate))

    def lb_chip():
        return send(lbhalf.at[0], lbhalf.at[1], lb_s.at[1], lb_r.at[1], (d, 2 * (1 - x) + c))

    def lb_back(core):
        return send(lbfull.at[core], lbfull.at[core], lb_s.at[2], lb_r.at[2], (d, mate))

    def g_side():
        return send(gsend.at[1 - y], grecv, gy_s, gy_r, (other_y, t))

    def g_line(off):
        zt = (z + off) % nz
        return send(gzsend.at[zt], gzrecv.at[z], gz_s.at[off], gz_r.at[off], (2 * zt + y, t))

    def share(dx, dy, ch):
        zz = jnp.where(dx == 1, 1 - x, x)
        yy = jnp.where(dy == 1, 1 - y, y)
        return send(
            pbuf.at[dx, dy, ch],
            prcv.at[dx, dy, ch],
            ps_s.at[dx, dy, ch],
            ps_r.at[dx, dy, ch],
            (2 * z + yy, 2 * zz + c),
        )

    def rows_in():
        rows_whole().wait_recv()
        relay(c).start()

    def rows_ready():
        send(x_ref, xbuf.at[y, 1 - c], xs_s.at[0], xs_r.at[0], (d, mate)).wait_recv()
        relay(1 - c).wait_recv()

    def unit(blk, ch):
        is_near = blk is near
        upto = 2 * (ch + 1) * SEGS
        if is_near:

            @pl.when(role_m)
            def _():
                arrive("near", blk, upto)

            others = jnp.logical_not(role_m)
        else:

            @pl.when(role_m)
            def _():
                arrive("far_m", blk, upto)

            @pl.when(role_2)
            def _():
                arrive("far_2", blk, upto)

            others = end
        for cc in range(2):
            mine = jnp.logical_and(c + 2 * blk == z, c == cc)

            @pl.when(jnp.logical_and(others, jnp.logical_not(mine)))
            def _():
                for k in range(ch * SEGS, (ch + 1) * SEGS):
                    hop(blk, 2 * k + cc, 3, z_in).wait_recv()

        dx = jnp.where(blk == x, 0, 1)
        for dy in (1, 0):
            yy = (y + dy) % 2
            p = jnp.dot(xbuf[yy, 0], wbuf[blk, 0, ch], preferred_element_type=F32)
            p = p + jnp.dot(xbuf[yy, 1], wbuf[blk, 1, ch], preferred_element_type=F32)
            if dy == 1:
                pbuf[dx, 1, ch] = p.astype(BF16)
                share(dx, 1, ch).start()
            else:

                @pl.when(dx == 1)
                def _():
                    pbuf[1, 0, ch] = p.astype(BF16)
                    share(1, 0, ch).start()

                @pl.when(dx == 0)
                def _():
                    cols = pl.ds(pl.multiple_of((y * chunks + ch) * CHUNK, CHUNK), CHUNK)
                    out_ref[:, cols] += p

    dp_wait(0, lambda p: hsend.at[p], hbuf)
    state = rows_of(hbuf, ndp)
    gains = gain_ref[...].astype(F32)
    line = lax.broadcasted_iota(jnp.int32, gains.shape, 0)
    gain = jnp.concatenate(
        [
            jnp.sum(jnp.where(line == d * (width // 128) + i, gains, 0.0), axis=0, keepdims=True)
            for i in range(width // 128)
        ],
        axis=1,
    )
    fetch(2).wait()
    new_k, new_v = [], []
    factor = 1.0 / math.sqrt(HD)

    for step in range(2):
        squares = jnp.sum(state * state, axis=-1, keepdims=True)
        part = exact_dot(state * gain, wqkv_ref[...])
        both = jnp.concatenate([part, jnp.broadcast_to(squares, (ndp * rolls, 128))], axis=1)
        for i in range(ndp):
            qsend[step, i] = both[i * rolls : (i + 1) * rolls]
        dp_start(4 + 2 * step, lambda p: qsend.at[step, p], qrecv.at[step])
        pump(2)
        qrecv[step, d] = qsend[step, d]
        if step == 1:
            lb_chip().wait_recv()
            lbfull[c] = (lbhalf[0] + lbhalf[1]).astype(BF16)
            lb_back(c).start()
        if step == 0:
            for k in range(2):
                for off in range(1, nz):
                    frm = (z + nz - off) % nz
                    send(
                        a_ref, abuf.at[y, frm, k], ab_s.at[k, off], ab_r.at[k, off], (2 * frm + y, t)
                    ).wait_recv()
            ab_side(y).start()
            dp_wait(3, lambda p: stats_ref, statbuf)
            tot = statbuf[0]
            for i in range(1, ndp):
                tot = tot + statbuf[i]
            mean = tot[0:1] / GROUP
            std = jnp.sqrt(jnp.maximum(tot[1:2] / GROUP - mean * mean, 0.09))
            fetch(4).wait()
            for r in range(rolls):
                one, rew = ones[r], rew_ref[r]
                live = live_ref[r].astype(F32)
                adv = (rew - jnp.sum(one * mean, axis=1, keepdims=True)) / jnp.sum(
                    one * std, axis=1, keepdims=True
                )
                slot = lax.broadcasted_iota(jnp.int32, (COMP, 1), 0).astype(F32)
                row_w = jnp.where(slot < live, adv / live, 0.0)
                seg = pl.ds(r * COMP, COMP)
                wt_ref[seg, :] = (row_w * up_ref[seg, :].astype(F32)).astype(BF16)
        dp_wait(4 + 2 * step, lambda p: qsend.at[step, p], qrecv.at[step])
        total = qrecv[step, 0]
        for i in range(1, ndp):
            total = total + qrecv[step, i]
        qkv = total[:, :qkvw] * lax.rsqrt(total[:, qkvw : qkvw + 1] / model + 1e-05)
        new_k.append(qkv[:, HEADS_TP * HD : HEADS_TP * HD + HD])
        new_v.append(qkv[:, HEADS_TP * HD + HD :])
        if step == 0:
            fetch(3).wait()
        for b in range(rolls):
            q = jnp.concatenate(
                [qkv[b : b + 1, h * HD : (h + 1) * HD] for h in range(HEADS_TP)], axis=0
            )
            scores = exact_dot(q, cache_ref[b, :, :HD], NT) * factor
            pos = lax.broadcasted_iota(jnp.int32, scores.shape, 1)
            scores = jnp.where(pos < lens_ref[b], scores, -1e30)
            extra = [
                jnp.sum(q * k[b : b + 1], axis=-1, keepdims=True) * factor for k in new_k
            ]
            top = jnp.max(scores, axis=-1, keepdims=True)
            for e in extra:
                top = jnp.maximum(top, e)
            expo = jnp.exp(scores - top)
            ee = [jnp.exp(e - top) for e in extra]
            den = jnp.sum(expo, axis=-1, keepdims=True)
            for e in ee:
                den = den + e
            att = jnp.dot(
                (expo / den).astype(BF16), cache_ref[b, :, HD:], preferred_element_type=F32
            )
            for e, v in zip(ee, new_v):
                att = att + (e / den).astype(BF16).astype(F32) * v[b : b + 1]
            att = att.astype(BF16).astype(F32)
            asend[step, b : b + 1, :] = jnp.concatenate(
                [att[h : h + 1] for h in range(HEADS_TP)], axis=1
            )
        dp_start(5 + 2 * step, lambda p: asend.at[step], arecv.at[step])
        pump(2)
        arecv[step, d] = asend[step]
        if step == 0:
            ab_side(1 - y).wait_recv()
            at, bt = (
                jnp.concatenate([abuf[i % 2, i // 2, k] for i in range(ndp)], axis=1)
                for k in range(2)
            )
            for k, (m, v) in enumerate(((at, x_ref), (bt, wt_ref))):
                lb = lax.dot_general(m, v[...], NT, preferred_element_type=F32)
                for i in range(2):
                    lbsend[i, k] = lb[:, i * (rows // 2) : (i + 1) * (rows // 2)]
            lb_core().start()
        else:
            lb_back(c).wait_send()
            lb_back(1 - c).wait_recv()
            low_t, back_t = lanes_of(lbfull.at[:, 0], 2), lanes_of(lbfull.at[:, 1], 2)
            ga = adapter_scale * jnp.dot(back_t, x_ref[...], preferred_element_type=F32)
            gb = adapter_scale * jnp.dot(low_t, wt_ref[...], preferred_element_type=F32)
            for i in range(ndp):
                for k, g in enumerate((ga, gb)):
                    part = g[:, i * piece : (i + 1) * piece]
                    gown[i % 2, i // 2, k] = part
                    gsend[i % 2, i // 2, k] = part.astype(BF16)
            g_side().start()
            out_ref[...] = adapter_scale * lax.dot_general(
                low_t, bt, TN, preferred_element_type=F32
            )
        dp_wait(5 + 2 * step, lambda p: asend.at[step], arecv.at[step])
        attended = rows_of(arecv.at[step], ndp).astype(BF16)
        usend[step, :, :width] = jnp.dot(attended, wo_ref[...], preferred_element_type=F32)
        usend[step, :, width:] = jnp.concatenate(
            [
                lax.dot_general(attended, at, NT, preferred_element_type=F32),
                jnp.zeros((ndp * rolls, 128 - rank), F32),
            ],
            axis=1,
        )
        tp_start(step, usend.at[step], urecv.at[step])
        pump(2)
        urecv[step, t] = usend[step]
        if step == 0:
            lb_core().wait_recv()
            lbhalf[0] = lbsend[c] + lbhalf[2]
            lb_chip().start()
            src_t = d // half
            for j in range(per):
                frm = (d % half) * per + j
                same = jnp.logical_and(src_t == t, frm == d)

                @pl.when(jnp.logical_not(same))
                def _():
                    send(b_ref, bdbuf.at[j], bd_s.at[0], bd_r.at[j], (frm, src_t)).wait_recv()

            bd = lanes_of(bdbuf, per)
        tp_wait(step, usend.at[step], urecv.at[step])
        upd = urecv[step, 0]
        for i in range(1, ntp):
            upd = upd + urecv[step, i]
        state = state + (
            upd[:, :width] + adapter_scale * exact_dot(upd[:, width : width + rank], bd)
        )

    for i in range(ndp):
        fsend[i] = state[i * rolls : (i + 1) * rolls]
    dp_start(8, lambda p: fsend.at[p], frecv)
    frecv[d] = fsend[d]
    rows_in()
    g_side().wait_recv()
    for i in range(nz):
        gzsend[i] = (gown[y, i] + grecv[i].astype(F32)).astype(BF16)
    for off in range(1, nz):
        g_line(off).start()
    pump(2)
    rows_ready()
    unit(near, 0)
    pump(2)
    unit(near, 1)
    pump(2)
    dp_wait(8, lambda p: fsend.at[p], frecv)
    for i in range(ndp):
        dec_ref[:, i * width : (i + 1) * width] = frecv[i]
    while waited["far_2"] < pieces or clock[0] < pieces + 2 + pieces:
        pump(1)
    unit(far, 0)
    pump(ticks)
    unit(far, 1)

    g = gown[y, z] + grecv[z].astype(F32)
    for off in range(1, nz):
        g_line(off).wait_recv()
        g = g + gzrecv[(z + nz - off) % nz].astype(F32)
    ga_ref[...] = g[0]
    gb_ref[...] = g[1]
    for ch in range(chunks):
        for dx, dy in ((1, 0), (0, 1), (1, 1)):
            share(dx, dy, ch).wait_recv()
            yy = (y + dy) % 2
            cols = pl.ds(pl.multiple_of((yy * chunks + ch) * CHUNK, CHUNK), CHUNK)
            out_ref[:, cols] += prcv[dx, dy, ch].astype(F32)

    def drain(which, full):
        send(full, full, wl_s.at[which], wl_r.at[0, 0, 0], (d, mate)).wait_send()

    @pl.when(z < nz - 1)
    def _():
        drain(0, wbuf.at[0, 0])

    @pl.when(z > 0)
    def _():
        drain(1, wbuf.at[0, 0])

    @pl.when(z % 2 != c)
    def _():
        drain(2, wbuf.at[0, 0])

    @pl.when(role_m)
    def _():
        drain(3, wbuf.at[0])

    @pl.when(jnp.logical_not(end))
    def _():
        drain(4, wbuf.at[0])

    for ch in range(chunks):
        for dx, dy in ((1, 0), (0, 1), (1, 1)):
            share(dx, dy, ch).wait_send()
    rows_whole().wait_send()
    relay(c).wait_send()
    g_side().wait_send()
    lb_core().wait_send()
    lb_chip().wait_send()
    ab_side(y).wait_send()
    for off in range(1, nz):
        g_line(off).wait_send()

    @pl.when(bdst != d)
    def _():
        send(b_ref, bdbuf.at[bslot], bd_s.at[0], bd_r.at[bslot], (bdst, t)).wait_send()

    for cp in sent:
        cp.wait_send()


def fused_shards(
    ndp,
    ntp,
    hidden,
    attention_norm_gain,
    query_key_value_weight,
    key_value_cache,
    cache_fill_lengths,
    output_weight_frozen,
    adapter_down_transposed,
    adapter_up_matrix,
    attention_rows,
    upstream,
    rewards,
    prompt_group_index,
    completion_live_lengths,
):
    rolls, model = hidden.shape
    slots = key_value_cache.shape[1]
    width = model // ndp
    rank, _, piece = adapter_down_transposed.shape
    rows, shard = attention_rows.shape
    qkvw = query_key_value_weight.shape[2]
    feats = output_weight_frozen.shape[1]
    chunks = width // CHUNK
    vm = pl.BlockSpec(memory_space=pltpu.VMEM)
    sm = pl.BlockSpec(memory_space=pltpu.SMEM)
    hbm = pl.BlockSpec(memory_space=pltpu.HBM)
    dma = pltpu.SemaphoreType.DMA
    V = pltpu.VMEM
    dec, out, ga, gb = pl.pallas_call(
        lambda *refs: fused_kernel(ndp, ntp, *refs),
        out_shape=(
            pltpu.VMEM((rolls, model), F32),
            pltpu.VMEM((rows, shard), F32),
            pltpu.VMEM((rank, piece), F32),
            pltpu.VMEM((rank, piece), F32),
        ),
        in_specs=[vm, vm, hbm, hbm, sm, hbm, vm, vm, hbm, hbm, sm, sm, sm],
        out_specs=(vm, vm, vm, vm),
        scratch_shapes=[
            V((ndp, rolls, width), F32),
            V((8, 128), F32),
            V((ndp, rolls, width), F32),
            V((2, ndp // 2, 2, rank, piece), BF16),
            V((width // piece, rank, piece), BF16),
            V((ndp, 8, 128), F32),
            V((2, ndp, rolls, qkvw + 128), F32),
            V((2, ndp, rolls, qkvw + 128), F32),
            V((2, rolls, feats), F32),
            V((2, ndp, rolls, feats), F32),
            V((2, ndp * rolls, width + 128), F32),
            V((2, ntp, ndp * rolls, width + 128), F32),
            V((ndp, rolls, width), F32),
            V((ndp, rolls, width), F32),
            V((2, 2, rank, rows // 2), F32),
            V((3, 2, rank, rows // 2), F32),
            V((2, 2, rank, rows // 2), BF16),
            V((2, ndp // 2, 2, rank, piece), F32),
            V((2, ndp // 2, 2, rank, piece), BF16),
            V((ndp // 2, 2, rank, piece), BF16),
            V((ndp // 2, 2, rank, piece), BF16),
            V((ndp // 2, 2, rank, piece), BF16),
            V((rows, shard), BF16),
            V((2, 2, rows, shard), BF16),
            V((2, 2, chunks, feats, CHUNK), BF16),
            V((2, 2, chunks, rows, CHUNK), BF16),
            V((2, 2, chunks, rows, CHUNK), BF16),
            dma((10, ndp)),
            dma((10, ndp)),
            dma((3, ntp)),
            dma((3, ntp)),
            dma((ntp,)),
            dma((width // piece,)),
            dma((3,)),
            dma((3,)),
            dma((5,)),
            dma((2, 2, chunks * SEGS)),
            dma((2, 2, chunks)),
            dma((2, 2, chunks)),
            dma,
            dma,
            dma((ndp // 2,)),
            dma((ndp // 2,)),
            dma((3,)),
            dma((3,)),
            dma((2, ndp // 2)),
            dma((2, ndp // 2)),
            V((feats, width), BF16),
            V((rows, shard), BF16),
            V((width, qkvw), BF16),
            V((rolls, slots, 2 * HD), BF16),
            V((rows, shard), BF16),
            dma((5,)),
        ],
        compiler_params=pltpu.CompilerParams(
            collective_id=0, has_side_effects=True, vmem_limit_bytes=64815104
        ),
    )(
        hidden,
        attention_norm_gain.reshape(model // 128, 128),
        query_key_value_weight[:, 0, :],
        key_value_cache[:, :, 0, :],
        cache_fill_lengths,
        output_weight_frozen[0],
        adapter_down_transposed[:, 0, :],
        adapter_up_matrix[:, 0, :],
        attention_rows,
        upstream,
        rewards,
        prompt_group_index,
        completion_live_lengths,
    )
    return dec, out, ga[:, None, :], gb[:, None, :]


def shards(
    hidden,
    attention_norm_gain,
    query_key_value_weight,
    key_value_cache,
    cache_fill_lengths,
    output_weight_frozen,
    adapter_down_transposed,
    adapter_up_matrix,
    attention_rows,
    upstream,
    rewards,
    prompt_group_index,
    completion_live_lengths,
):
    a_piece, b_piece = (
        lax.all_gather(adapter_down_transposed, "dp", axis=2, tiled=True),
        lax.all_gather(adapter_up_matrix, "dp", axis=2, tiled=True),
    )
    b_whole = lax.all_gather(b_piece, "tp", axis=1, tiled=True)
    up_matrix_flat = b_whole.reshape(b_whole.shape[0], -1).astype(jnp.float32)
    a_local = a_piece[:, 0, :]
    up_matrix_columns = b_piece[:, 0, :]
    w_rows = query_key_value_weight[:, 0, :].astype(jnp.float32)
    w_cols = output_weight_frozen[0]
    query_width = HEADS_TP * HD
    local_rolls = hidden.shape[0]
    decode_state = hidden.astype(jnp.float32)
    keys_new = []
    values_new = []
    for step in range(2):
        normed = rms_norm(decode_state, attention_norm_gain)
        spread = lax.all_to_all(normed, "dp", split_axis=1, concat_axis=0, tiled=True)
        partial_value = jnp.dot(spread, w_rows, precision=lax.Precision.HIGHEST)
        qkv = lax.psum_scatter(partial_value, "dp", scatter_dimension=0, tiled=True)
        query = qkv[:, :query_width].reshape(local_rolls, HEADS_TP, HD)
        keys_new.append(qkv[:, query_width : query_width + HD])
        values_new.append(qkv[:, query_width + HD :])
        attended = attend(
            query,
            key_value_cache[:, :, 0, :],
            cache_fill_lengths,
            jnp.stack(keys_new, axis=1),
            jnp.stack(values_new, axis=1),
        )
        columns = jnp.dot(
            lax.all_gather(attended, "dp", axis=0, tiled=True),
            w_cols,
            preferred_element_type=jnp.float32,
        )
        returned_values = lax.all_to_all(columns, "dp", split_axis=0, concat_axis=1, tiled=True)
        low_rank_decode = jnp.dot(attended, a_local.T, preferred_element_type=jnp.float32)
        state_update = returned_values + adapter_scale * jnp.dot(
            low_rank_decode, up_matrix_flat, precision=lax.Precision.HIGHEST
        )
        decode_state = decode_state + lax.psum(state_update, "tp")
    groups = local_rolls * lax.axis_size("dp") // GROUP
    onehot = (prompt_group_index[:, None] == jnp.arange(groups, dtype=jnp.int32)[None, :]).astype(
        jnp.float32
    )
    totals, squares = lax.psum(
        (
            jnp.sum(onehot * rewards[:, None], axis=0),
            jnp.sum(onehot * (rewards * rewards)[:, None], axis=0),
        ),
        "dp",
    )
    mean = totals / GROUP
    std = jnp.sqrt(jnp.maximum(squares / GROUP - mean * mean, 0.09))
    advantage = (rewards - jnp.sum(onehot * mean[None, :], axis=1)) / jnp.sum(
        onehot * std[None, :], axis=1
    )
    per_roll = advantage / completion_live_lengths.astype(jnp.float32)
    rows = attention_rows.shape[0]
    slot = jnp.arange(rows, dtype=jnp.int32) % COMP
    limit = jnp.repeat(completion_live_lengths, COMP)
    row_w = jnp.where(slot < limit, jnp.repeat(per_roll, COMP), 0.0)
    whole_rows = jnp.dot(
        attention_rows,
        lax.all_gather(output_weight_frozen, "dp", axis=2, tiled=True)[0],
        preferred_element_type=jnp.float32,
    )
    frozen_output_rows = lax.psum_scatter(whole_rows, "tp", scatter_dimension=1, tiled=True)
    low_sum = lax.psum(jnp.dot(attention_rows, a_local.T, preferred_element_type=jnp.float32), "tp")
    low_rank_rows = low_sum.astype(jnp.bfloat16)
    adapted_output_rows = frozen_output_rows + adapter_scale * jnp.dot(
        low_rank_rows, up_matrix_columns, preferred_element_type=jnp.float32
    )
    advantage_weighted = (row_w[:, None] * upstream.astype(jnp.float32)).astype(jnp.bfloat16)
    backward_result = lax.psum(
        jnp.dot(advantage_weighted, up_matrix_columns.T, preferred_element_type=jnp.float32), "tp"
    ).astype(jnp.bfloat16)
    down_gradient = adapter_scale * lax.dot_general(
        backward_result,
        attention_rows,
        (((0,), (0,)), ((), ())),
        preferred_element_type=jnp.float32,
    )
    up_gradient = adapter_scale * lax.dot_general(
        low_rank_rows,
        advantage_weighted,
        (((0,), (0,)), ((), ())),
        preferred_element_type=jnp.float32,
    )
    grad_a_part, grad_b_part = (
        lax.psum_scatter(down_gradient[:, None, :], "dp", scatter_dimension=2, tiled=True),
        lax.psum_scatter(up_gradient[:, None, :], "dp", scatter_dimension=2, tiled=True),
    )
    return (decode_state, adapted_output_rows, grad_a_part, grad_b_part)


def solution(mesh):
    placed = (
        P("dp", None),
        P(),
        P("dp", "tp", None),
        P("dp", None, "tp", None),
        P("dp"),
        P("tp", None, "dp"),
        P(None, "tp", "dp"),
        P(None, "tp", "dp"),
        P("dp", "tp"),
        P("dp", "tp"),
        P("dp"),
        P("dp"),
        P("dp"),
    )
    ndp, ntp = mesh.shape["dp"], mesh.shape["tp"]

    def body(*args):
        width = args[5].shape[2]
        piece = args[6].shape[2]
        if ntp == 4 and ndp == 8 and piece % 128 == 0 and width % CHUNK == 0:
            return fused_shards(ndp, ntp, *args)
        return shards(*args)

    return jax.shard_map(
        body,
        mesh=mesh,
        in_specs=placed,
        out_specs=(P("dp", None), P("dp", "tp"), P(None, "tp", "dp"), P(None, "tp", "dp")),
        check_vma=False,
    )
```

```python
import math

import jax
import jax.numpy as jnp
from jax import lax
from jax.experimental import pallas as pl
from jax.experimental.pallas import tpu as pltpu
from jax.sharding import PartitionSpec as P

HD = 128
HEADS_TP = 8
GROUP = 4
COMP = 256


adapter_scale = 2.0


def rms_norm(decode_state, gain):
    scale = lax.rsqrt(jnp.mean(decode_state * decode_state, axis=-1, keepdims=True) + 1e-05)
    return decode_state * scale * gain.astype(jnp.float32)


def attend(query, cache, lengths, new_keys, new_values):
    head = query.shape[-1]
    slots = cache.shape[1]
    factor = 1.0 / math.sqrt(head)
    keys = cache[:, :, :head].astype(jnp.float32)
    values = cache[:, :, head:]
    scores = jnp.einsum("bhd,bcd->bhc", query, keys, precision=lax.Precision.HIGHEST) * factor
    valid = jnp.arange(slots, dtype=jnp.int32)[None, None, :] < lengths[:, None, None]
    scores = jnp.where(valid, scores, -1e30)
    extra = jnp.einsum("bhd,bed->bhe", query, new_keys, precision=lax.Precision.HIGHEST) * factor
    joined = jnp.concatenate([scores, extra], axis=-1)
    top = jnp.max(joined, axis=-1, keepdims=True)
    expo = jnp.exp(joined - top)
    probs = (expo / jnp.sum(expo, axis=-1, keepdims=True)).astype(jnp.bfloat16)
    out = jnp.einsum("bhc,bcd->bhd", probs[..., :slots], values, preferred_element_type=jnp.float32)
    out = out + jnp.einsum(
        "bhe,bed->bhd",
        probs[..., slots:].astype(jnp.float32),
        new_values,
        precision=lax.Precision.HIGHEST,
    )
    return out.astype(jnp.bfloat16).reshape(query.shape[0], -1)


MESH = pl.DeviceIdType.MESH
F32 = jnp.float32
BF16 = jnp.bfloat16
NT = (((1,), (1,)), ((), ()))
TN = (((0,), (0,)), ((), ()))
CHUNK = 256
SEGS = 4
ROW_PARTS = 8


def split3(v):
    hi = v.astype(BF16)
    rest = v - hi.astype(F32)
    mid = rest.astype(BF16)
    lo = (rest - mid.astype(F32)).astype(BF16)
    return jnp.concatenate([hi, mid, lo], axis=0)


def exact_dot(v, w, dims=(((1,), (0,)), ((), ()))):
    n = v.shape[0]
    r = lax.dot_general(split3(v), w, dims, preferred_element_type=F32)
    return r[:n] + r[n : 2 * n] + r[2 * n :]


def rows_of(ref, n):
    return jnp.concatenate([ref[i] for i in range(n)], axis=0)


def lanes_of(ref, n):
    return jnp.concatenate([ref[i] for i in range(n)], axis=1)


def fused_kernel(
    ndp,
    ntp,
    h_ref,
    gain_ref,
    wqkv_in,
    cache_in,
    lens_ref,
    wo_in,
    a_ref,
    b_ref,
    x_in,
    up_in,
    rew_ref,
    idx_ref,
    live_ref,
    dec_out,
    rows_out,
    ga_out,
    gb_out,
    hsend,
    stats_ref,
    hbuf,
    abuf,
    bdbuf,
    statbuf,
    qsend,
    qrecv,
    asend,
    arecv,
    usend,
    urecv,
    fsend,
    frecv,
    lbsend,
    lbhalf,
    lbfull,
    gown,
    gsend,
    grecv,
    gzsend,
    gzrecv,
    wt_ref,
    xbuf,
    wbuf,
    pbuf,
    prcv,
    ds_s,
    ds_r,
    ts_s,
    ts_r,
    bd_s,
    bd_r,
    xs_s,
    xs_r,
    wl_s,
    wl_r,
    ps_s,
    ps_r,
    gy_s,
    gy_r,
    gz_s,
    gz_r,
    lb_s,
    lb_r,
    ab_s,
    ab_r,
    wo_ref,
    x_ref,
    wqkv_ref,
    cache_ref,
    up_ref,
    in_s,
    out_ref,
    dec_ref,
    ga_ref,
    gb_ref,
    out_s,
    fin_s,
):
    d = lax.axis_index("dp")
    t = lax.axis_index("tp")
    z, y = d // 2, d % 2
    x, c = t // 2, t % 2
    nz = ndp // 2
    rolls, model = h_ref.shape
    width = model // ndp
    rank = a_ref.shape[0]
    piece = a_ref.shape[1]
    chunks = wo_ref.shape[1] // CHUNK
    qkvw = wqkv_ref.shape[1]
    rows = x_ref.shape[0]
    mate = 2 * x + (1 - c)
    other_y = 2 * z + (1 - y)

    def fetch(k):
        src, dst = (
            (wo_in, wo_ref),
            (x_in, x_ref),
            (wqkv_in, wqkv_ref),
            (cache_in, cache_ref),
            (up_in, up_ref),
        )[k]
        return pltpu.make_async_copy(src, dst, in_s.at[k])

    for k in range(5):
        fetch(k).start()
    barrier = pltpu.get_barrier_semaphore()
    for i in range(ndp):
        for j in range(ntp):
            if i or j:
                pl.semaphore_signal(
                    barrier,
                    inc=1,
                    device_id=((d + i) % ndp, (t + j) % ntp),
                    device_id_type=MESH,
                )
    pl.semaphore_wait(barrier, ndp * ntp - 1)

    sent = []

    def send(src, dst, s, r, dev):
        cp = pltpu.make_async_remote_copy(
            src_ref=src, dst_ref=dst, send_sem=s, recv_sem=r, device_id=dev, device_id_type=MESH
        )
        return cp

    def dp_start(e, src, dst):
        for off in range(1, ndp):
            peer = (d + off) % ndp
            send(src(peer), dst.at[d], ds_s.at[e], ds_r.at[e], (peer, t)).start()
        whole = dst.at[pl.ds(0, ndp - 1)]
        sent.append(send(whole, whole, ds_s.at[e], ds_r.at[e], (d, (t + 1) % ntp)))

    def dp_wait(e, dst):
        whole = dst.at[pl.ds(0, ndp - 1)]
        send(whole, whole, ds_s.at[e], ds_r.at[e], (d, (t + 1) % ntp)).wait_recv()

    def tp_start(e, src, dst):
        for off in range(1, ntp):
            peer = (t + off) % ntp
            send(src, dst.at[t], ts_s.at[e], ts_r.at[e], (d, peer)).start()
        whole = dst.at[pl.ds(0, ntp - 1)]
        sent.append(send(whole, whole, ts_s.at[e], ts_r.at[e], (d, (t + 1) % ntp)))

    def tp_wait(e, dst):
        whole = dst.at[pl.ds(0, ntp - 1)]
        send(whole, whole, ts_s.at[e], ts_r.at[e], (d, (t + 1) % ntp)).wait_recv()

    hidden = h_ref[...].astype(F32)
    for i in range(ndp):
        hsend[i] = hidden[:, i * width : (i + 1) * width]
    lane = lax.broadcasted_iota(jnp.int32, (1, 128), 1)
    ones = [jnp.where(lane == idx_ref[r], 1.0, 0.0) for r in range(rolls)]
    stats_ref[...] = jnp.zeros_like(stats_ref)
    for r in range(rolls):
        stats_ref[0:1] += ones[r] * rew_ref[r]
        stats_ref[1:2] += ones[r] * (rew_ref[r] * rew_ref[r])

    dp_start(0, lambda p: hsend.at[p], hbuf)
    hbuf[d] = hsend[d]
    abuf[y, z, 0] = a_ref[...]
    abuf[y, z, 1] = b_ref[...]
    for k, ref in enumerate((a_ref, b_ref)):
        for off in range(1, nz):
            peer = 2 * ((z + off) % nz) + y
            send(ref, abuf.at[y, z, k], ab_s.at[0], ab_r.at[0], (peer, t)).start()
    others = abuf.at[0, pl.ds(0, nz - 1)]
    sent.append(send(others, others, ab_s.at[0], ab_r.at[0], (other_y, t)))
    dp_start(1, lambda p: stats_ref, statbuf)
    statbuf[d] = stats_ref[...]
    per = width // piece
    half = ndp // per
    bdst = t * half + d // per
    bslot = d % per
    for j in range(ntp):
        tj = (t + j) % ntp
        if j == 0:
            here = bdst == d

            @pl.when(here)
            def _():
                bdbuf[bslot] = b_ref[...]

            @pl.when(jnp.logical_not(here))
            def _():
                send(b_ref, bdbuf.at[bslot], bd_s.at[0], bd_r.at[bslot], (bdst, tj)).start()

        else:
            send(b_ref, bdbuf.at[bslot], bd_s.at[1], bd_r.at[bslot], (bdst, tj)).start()
    copies = bdbuf.at[pl.ds(0, ntp - 1)]
    sent.append(send(copies, copies, bd_s.at[1], bd_r.at[0], (other_y, t)))
    fetch(0).wait()
    fetch(1).wait()
    xcp = send(x_ref, xbuf.at[y, c], xs_s.at[0], xs_r.at[0], (d, mate))
    xcp.start()
    sent.append(xcp)
    xbuf[y, c] = x_ref[...]

    def row_send(k):
        part = rows // ROW_PARTS
        if k >= ROW_PARTS:
            return
        seg = pl.ds(k * part, part)
        send(
            x_ref.at[seg], xbuf.at[y, c, seg], xs_s.at[1], xs_r.at[1], (other_y, t)
        ).start()

    def rows_whole():
        return send(x_ref, xbuf.at[1 - y, c], xs_s.at[1], xs_r.at[1], (other_y, t))

    def relay(dst_core):
        return send(
            xbuf.at[1 - y, c], xbuf.at[1 - y, dst_core], xs_s.at[2], xs_r.at[2], (d, mate)
        )

    feats = wo_ref.shape[0]
    pieces = chunks * SEGS
    near, far = z // 2, 1 - z // 2
    end = jnp.logical_or(z == 0, z == nz - 1)
    role_m = jnp.logical_and(jnp.logical_not(end), c == z // 2)
    role_2 = jnp.logical_and(jnp.logical_not(end), c != z // 2)
    z_up, z_dn = jnp.minimum(z + 1, nz - 1), jnp.maximum(z - 1, 0)
    z_in = jnp.where(z < 2, z_up, z_dn)
    z_out = jnp.where(z < 2, z_dn, z_up)

    cuts = [(ch, 0, CHUNK) for ch in range(chunks - 1)]
    cuts += [(chunks - 1, h * 128, 128) for h in range(CHUNK // 128)]

    def seg_of(k):
        ch, part = k // SEGS, k % SEGS
        if ch < chunks - 1:
            size = feats // SEGS
            return ch, pl.ds(part * size, size), 0, CHUNK
        halves = CHUNK // 128
        size = feats * halves // SEGS
        per_half = SEGS // halves
        return ch, pl.ds((part % per_half) * size, size), (part // per_half) * 128, 128

    def own(k, which, zt):
        ch, seg, off, num = seg_of(k)
        return send(
            wo_ref.at[seg, pl.ds(ch * CHUNK + off, num)],
            wbuf.at[z // 2, c, ch, seg, pl.ds(off, num)],
            wl_s.at[which],
            wl_r.at[z // 2, c, k],
            (2 * zt + y, 2 * x + z % 2),
        )

    def hop(blk, j, which, zt):
        k, cc = j // 2, j % 2
        ch, seg, off, num = seg_of(k)
        ref = wbuf.at[blk, cc, ch, seg, pl.ds(off, num)]
        return send(ref, ref, wl_s.at[which], wl_r.at[blk, cc, k], (2 * zt + y, t))

    def own_tick(k):
        @pl.when(z < nz - 1)
        def _():
            own(k, 0, z_up).start()

        @pl.when(z > 0)
        def _():
            own(k, 1, z_dn).start()

        @pl.when(z % 2 != c)
        def _():
            own(k, 2, z).start()

    waited = {"near": 0, "far_m": 0, "far_2": 0}

    def arrive(name, blk, upto):
        for j in range(waited[name], upto):
            hop(blk, j, 3, z_in).wait_recv()
        waited[name] = max(waited[name], upto)

    def relay_tick(name, blk, lo, hi, which, zt):
        hi = min(hi, 2 * pieces)
        arrive(name, blk, hi)
        for j in range(lo, hi):
            hop(blk, j, which, zt).start()

    clock = [0]
    ticks = 3 * pieces

    def tick():
        n = clock[0]
        if n >= ticks:
            return
        clock[0] += 1
        if n < pieces:
            own_tick(n)
            row_send(n)
            return
        m = n - pieces

        @pl.when(role_m)
        def _():
            if m < pieces:
                relay_tick("near", near, 2 * m, 2 * m + 2, 3, z_in)
                relay_tick("far_m", far, 2 * m, 2 * m + 2, 4, z_out)

        if m >= pieces:

            @pl.when(role_2)
            def _():
                relay_tick("far_2", far, 2 * (m - pieces), 2 * (m - pieces) + 2, 4, z_out)

    def pump(n):
        for _ in range(n):
            tick()

    pump(2)

    @pl.when(z % 2 == c)
    def _():
        for ch in range(chunks):
            wbuf[z // 2, c, ch] = wo_ref[:, ch * CHUNK : (ch + 1) * CHUNK]

    def ab_side(yy):
        return send(abuf.at[yy], abuf.at[yy], ab_s.at[1], ab_r.at[1], (other_y, t))

    def lb_core():
        return send(lbsend.at[1 - c], lbhalf.at[2], lb_s.at[0], lb_r.at[0], (d, mate))

    def lb_chip():
        return send(lbhalf.at[0], lbhalf.at[1], lb_s.at[1], lb_r.at[1], (d, 2 * (1 - x) + c))

    def lb_back(core):
        return send(lbfull.at[core], lbfull.at[core], lb_s.at[2], lb_r.at[2], (d, mate))

    def g_side():
        return send(gsend.at[1 - y], grecv, gy_s, gy_r, (other_y, t))

    def g_line(off):
        zt = (z + off) % nz
        return send(gzsend.at[zt], gzrecv.at[z], gz_s, gz_r, (2 * zt + y, t))

    def g_lines():
        whole = gzrecv.at[pl.ds(0, nz - 1)]
        return send(whole, whole, gz_s, gz_r, (other_y, t))

    def share(dx, dy, u):
        zz = jnp.where(dx == 1, 1 - x, x)
        yy = jnp.where(dy == 1, 1 - y, y)
        ch, off, num = cuts[u]
        cols = pl.ds(off, num)
        return send(
            pbuf.at[2 * dx + dy, ch, :, cols],
            prcv.at[2 * dx + dy, ch, :, cols],
            ps_s,
            ps_r.at[u],
            (2 * z + yy, 2 * zz + c),
        )

    def rows_in():
        rows_whole().wait_recv()
        relay(c).start()

    def rows_ready():
        send(x_ref, xbuf.at[y, 1 - c], xs_s.at[0], xs_r.at[0], (d, mate)).wait_recv()
        relay(1 - c).wait_recv()

    def columns(yy, u):
        ch, off, num = cuts[u]
        return pl.ds(pl.multiple_of((yy * chunks + ch) * CHUNK + off, 128), num)

    def final(k):
        src, dst = ((dec_ref, dec_out), (ga_ref, ga_out), (gb_ref, gb_out))[k]
        return pltpu.make_async_copy(src, dst, fin_s.at[k])

    def emit(dy, u):
        cols = columns((y + dy) % 2, u)
        return pltpu.make_async_copy(out_ref.at[:, cols], rows_out.at[:, cols], out_s)

    def unit(blk, u):
        is_near = blk is near
        ch, off, num = cuts[u]
        cols = pl.ds(off, num)
        own_ks = [k for k in range(pieces) if seg_of(k)[0] == ch and seg_of(k)[2] == off]
        upto = 2 * (max(own_ks) + 1)
        if is_near:

            @pl.when(role_m)
            def _():
                arrive("near", blk, upto)

            others = jnp.logical_not(role_m)
        else:

            @pl.when(role_m)
            def _():
                arrive("far_m", blk, upto)

            @pl.when(role_2)
            def _():
                arrive("far_2", blk, upto)

            others = end
        for cc in range(2):
            mine = jnp.logical_and(c + 2 * blk == z, c == cc)

            @pl.when(jnp.logical_and(others, jnp.logical_not(mine)))
            def _():
                for k in own_ks:
                    hop(blk, 2 * k + cc, 3, z_in).wait_recv()

        dx = jnp.where(blk == x, 0, 1)
        for dy in (1, 0):
            yy = (y + dy) % 2
            p = jnp.dot(xbuf[yy, 0], wbuf[blk, 0, ch, :, cols], preferred_element_type=F32)
            p = p + jnp.dot(xbuf[yy, 1], wbuf[blk, 1, ch, :, cols], preferred_element_type=F32)
            if dy == 1:
                pbuf[2 * dx + 1, ch, :, cols] = p.astype(BF16)
                share(dx, 1, u).start()
            else:

                @pl.when(dx == 1)
                def _():
                    pbuf[2, ch, :, cols] = p.astype(BF16)
                    share(1, 0, u).start()

                @pl.when(dx == 0)
                def _():
                    out_ref[:, columns(y, u)] += p

    dp_wait(0, hbuf)
    state = rows_of(hbuf, ndp)
    gains = gain_ref[...].astype(F32)
    line = lax.broadcasted_iota(jnp.int32, gains.shape, 0)
    gain = jnp.concatenate(
        [
            jnp.sum(jnp.where(line == d * (width // 128) + i, gains, 0.0), axis=0, keepdims=True)
            for i in range(width // 128)
        ],
        axis=1,
    )
    fetch(2).wait()
    new_k, new_v = [], []
    factor = 1.0 / math.sqrt(HD)

    for step in range(2):
        squares = jnp.sum(state * state, axis=-1, keepdims=True)
        part = exact_dot(state * gain, wqkv_ref[...])
        both = jnp.concatenate([part, jnp.broadcast_to(squares, (ndp * rolls, 128))], axis=1)
        for i in range(ndp):
            qsend[step, i] = both[i * rolls : (i + 1) * rolls]
        dp_start(2 + 2 * step, lambda p: qsend.at[step, p], qrecv.at[step])
        pump(2)
        qrecv[step, d] = qsend[step, d]
        if step == 1:
            lb_chip().wait_recv()
            lbfull[c] = (lbhalf[0] + lbhalf[1]).astype(BF16)
            lb_back(c).start()
        if step == 0:
            send(others, others, ab_s.at[0], ab_r.at[0], (other_y, t)).wait_recv()
            ab_side(y).start()
            dp_wait(1, statbuf)
            tot = statbuf[0]
            for i in range(1, ndp):
                tot = tot + statbuf[i]
            mean = tot[0:1] / GROUP
            std = jnp.sqrt(jnp.maximum(tot[1:2] / GROUP - mean * mean, 0.09))
            fetch(4).wait()
            for r in range(rolls):
                one, rew = ones[r], rew_ref[r]
                live = live_ref[r].astype(F32)
                adv = (rew - jnp.sum(one * mean, axis=1, keepdims=True)) / jnp.sum(
                    one * std, axis=1, keepdims=True
                )
                slot = lax.broadcasted_iota(jnp.int32, (COMP, 1), 0).astype(F32)
                row_w = jnp.where(slot < live, adv / live, 0.0)
                seg = pl.ds(r * COMP, COMP)
                wt_ref[seg, :] = (row_w * up_ref[seg, :].astype(F32)).astype(BF16)
        dp_wait(2 + 2 * step, qrecv.at[step])
        total = qrecv[step, 0]
        for i in range(1, ndp):
            total = total + qrecv[step, i]
        qkv = total[:, :qkvw] * lax.rsqrt(total[:, qkvw : qkvw + 1] / model + 1e-05)
        new_k.append(qkv[:, HEADS_TP * HD : HEADS_TP * HD + HD])
        new_v.append(qkv[:, HEADS_TP * HD + HD :])
        if step == 0:
            fetch(3).wait()
        for b in range(rolls):
            q = jnp.concatenate(
                [qkv[b : b + 1, h * HD : (h + 1) * HD] for h in range(HEADS_TP)], axis=0
            )
            scores = exact_dot(q, cache_ref[b, :, :HD], NT) * factor
            pos = lax.broadcasted_iota(jnp.int32, scores.shape, 1)
            scores = jnp.where(pos < lens_ref[b], scores, -1e30)
            extra = [
                jnp.sum(q * k[b : b + 1], axis=-1, keepdims=True) * factor for k in new_k
            ]
            top = jnp.max(scores, axis=-1, keepdims=True)
            for e in extra:
                top = jnp.maximum(top, e)
            expo = jnp.exp(scores - top)
            ee = [jnp.exp(e - top) for e in extra]
            den = jnp.sum(expo, axis=-1, keepdims=True)
            for e in ee:
                den = den + e
            att = jnp.dot(
                (expo / den).astype(BF16), cache_ref[b, :, HD:], preferred_element_type=F32
            )
            for e, v in zip(ee, new_v):
                att = att + (e / den).astype(BF16).astype(F32) * v[b : b + 1]
            att = att.astype(BF16).astype(F32)
            asend[step, b : b + 1, :] = jnp.concatenate(
                [att[h : h + 1] for h in range(HEADS_TP)], axis=1
            )
        dp_start(3 + 2 * step, lambda p: asend.at[step], arecv.at[step])
        pump(2)
        arecv[step, d] = asend[step]
        if step == 0:
            ab_side(1 - y).wait_recv()
            at, bt = (
                jnp.concatenate([abuf[i % 2, i // 2, k] for i in range(ndp)], axis=1)
                for k in range(2)
            )
            for k, (m, v) in enumerate(((at, x_ref), (bt, wt_ref))):
                lb = lax.dot_general(m, v[...], NT, preferred_element_type=F32)
                for i in range(2):
                    lbsend[i, k] = lb[:, i * (rows // 2) : (i + 1) * (rows // 2)]
            lb_core().start()
        else:
            lb_back(c).wait_send()
            lb_back(1 - c).wait_recv()
            low_t, back_t = lanes_of(lbfull.at[:, 0], 2), lanes_of(lbfull.at[:, 1], 2)
            ga = adapter_scale * jnp.dot(back_t, x_ref[...], preferred_element_type=F32)
            gb = adapter_scale * jnp.dot(low_t, wt_ref[...], preferred_element_type=F32)
            for i in range(ndp):
                for k, g in enumerate((ga, gb)):
                    part = g[:, i * piece : (i + 1) * piece]
                    gown[i % 2, i // 2, k] = part
                    gsend[i % 2, i // 2, k] = part.astype(BF16)
            g_side().start()
            out_ref[...] = adapter_scale * lax.dot_general(
                low_t, bt, TN, preferred_element_type=F32
            )
        dp_wait(3 + 2 * step, arecv.at[step])
        attended = rows_of(arecv.at[step], ndp).astype(BF16)
        usend[step, :, :width] = jnp.dot(attended, wo_ref[...], preferred_element_type=F32)
        usend[step, :, width:] = jnp.concatenate(
            [
                lax.dot_general(attended, at, NT, preferred_element_type=F32),
                jnp.zeros((ndp * rolls, 128 - rank), F32),
            ],
            axis=1,
        )
        tp_start(step, usend.at[step], urecv.at[step])
        pump(2)
        urecv[step, t] = usend[step]
        if step == 0:
            lb_core().wait_recv()
            lbhalf[0] = lbsend[c] + lbhalf[2]
            lb_chip().start()
            src_t = d // half
            for j in range(per):
                frm = (d % half) * per + j
                same = jnp.logical_and(src_t == t, frm == d)

                @pl.when(jnp.logical_not(same))
                def _():
                    send(b_ref, bdbuf.at[j], bd_s.at[0], bd_r.at[j], (frm, src_t)).wait_recv()

            bd = lanes_of(bdbuf, per)
        tp_wait(step, urecv.at[step])
        upd = urecv[step, 0]
        for i in range(1, ntp):
            upd = upd + urecv[step, i]
        state = state + (
            upd[:, :width] + adapter_scale * exact_dot(upd[:, width : width + rank], bd)
        )

    for i in range(ndp):
        fsend[i] = state[i * rolls : (i + 1) * rolls]
    dp_start(6, lambda p: fsend.at[p], frecv)
    frecv[d] = fsend[d]
    rows_in()
    g_side().wait_recv()
    for i in range(nz):
        gzsend[i] = (gown[y, i] + grecv[i].astype(F32)).astype(BF16)
    for off in range(1, nz):
        g_line(off).start()
    pump(2)
    rows_ready()
    for u in range(len(cuts)):
        unit(near, u)
        pump(2)
    dp_wait(6, frecv)
    for i in range(ndp):
        dec_ref[:, i * width : (i + 1) * width] = frecv[i]
    final(0).start()
    for cp in sent:
        cp.wait_send()
    while clock[0] < 2 * pieces + pieces // 2:
        pump(1)
    unit(far, 0)
    pump(ticks)
    g = gown[y, z] + grecv[z].astype(F32)
    g_lines().wait_recv()
    for off in range(1, nz):
        g = g + gzrecv[(z + nz - off) % nz].astype(F32)
    ga_ref[...] = g[0]
    gb_ref[...] = g[1]
    final(1).start()
    final(2).start()
    for u in range(1, len(cuts)):
        unit(far, u)
    for u in range(len(cuts)):
        ch, off, num = cuts[u]
        three = prcv.at[pl.ds(1, 3), ch, :, pl.ds(off, num)]
        send(three, three, ps_s, ps_r.at[u], (d, mate)).wait_recv()
        for dx, dy in ((1, 0), (0, 1), (1, 1)):
            got = prcv[2 * dx + dy, ch, :, pl.ds(off, num)].astype(F32)
            out_ref[:, columns((y + dy) % 2, u)] += got
        for dy in range(2):
            emit(dy, u).start()

    pltpu.make_async_copy(out_ref, rows_out, out_s).wait()
    for k in range(3):
        final(k).wait()

    def drain(which, full):
        send(full, full, wl_s.at[which], wl_r.at[0, 0, 0], (d, mate)).wait_send()

    @pl.when(z < nz - 1)
    def _():
        drain(0, wbuf.at[0, 0])

    @pl.when(z > 0)
    def _():
        drain(1, wbuf.at[0, 0])

    @pl.when(z % 2 != c)
    def _():
        drain(2, wbuf.at[0, 0])

    @pl.when(role_m)
    def _():
        drain(3, wbuf.at[0])

    @pl.when(jnp.logical_not(end))
    def _():
        drain(4, wbuf.at[0])

    three = pbuf.at[pl.ds(1, 3)]
    send(three, three, ps_s, ps_r.at[0], (d, mate)).wait_send()
    rows_whole().wait_send()
    relay(c).wait_send()
    g_side().wait_send()
    lb_core().wait_send()
    lb_chip().wait_send()
    ab_side(y).wait_send()
    g_lines().wait_send()

    @pl.when(bdst != d)
    def _():
        send(b_ref, bdbuf.at[bslot], bd_s.at[0], bd_r.at[bslot], (bdst, t)).wait_send()


def fused_shards(
    ndp,
    ntp,
    hidden,
    attention_norm_gain,
    query_key_value_weight,
    key_value_cache,
    cache_fill_lengths,
    output_weight_frozen,
    adapter_down_transposed,
    adapter_up_matrix,
    attention_rows,
    upstream,
    rewards,
    prompt_group_index,
    completion_live_lengths,
):
    rolls, model = hidden.shape
    slots = key_value_cache.shape[1]
    width = model // ndp
    rank, _, piece = adapter_down_transposed.shape
    rows, shard = attention_rows.shape
    qkvw = query_key_value_weight.shape[2]
    feats = output_weight_frozen.shape[1]
    chunks = width // CHUNK
    vm = pl.BlockSpec(memory_space=pltpu.VMEM)
    sm = pl.BlockSpec(memory_space=pltpu.SMEM)
    hbm = pl.BlockSpec(memory_space=pltpu.HBM)
    dma = pltpu.SemaphoreType.DMA
    V = pltpu.VMEM
    dec, out, ga, gb = pl.pallas_call(
        lambda *refs: fused_kernel(ndp, ntp, *refs),
        out_shape=(
            pltpu.VMEM((rolls, model), F32),
            pltpu.VMEM((rows, shard), F32),
            pltpu.VMEM((rank, piece), F32),
            pltpu.VMEM((rank, piece), F32),
        ),
        in_specs=[vm, vm, hbm, hbm, sm, hbm, vm, vm, hbm, hbm, sm, sm, sm],
        out_specs=(pl.BlockSpec(memory_space=pl.ANY),) * 4,
        scratch_shapes=[
            V((ndp, rolls, width), F32),
            V((8, 128), F32),
            V((ndp, rolls, width), F32),
            V((2, ndp // 2, 2, rank, piece), BF16),
            V((width // piece, rank, piece), BF16),
            V((ndp, 8, 128), F32),
            V((2, ndp, rolls, qkvw + 128), F32),
            V((2, ndp, rolls, qkvw + 128), F32),
            V((2, rolls, feats), F32),
            V((2, ndp, rolls, feats), F32),
            V((2, ndp * rolls, width + 128), F32),
            V((2, ntp, ndp * rolls, width + 128), F32),
            V((ndp, rolls, width), F32),
            V((ndp, rolls, width), F32),
            V((2, 2, rank, rows // 2), F32),
            V((3, 2, rank, rows // 2), F32),
            V((2, 2, rank, rows // 2), BF16),
            V((2, ndp // 2, 2, rank, piece), F32),
            V((2, ndp // 2, 2, rank, piece), BF16),
            V((ndp // 2, 2, rank, piece), BF16),
            V((ndp // 2, 2, rank, piece), BF16),
            V((ndp // 2, 2, rank, piece), BF16),
            V((rows, shard), BF16),
            V((2, 2, rows, shard), BF16),
            V((2, 2, chunks, feats, CHUNK), BF16),
            V((4, chunks, rows, CHUNK), BF16),
            V((4, chunks, rows, CHUNK), BF16),
            dma((7,)),
            dma((7,)),
            dma((2,)),
            dma((2,)),
            dma((2,)),
            dma((width // piece,)),
            dma((3,)),
            dma((3,)),
            dma((5,)),
            dma((2, 2, chunks * SEGS)),
            dma,
            dma((chunks - 1 + CHUNK // 128,)),
            dma,
            dma,
            dma,
            dma,
            dma((3,)),
            dma((3,)),
            dma((2,)),
            dma((2,)),
            V((feats, width), BF16),
            V((rows, shard), BF16),
            V((width, qkvw), BF16),
            V((rolls, slots, 2 * HD), BF16),
            V((rows, shard), BF16),
            dma((5,)),
            V((rows, shard), F32),
            V((rolls, model), F32),
            V((rank, piece), F32),
            V((rank, piece), F32),
            dma,
            dma((3,)),
        ],
        compiler_params=pltpu.CompilerParams(
            collective_id=0, has_side_effects=True, vmem_limit_bytes=64815104
        ),
    )(
        hidden,
        attention_norm_gain.reshape(model // 128, 128),
        query_key_value_weight[:, 0, :],
        key_value_cache[:, :, 0, :],
        cache_fill_lengths,
        output_weight_frozen[0],
        adapter_down_transposed[:, 0, :],
        adapter_up_matrix[:, 0, :],
        attention_rows,
        upstream,
        rewards,
        prompt_group_index,
        completion_live_lengths,
    )
    return dec, out, ga[:, None, :], gb[:, None, :]


def shards(
    hidden,
    attention_norm_gain,
    query_key_value_weight,
    key_value_cache,
    cache_fill_lengths,
    output_weight_frozen,
    adapter_down_transposed,
    adapter_up_matrix,
    attention_rows,
    upstream,
    rewards,
    prompt_group_index,
    completion_live_lengths,
):
    a_piece, b_piece = (
        lax.all_gather(adapter_down_transposed, "dp", axis=2, tiled=True),
        lax.all_gather(adapter_up_matrix, "dp", axis=2, tiled=True),
    )
    b_whole = lax.all_gather(b_piece, "tp", axis=1, tiled=True)
    up_matrix_flat = b_whole.reshape(b_whole.shape[0], -1).astype(jnp.float32)
    a_local = a_piece[:, 0, :]
    up_matrix_columns = b_piece[:, 0, :]
    w_rows = query_key_value_weight[:, 0, :].astype(jnp.float32)
    w_cols = output_weight_frozen[0]
    query_width = HEADS_TP * HD
    local_rolls = hidden.shape[0]
    decode_state = hidden.astype(jnp.float32)
    keys_new = []
    values_new = []
    for step in range(2):
        normed = rms_norm(decode_state, attention_norm_gain)
        spread = lax.all_to_all(normed, "dp", split_axis=1, concat_axis=0, tiled=True)
        partial_value = jnp.dot(spread, w_rows, precision=lax.Precision.HIGHEST)
        qkv = lax.psum_scatter(partial_value, "dp", scatter_dimension=0, tiled=True)
        query = qkv[:, :query_width].reshape(local_rolls, HEADS_TP, HD)
        keys_new.append(qkv[:, query_width : query_width + HD])
        values_new.append(qkv[:, query_width + HD :])
        attended = attend(
            query,
            key_value_cache[:, :, 0, :],
            cache_fill_lengths,
            jnp.stack(keys_new, axis=1),
            jnp.stack(values_new, axis=1),
        )
        columns = jnp.dot(
            lax.all_gather(attended, "dp", axis=0, tiled=True),
            w_cols,
            preferred_element_type=jnp.float32,
        )
        returned_values = lax.all_to_all(columns, "dp", split_axis=0, concat_axis=1, tiled=True)
        low_rank_decode = jnp.dot(attended, a_local.T, preferred_element_type=jnp.float32)
        state_update = returned_values + adapter_scale * jnp.dot(
            low_rank_decode, up_matrix_flat, precision=lax.Precision.HIGHEST
        )
        decode_state = decode_state + lax.psum(state_update, "tp")
    groups = local_rolls * lax.axis_size("dp") // GROUP
    onehot = (prompt_group_index[:, None] == jnp.arange(groups, dtype=jnp.int32)[None, :]).astype(
        jnp.float32
    )
    totals, squares = lax.psum(
        (
            jnp.sum(onehot * rewards[:, None], axis=0),
            jnp.sum(onehot * (rewards * rewards)[:, None], axis=0),
        ),
        "dp",
    )
    mean = totals / GROUP
    std = jnp.sqrt(jnp.maximum(squares / GROUP - mean * mean, 0.09))
    advantage = (rewards - jnp.sum(onehot * mean[None, :], axis=1)) / jnp.sum(
        onehot * std[None, :], axis=1
    )
    per_roll = advantage / completion_live_lengths.astype(jnp.float32)
    rows = attention_rows.shape[0]
    slot = jnp.arange(rows, dtype=jnp.int32) % COMP
    limit = jnp.repeat(completion_live_lengths, COMP)
    row_w = jnp.where(slot < limit, jnp.repeat(per_roll, COMP), 0.0)
    whole_rows = jnp.dot(
        attention_rows,
        lax.all_gather(output_weight_frozen, "dp", axis=2, tiled=True)[0],
        preferred_element_type=jnp.float32,
    )
    frozen_output_rows = lax.psum_scatter(whole_rows, "tp", scatter_dimension=1, tiled=True)
    low_sum = lax.psum(jnp.dot(attention_rows, a_local.T, preferred_element_type=jnp.float32), "tp")
    low_rank_rows = low_sum.astype(jnp.bfloat16)
    adapted_output_rows = frozen_output_rows + adapter_scale * jnp.dot(
        low_rank_rows, up_matrix_columns, preferred_element_type=jnp.float32
    )
    advantage_weighted = (row_w[:, None] * upstream.astype(jnp.float32)).astype(jnp.bfloat16)
    backward_result = lax.psum(
        jnp.dot(advantage_weighted, up_matrix_columns.T, preferred_element_type=jnp.float32), "tp"
    ).astype(jnp.bfloat16)
    down_gradient = adapter_scale * lax.dot_general(
        backward_result,
        attention_rows,
        (((0,), (0,)), ((), ())),
        preferred_element_type=jnp.float32,
    )
    up_gradient = adapter_scale * lax.dot_general(
        low_rank_rows,
        advantage_weighted,
        (((0,), (0,)), ((), ())),
        preferred_element_type=jnp.float32,
    )
    grad_a_part, grad_b_part = (
        lax.psum_scatter(down_gradient[:, None, :], "dp", scatter_dimension=2, tiled=True),
        lax.psum_scatter(up_gradient[:, None, :], "dp", scatter_dimension=2, tiled=True),
    )
    return (decode_state, adapted_output_rows, grad_a_part, grad_b_part)


def solution(mesh):
    placed = (
        P("dp", None),
        P(),
        P("dp", "tp", None),
        P("dp", None, "tp", None),
        P("dp"),
        P("tp", None, "dp"),
        P(None, "tp", "dp"),
        P(None, "tp", "dp"),
        P("dp", "tp"),
        P("dp", "tp"),
        P("dp"),
        P("dp"),
        P("dp"),
    )
    ndp, ntp = mesh.shape["dp"], mesh.shape["tp"]

    def body(*args):
        width = args[5].shape[2]
        piece = args[6].shape[2]
        if ntp == 4 and ndp == 8 and piece % 128 == 0 and width % CHUNK == 0:
            return fused_shards(ndp, ntp, *args)
        return shards(*args)

    return jax.shard_map(
        body,
        mesh=mesh,
        in_specs=placed,
        out_specs=(P("dp", None), P("dp", "tp"), P(None, "tp", "dp"), P(None, "tp", "dp")),
        check_vma=False,
    )
```

```python
import math

import jax
import jax.numpy as jnp
from jax import lax
from jax.experimental import pallas as pl
from jax.experimental.pallas import tpu as pltpu
from jax.sharding import PartitionSpec as P

HD = 128
HEADS_TP = 8
GROUP = 4
COMP = 256


adapter_scale = 2.0


def rms_norm(decode_state, gain):
    scale = lax.rsqrt(jnp.mean(decode_state * decode_state, axis=-1, keepdims=True) + 1e-05)
    return decode_state * scale * gain.astype(jnp.float32)


def attend(query, cache, lengths, new_keys, new_values):
    head = query.shape[-1]
    slots = cache.shape[1]
    factor = 1.0 / math.sqrt(head)
    keys = cache[:, :, :head].astype(jnp.float32)
    values = cache[:, :, head:]
    scores = jnp.einsum("bhd,bcd->bhc", query, keys, precision=lax.Precision.HIGHEST) * factor
    valid = jnp.arange(slots, dtype=jnp.int32)[None, None, :] < lengths[:, None, None]
    scores = jnp.where(valid, scores, -1e30)
    extra = jnp.einsum("bhd,bed->bhe", query, new_keys, precision=lax.Precision.HIGHEST) * factor
    joined = jnp.concatenate([scores, extra], axis=-1)
    top = jnp.max(joined, axis=-1, keepdims=True)
    expo = jnp.exp(joined - top)
    probs = (expo / jnp.sum(expo, axis=-1, keepdims=True)).astype(jnp.bfloat16)
    out = jnp.einsum("bhc,bcd->bhd", probs[..., :slots], values, preferred_element_type=jnp.float32)
    out = out + jnp.einsum(
        "bhe,bed->bhd",
        probs[..., slots:].astype(jnp.float32),
        new_values,
        precision=lax.Precision.HIGHEST,
    )
    return out.astype(jnp.bfloat16).reshape(query.shape[0], -1)


MESH = pl.DeviceIdType.MESH
F32 = jnp.float32
BF16 = jnp.bfloat16
NT = (((1,), (1,)), ((), ()))
TN = (((0,), (0,)), ((), ()))
CHUNK = 256
SEGS = 4
ROW_PARTS = 8


def split3(v):
    hi = v.astype(BF16)
    rest = v - hi.astype(F32)
    mid = rest.astype(BF16)
    lo = (rest - mid.astype(F32)).astype(BF16)
    return jnp.concatenate([hi, mid, lo], axis=0)


def exact_dot(v, w, dims=(((1,), (0,)), ((), ()))):
    n = v.shape[0]
    r = lax.dot_general(split3(v), w, dims, preferred_element_type=F32)
    return r[:n] + r[n : 2 * n] + r[2 * n :]


def rows_of(ref, n):
    return jnp.concatenate([ref[i] for i in range(n)], axis=0)


def lanes_of(ref, n):
    return jnp.concatenate([ref[i] for i in range(n)], axis=1)


def fused_kernel(
    ndp,
    ntp,
    h_ref,
    gain_ref,
    wqkv_in,
    cache_in,
    lens_ref,
    wo_in,
    a_ref,
    b_ref,
    x_in,
    up_in,
    rew_ref,
    idx_ref,
    live_ref,
    dec_out,
    rows_out,
    ga_out,
    gb_out,
    hsend,
    stats_ref,
    hbuf,
    abuf,
    bdbuf,
    statbuf,
    qsend,
    qside,
    qline,
    qrecv,
    asend,
    arecv,
    usend,
    urecv,
    fsend,
    frecv,
    lbsend,
    lbhalf,
    lbfull,
    gown,
    gsend,
    grecv,
    gzsend,
    gzrecv,
    wt_ref,
    xbuf,
    wbuf,
    pbuf,
    prcv,
    ds_s,
    ds_r,
    ts_s,
    ts_r,
    bd_s,
    bd_r,
    xs_s,
    xs_r,
    wl_s,
    wl_r,
    ps_s,
    ps_r,
    gy_s,
    gy_r,
    gz_s,
    gz_r,
    lb_s,
    lb_r,
    ab_s,
    ab_r,
    wo_ref,
    x_ref,
    wqkv_ref,
    cache_ref,
    up_ref,
    in_s,
    out_ref,
    dec_ref,
    ga_ref,
    gb_ref,
    out_s,
    fin_s,
    qy_s,
    qy_r,
    qz_s,
    qz_r,
    ay_s,
    ay_r,
    az_s,
    az_r,
):
    d = lax.axis_index("dp")
    t = lax.axis_index("tp")
    z, y = d // 2, d % 2
    x, c = t // 2, t % 2
    nz = ndp // 2
    rolls, model = h_ref.shape
    width = model // ndp
    rank = a_ref.shape[0]
    piece = a_ref.shape[1]
    chunks = wo_ref.shape[1] // CHUNK
    qkvw = wqkv_ref.shape[1]
    rows = x_ref.shape[0]
    mate = 2 * x + (1 - c)
    other_y = 2 * z + (1 - y)

    def fetch(k):
        src, dst = (
            (wo_in, wo_ref),
            (x_in, x_ref),
            (wqkv_in, wqkv_ref),
            (cache_in, cache_ref),
            (up_in, up_ref),
        )[k]
        return pltpu.make_async_copy(src, dst, in_s.at[k])

    for k in range(5):
        fetch(k).start()
    barrier = pltpu.get_barrier_semaphore()
    for i in range(ndp):
        for j in range(ntp):
            if i or j:
                pl.semaphore_signal(
                    barrier,
                    inc=1,
                    device_id=((d + i) % ndp, (t + j) % ntp),
                    device_id_type=MESH,
                )
    pl.semaphore_wait(barrier, ndp * ntp - 1)

    sent = []

    def send(src, dst, s, r, dev):
        cp = pltpu.make_async_remote_copy(
            src_ref=src, dst_ref=dst, send_sem=s, recv_sem=r, device_id=dev, device_id_type=MESH
        )
        return cp

    def dp_start(e, src, dst):
        for off in range(1, ndp):
            peer = (d + off) % ndp
            send(src(peer), dst.at[d], ds_s.at[e], ds_r.at[e], (peer, t)).start()
        whole = dst.at[pl.ds(0, ndp - 1)]
        sent.append(send(whole, whole, ds_s.at[e], ds_r.at[e], (d, (t + 1) % ntp)))

    def dp_wait(e, dst):
        whole = dst.at[pl.ds(0, ndp - 1)]
        send(whole, whole, ds_s.at[e], ds_r.at[e], (d, (t + 1) % ntp)).wait_recv()

    def tp_start(e, src, dst):
        for off in range(1, ntp):
            peer = (t + off) % ntp
            send(src, dst.at[t], ts_s.at[e], ts_r.at[e], (d, peer)).start()
        whole = dst.at[pl.ds(0, ntp - 1)]
        sent.append(send(whole, whole, ts_s.at[e], ts_r.at[e], (d, (t + 1) % ntp)))

    def tp_wait(e, dst):
        whole = dst.at[pl.ds(0, ntp - 1)]
        send(whole, whole, ts_s.at[e], ts_r.at[e], (d, (t + 1) % ntp)).wait_recv()

    for i in range(ndp):
        hsend[i] = h_ref[:, i * width : (i + 1) * width]
    lane = lax.broadcasted_iota(jnp.int32, (1, 128), 1)
    ones = [jnp.where(lane == idx_ref[r], 1.0, 0.0) for r in range(rolls)]
    stats_ref[...] = jnp.zeros_like(stats_ref)
    for r in range(rolls):
        stats_ref[0:1] += ones[r] * rew_ref[r]
        stats_ref[1:2] += ones[r] * (rew_ref[r] * rew_ref[r])

    dp_start(0, lambda p: hsend.at[p], hbuf)
    hbuf[d] = hsend[d]
    abuf[y, z, 0] = a_ref[...]
    abuf[y, z, 1] = b_ref[...]
    for k, ref in enumerate((a_ref, b_ref)):
        for off in range(1, nz):
            peer = 2 * ((z + off) % nz) + y
            send(ref, abuf.at[y, z, k], ab_s.at[0], ab_r.at[0], (peer, t)).start()
    others = abuf.at[0, pl.ds(0, nz - 1)]
    sent.append(send(others, others, ab_s.at[0], ab_r.at[0], (other_y, t)))
    dp_start(1, lambda p: stats_ref, statbuf)
    statbuf[d] = stats_ref[...]
    per = width // piece
    half = ndp // per
    src_t = d // half

    def up_block(tj):
        return send(bdbuf, bdbuf, bd_s, bd_r, (d, tj))

    fetch(0).wait()
    fetch(1).wait()
    xcp = send(x_ref, xbuf.at[y, c], xs_s.at[0], xs_r.at[0], (d, mate))
    xcp.start()
    sent.append(xcp)
    xbuf[y, c] = x_ref[...]

    def row_send(k):
        part = rows // ROW_PARTS
        if k >= ROW_PARTS:
            return
        seg = pl.ds(k * part, part)
        send(
            x_ref.at[seg], xbuf.at[y, c, seg], xs_s.at[1], xs_r.at[1], (other_y, t)
        ).start()

    def rows_whole():
        return send(x_ref, xbuf.at[1 - y, c], xs_s.at[1], xs_r.at[1], (other_y, t))

    def relay(dst_core):
        return send(
            xbuf.at[1 - y, c], xbuf.at[1 - y, dst_core], xs_s.at[2], xs_r.at[2], (d, mate)
        )

    feats = wo_ref.shape[0]
    pieces = chunks * SEGS
    near, far = z // 2, 1 - z // 2
    end = jnp.logical_or(z == 0, z == nz - 1)
    role_m = jnp.logical_and(jnp.logical_not(end), c == z // 2)
    role_2 = jnp.logical_and(jnp.logical_not(end), c != z // 2)
    z_up, z_dn = jnp.minimum(z + 1, nz - 1), jnp.maximum(z - 1, 0)
    z_in = jnp.where(z < 2, z_up, z_dn)
    z_out = jnp.where(z < 2, z_dn, z_up)

    cuts = [(ch, 0, CHUNK) for ch in range(chunks - 1)]
    cuts += [(chunks - 1, h * 128, 128) for h in range(CHUNK // 128)]

    def seg_of(k):
        ch, part = k // SEGS, k % SEGS
        if ch < chunks - 1:
            size = feats // SEGS
            return ch, pl.ds(part * size, size), 0, CHUNK
        halves = CHUNK // 128
        size = feats * halves // SEGS
        per_half = SEGS // halves
        return ch, pl.ds((part % per_half) * size, size), (part // per_half) * 128, 128

    def own(k, which, zt):
        ch, seg, off, num = seg_of(k)
        return send(
            wo_ref.at[seg, pl.ds(ch * CHUNK + off, num)],
            wbuf.at[z // 2, c, ch, seg, pl.ds(off, num)],
            wl_s.at[which],
            wl_r.at[z // 2, c, k],
            (2 * zt + y, 2 * x + z % 2),
        )

    def hop(blk, j, which, zt):
        k, cc = j // 2, j % 2
        ch, seg, off, num = seg_of(k)
        ref = wbuf.at[blk, cc, ch, seg, pl.ds(off, num)]
        return send(ref, ref, wl_s.at[which], wl_r.at[blk, cc, k], (2 * zt + y, t))

    def own_tick(k):
        @pl.when(z < nz - 1)
        def _():
            own(k, 0, z_up).start()

        @pl.when(z > 0)
        def _():
            own(k, 1, z_dn).start()

        @pl.when(z % 2 != c)
        def _():
            own(k, 2, z).start()

    waited = {"near": 0, "far_m": 0, "far_2": 0}

    def arrive(name, blk, upto):
        for j in range(waited[name], upto):
            hop(blk, j, 3, z_in).wait_recv()
        waited[name] = max(waited[name], upto)

    def relay_tick(name, blk, lo, hi, which, zt):
        hi = min(hi, 2 * pieces)
        arrive(name, blk, hi)
        for j in range(lo, hi):
            hop(blk, j, which, zt).start()

    clock = [0]
    ticks = 3 * pieces

    def tick():
        n = clock[0]
        if n >= ticks:
            return
        clock[0] += 1
        if n < pieces:
            own_tick(n)
            row_send(n)
            return
        m = n - pieces

        @pl.when(role_m)
        def _():
            if m < pieces:
                relay_tick("near", near, 2 * m, 2 * m + 2, 3, z_in)
                relay_tick("far_m", far, 2 * m, 2 * m + 2, 4, z_out)

        if m >= pieces:

            @pl.when(role_2)
            def _():
                relay_tick("far_2", far, 2 * (m - pieces), 2 * (m - pieces) + 2, 4, z_out)

    def pump(n):
        for _ in range(n):
            tick()

    pump(2)

    @pl.when(z % 2 == c)
    def _():
        for ch in range(chunks):
            wbuf[z // 2, c, ch] = wo_ref[:, ch * CHUNK : (ch + 1) * CHUNK]

    def q_side(step):
        return send(qsend.at[step, 1 - y], qside.at[step], qy_s.at[step], qy_r.at[step], (other_y, t))

    def q_lines(step):
        whole = qrecv.at[step, pl.ds(0, nz - 1)]
        return send(whole, whole, qz_s.at[step], qz_r.at[step], (other_y, t))

    def a_side(step, yy):
        ref = arecv.at[step, yy]
        return send(ref, ref, ay_s.at[step], ay_r.at[step], (other_y, t))

    def a_lines(step):
        whole = arecv.at[step, 0, pl.ds(0, nz - 1)]
        return send(whole, whole, az_s.at[step], az_r.at[step], (other_y, t))

    def ab_side(yy):
        return send(abuf.at[yy], abuf.at[yy], ab_s.at[1], ab_r.at[1], (other_y, t))

    def lb_core():
        return send(lbsend.at[1 - c], lbhalf.at[2], lb_s.at[0], lb_r.at[0], (d, mate))

    def lb_chip():
        return send(lbhalf.at[0], lbhalf.at[1], lb_s.at[1], lb_r.at[1], (d, 2 * (1 - x) + c))

    def lb_back(core):
        return send(lbfull.at[core], lbfull.at[core], lb_s.at[2], lb_r.at[2], (d, mate))

    def g_side():
        return send(gsend.at[1 - y], grecv, gy_s, gy_r, (other_y, t))

    def g_line(off):
        zt = (z + off) % nz
        return send(gzsend.at[zt], gzrecv.at[z], gz_s, gz_r, (2 * zt + y, t))

    def g_lines():
        whole = gzrecv.at[pl.ds(0, nz - 1)]
        return send(whole, whole, gz_s, gz_r, (other_y, t))

    def share(dx, dy, u):
        zz = jnp.where(dx == 1, 1 - x, x)
        yy = jnp.where(dy == 1, 1 - y, y)
        ch, off, num = cuts[u]
        cols = pl.ds(off, num)
        return send(
            pbuf.at[2 * dx + dy, ch, :, cols],
            prcv.at[2 * dx + dy, ch, :, cols],
            ps_s,
            ps_r.at[u],
            (2 * z + yy, 2 * zz + c),
        )

    def rows_in():
        rows_whole().wait_recv()
        relay(c).start()

    def rows_ready():
        send(x_ref, xbuf.at[y, 1 - c], xs_s.at[0], xs_r.at[0], (d, mate)).wait_recv()
        relay(1 - c).wait_recv()

    def columns(yy, u):
        ch, off, num = cuts[u]
        return pl.ds(pl.multiple_of((yy * chunks + ch) * CHUNK + off, 128), num)

    def final(k):
        src, dst = ((dec_ref, dec_out), (ga_ref, ga_out), (gb_ref, gb_out))[k]
        return pltpu.make_async_copy(src, dst, fin_s.at[k])

    def emit(dy, u):
        cols = columns((y + dy) % 2, u)
        return pltpu.make_async_copy(out_ref.at[:, cols], rows_out.at[:, cols], out_s)

    def unit(blk, u):
        is_near = blk is near
        ch, off, num = cuts[u]
        cols = pl.ds(off, num)
        own_ks = [k for k in range(pieces) if seg_of(k)[0] == ch and seg_of(k)[2] == off]
        upto = 2 * (max(own_ks) + 1)
        if is_near:

            @pl.when(role_m)
            def _():
                arrive("near", blk, upto)

            others = jnp.logical_not(role_m)
        else:

            @pl.when(role_m)
            def _():
                arrive("far_m", blk, upto)

            @pl.when(role_2)
            def _():
                arrive("far_2", blk, upto)

            others = end
        for cc in range(2):
            mine = jnp.logical_and(c + 2 * blk == z, c == cc)

            @pl.when(jnp.logical_and(others, jnp.logical_not(mine)))
            def _():
                for k in own_ks:
                    hop(blk, 2 * k + cc, 3, z_in).wait_recv()

        dx = jnp.where(blk == x, 0, 1)
        for dy in (1, 0):
            yy = (y + dy) % 2
            p = jnp.dot(xbuf[yy, 0], wbuf[blk, 0, ch, :, cols], preferred_element_type=F32)
            p = p + jnp.dot(xbuf[yy, 1], wbuf[blk, 1, ch, :, cols], preferred_element_type=F32)
            if dy == 1:
                pbuf[2 * dx + 1, ch, :, cols] = p.astype(BF16)
                share(dx, 1, u).start()
            else:

                @pl.when(dx == 1)
                def _():
                    pbuf[2, ch, :, cols] = p.astype(BF16)
                    share(1, 0, u).start()

                @pl.when(dx == 0)
                def _():
                    out_ref[:, columns(y, u)] += p

    dp_wait(0, hbuf)
    state = jnp.concatenate([hbuf[i].astype(F32) for i in range(ndp)], axis=0)
    gains = gain_ref[...].astype(F32)
    line = lax.broadcasted_iota(jnp.int32, gains.shape, 0)
    gain = jnp.concatenate(
        [
            jnp.sum(jnp.where(line == d * (width // 128) + i, gains, 0.0), axis=0, keepdims=True)
            for i in range(width // 128)
        ],
        axis=1,
    )
    fetch(2).wait()
    new_k, new_v = [], []
    factor = 1.0 / math.sqrt(HD)

    for step in range(2):
        squares = jnp.sum(state * state, axis=-1, keepdims=True)
        part = exact_dot(state * gain, wqkv_ref[...])
        both = jnp.concatenate([part, jnp.broadcast_to(squares, (ndp * rolls, 128))], axis=1)
        for i in range(ndp):
            qsend[step, i % 2, i // 2] = both[i * rolls : (i + 1) * rolls]
        q_side(step).start()
        pump(1)
        if step == 1:
            lb_chip().wait_recv()
            lbfull[c] = (lbhalf[0] + lbhalf[1]).astype(BF16)
            lb_back(c).start()
        if step == 0:
            send(others, others, ab_s.at[0], ab_r.at[0], (other_y, t)).wait_recv()
            ab_side(y).start()
            dp_wait(1, statbuf)
            tot = statbuf[0]
            for i in range(1, ndp):
                tot = tot + statbuf[i]
            mean = tot[0:1] / GROUP
            std = jnp.sqrt(jnp.maximum(tot[1:2] / GROUP - mean * mean, 0.09))
            fetch(4).wait()
            for r in range(rolls):
                one, rew = ones[r], rew_ref[r]
                live = live_ref[r].astype(F32)
                adv = (rew - jnp.sum(one * mean, axis=1, keepdims=True)) / jnp.sum(
                    one * std, axis=1, keepdims=True
                )
                slot = lax.broadcasted_iota(jnp.int32, (COMP, 1), 0).astype(F32)
                row_w = jnp.where(slot < live, adv / live, 0.0)
                seg = pl.ds(r * COMP, COMP)
                wt_ref[seg, :] = (row_w * up_ref[seg, :].astype(F32)).astype(BF16)
        q_side(step).wait_recv()
        for i in range(nz):
            qline[step, i] = qsend[step, y, i] + qside[step, i]
        for off in range(1, nz):
            zt = (z + off) % nz
            src, dst = qline.at[step, zt], qrecv.at[step, z]
            send(src, dst, qz_s.at[step], qz_r.at[step], (2 * zt + y, t)).start()
        pump(2)
        q_lines(step).wait_recv()
        total = qline[step, z]
        for off in range(1, nz):
            total = total + qrecv[step, (z + off) % nz]
        qkv = total[:, :qkvw] * lax.rsqrt(total[:, qkvw : qkvw + 1] / model + 1e-05)
        new_k.append(qkv[:, HEADS_TP * HD : HEADS_TP * HD + HD])
        new_v.append(qkv[:, HEADS_TP * HD + HD :])
        if step == 0:
            fetch(3).wait()
        heads = []
        for b in range(rolls):
            q = jnp.concatenate(
                [qkv[b : b + 1, h * HD : (h + 1) * HD] for h in range(HEADS_TP)], axis=0
            )
            scores = exact_dot(q, cache_ref[b, :, :HD], NT) * factor
            pos = lax.broadcasted_iota(jnp.int32, scores.shape, 1)
            scores = jnp.where(pos < lens_ref[b], scores, -1e30)
            extra = [
                jnp.sum(q * k[b : b + 1], axis=-1, keepdims=True) * factor for k in new_k
            ]
            top = jnp.max(scores, axis=-1, keepdims=True)
            for e in extra:
                top = jnp.maximum(top, e)
            expo = jnp.exp(scores - top)
            ee = [jnp.exp(e - top) for e in extra]
            den = jnp.sum(expo, axis=-1, keepdims=True)
            for e in ee:
                den = den + e
            att = jnp.dot(
                (expo / den).astype(BF16), cache_ref[b, :, HD:], preferred_element_type=F32
            )
            for e, v in zip(ee, new_v):
                att = att + (e / den).astype(BF16).astype(F32) * v[b : b + 1]
            heads.append(jnp.concatenate([att[h : h + 1] for h in range(HEADS_TP)], axis=1))
        asend[step] = jnp.concatenate(heads, axis=0).astype(BF16)
        for off in range(1, nz):
            zt = (z + off) % nz
            send(
                asend.at[step], arecv.at[step, y, z], az_s.at[step], az_r.at[step], (2 * zt + y, t)
            ).start()
        pump(1)
        arecv[step, y, z] = asend[step]
        if step == 0:
            ab_side(1 - y).wait_recv()
            at, bt = (
                jnp.concatenate([abuf[i % 2, i // 2, k] for i in range(ndp)], axis=1)
                for k in range(2)
            )

            @pl.when(t == src_t)
            def _():
                for j in range(per):
                    bdbuf[j] = abuf[j % 2, (d % half) * (per // 2) + j // 2, 1]
                for off in range(1, ntp):
                    up_block((t + off) % ntp).start()

            for k, (m, v) in enumerate(((at, x_ref), (bt, wt_ref))):
                lb = lax.dot_general(m, v[...], NT, preferred_element_type=F32)
                for i in range(2):
                    lbsend[i, k] = lb[:, i * (rows // 2) : (i + 1) * (rows // 2)]
            lb_core().start()
        else:
            lb_back(c).wait_send()
            lb_back(1 - c).wait_recv()
            low_t, back_t = lanes_of(lbfull.at[:, 0], 2), lanes_of(lbfull.at[:, 1], 2)
            ga = adapter_scale * jnp.dot(back_t, x_ref[...], preferred_element_type=F32)
            gb = adapter_scale * jnp.dot(low_t, wt_ref[...], preferred_element_type=F32)
            for i in range(ndp):
                for k, g in enumerate((ga, gb)):
                    part = g[:, i * piece : (i + 1) * piece]
                    gown[i % 2, i // 2, k] = part
                    gsend[i % 2, i // 2, k] = part.astype(BF16)
            g_side().start()
            out_ref[...] = adapter_scale * lax.dot_general(
                low_t, bt, TN, preferred_element_type=F32
            )
        a_lines(step).wait_recv()
        a_side(step, y).start()
        pump(1)
        a_side(step, 1 - y).wait_recv()
        attended = jnp.concatenate(
            [arecv[step, i % 2, i // 2].astype(F32) for i in range(ndp)], axis=0
        ).astype(BF16)
        usend[step, :, :width] = jnp.dot(attended, wo_ref[...], preferred_element_type=F32)
        usend[step, :, width:] = jnp.concatenate(
            [
                lax.dot_general(attended, at, NT, preferred_element_type=F32),
                jnp.zeros((ndp * rolls, 128 - rank), F32),
            ],
            axis=1,
        )
        tp_start(step, usend.at[step], urecv.at[step])
        pump(2)
        urecv[step, t] = usend[step]
        if step == 0:
            lb_core().wait_recv()
            lbhalf[0] = lbsend[c] + lbhalf[2]
            lb_chip().start()

            @pl.when(t != src_t)
            def _():
                up_block(src_t).wait_recv()

            bd = lanes_of(bdbuf, per)
        tp_wait(step, urecv.at[step])
        upd = urecv[step, 0]
        for i in range(1, ntp):
            upd = upd + urecv[step, i]
        state = state + (
            upd[:, :width] + adapter_scale * exact_dot(upd[:, width : width + rank], bd)
        )

    for i in range(ndp):
        fsend[i] = state[i * rolls : (i + 1) * rolls]
    dp_start(2, lambda p: fsend.at[p], frecv)
    frecv[d] = fsend[d]
    rows_in()
    g_side().wait_recv()
    for i in range(nz):
        gzsend[i] = (gown[y, i] + grecv[i].astype(F32)).astype(BF16)
    for off in range(1, nz):
        g_line(off).start()
    pump(2)
    rows_ready()
    for u in range(len(cuts)):
        unit(near, u)
        pump(2)
    dp_wait(2, frecv)
    for i in range(ndp):
        dec_ref[:, i * width : (i + 1) * width] = frecv[i]
    final(0).start()
    for cp in sent:
        cp.wait_send()
    while clock[0] < 2 * pieces + pieces // 2:
        pump(1)
    unit(far, 0)
    pump(ticks)
    g = gown[y, z] + grecv[z].astype(F32)
    g_lines().wait_recv()
    for off in range(1, nz):
        g = g + gzrecv[(z + nz - off) % nz].astype(F32)
    ga_ref[...] = g[0]
    gb_ref[...] = g[1]
    final(1).start()
    final(2).start()
    for u in range(1, len(cuts)):
        unit(far, u)
    for u in range(len(cuts)):
        ch, off, num = cuts[u]
        three = prcv.at[pl.ds(1, 3), ch, :, pl.ds(off, num)]
        send(three, three, ps_s, ps_r.at[u], (d, mate)).wait_recv()
        for dx, dy in ((1, 0), (0, 1), (1, 1)):
            got = prcv[2 * dx + dy, ch, :, pl.ds(off, num)].astype(F32)
            out_ref[:, columns((y + dy) % 2, u)] += got
        for dy in range(2):
            emit(dy, u).start()

    pltpu.make_async_copy(out_ref, rows_out, out_s).wait()
    for k in range(3):
        final(k).wait()

    def drain(which, full):
        send(full, full, wl_s.at[which], wl_r.at[0, 0, 0], (d, mate)).wait_send()

    @pl.when(z < nz - 1)
    def _():
        drain(0, wbuf.at[0, 0])

    @pl.when(z > 0)
    def _():
        drain(1, wbuf.at[0, 0])

    @pl.when(z % 2 != c)
    def _():
        drain(2, wbuf.at[0, 0])

    @pl.when(role_m)
    def _():
        drain(3, wbuf.at[0])

    @pl.when(jnp.logical_not(end))
    def _():
        drain(4, wbuf.at[0])

    three = pbuf.at[pl.ds(1, 3)]
    send(three, three, ps_s, ps_r.at[0], (d, mate)).wait_send()
    rows_whole().wait_send()
    relay(c).wait_send()
    g_side().wait_send()
    for step in range(2):
        q_side(step).wait_send()
        q_lines(step).wait_send()
        a_side(step, y).wait_send()
        a_lines(step).wait_send()
    lb_core().wait_send()
    lb_chip().wait_send()
    ab_side(y).wait_send()
    g_lines().wait_send()

    @pl.when(t == src_t)
    def _():
        copies = wo_ref.at[pl.ds(0, (ntp - 1) * rank)]
        send(copies, copies, bd_s, bd_r, (d, mate)).wait_send()


def fused_shards(
    ndp,
    ntp,
    hidden,
    attention_norm_gain,
    query_key_value_weight,
    key_value_cache,
    cache_fill_lengths,
    output_weight_frozen,
    adapter_down_transposed,
    adapter_up_matrix,
    attention_rows,
    upstream,
    rewards,
    prompt_group_index,
    completion_live_lengths,
):
    rolls, model = hidden.shape
    slots = key_value_cache.shape[1]
    width = model // ndp
    rank, _, piece = adapter_down_transposed.shape
    rows, shard = attention_rows.shape
    qkvw = query_key_value_weight.shape[2]
    feats = output_weight_frozen.shape[1]
    chunks = width // CHUNK
    vm = pl.BlockSpec(memory_space=pltpu.VMEM)
    sm = pl.BlockSpec(memory_space=pltpu.SMEM)
    hbm = pl.BlockSpec(memory_space=pltpu.HBM)
    dma = pltpu.SemaphoreType.DMA
    V = pltpu.VMEM
    dec, out, ga, gb = pl.pallas_call(
        lambda *refs: fused_kernel(ndp, ntp, *refs),
        out_shape=(
            pltpu.VMEM((rolls, model), F32),
            pltpu.VMEM((rows, shard), F32),
            pltpu.VMEM((rank, piece), F32),
            pltpu.VMEM((rank, piece), F32),
        ),
        in_specs=[vm, vm, hbm, hbm, sm, hbm, vm, vm, hbm, hbm, sm, sm, sm],
        out_specs=(pl.BlockSpec(memory_space=pl.ANY),) * 4,
        scratch_shapes=[
            V((ndp, rolls, width), BF16),
            V((2, 128), F32),
            V((ndp, rolls, width), BF16),
            V((2, ndp // 2, 2, rank, piece), BF16),
            V((width // piece, rank, piece), BF16),
            V((ndp, 2, 128), F32),
            V((2, 2, ndp // 2, rolls, qkvw + 128), F32),
            V((2, ndp // 2, rolls, qkvw + 128), F32),
            V((2, ndp // 2, rolls, qkvw + 128), F32),
            V((2, ndp // 2, rolls, qkvw + 128), F32),
            V((2, rolls, feats), BF16),
            V((2, 2, ndp // 2, rolls, feats), BF16),
            V((2, ndp * rolls, width + 128), F32),
            V((2, ntp, ndp * rolls, width + 128), F32),
            V((ndp, rolls, width), F32),
            V((ndp, rolls, width), F32),
            V((2, 2, rank, rows // 2), F32),
            V((3, 2, rank, rows // 2), F32),
            V((2, 2, rank, rows // 2), BF16),
            V((2, ndp // 2, 2, rank, piece), F32),
            V((2, ndp // 2, 2, rank, piece), BF16),
            V((ndp // 2, 2, rank, piece), BF16),
            V((ndp // 2, 2, rank, piece), BF16),
            V((ndp // 2, 2, rank, piece), BF16),
            V((rows, shard), BF16),
            V((2, 2, rows, shard), BF16),
            V((2, 2, chunks, feats, CHUNK), BF16),
            V((4, chunks, rows, CHUNK), BF16),
            V((4, chunks, rows, CHUNK), BF16),
            dma((3,)),
            dma((3,)),
            dma((2,)),
            dma((2,)),
            dma,
            dma,
            dma((3,)),
            dma((3,)),
            dma((5,)),
            dma((2, 2, chunks * SEGS)),
            dma,
            dma((chunks - 1 + CHUNK // 128,)),
            dma,
            dma,
            dma,
            dma,
            dma((3,)),
            dma((3,)),
            dma((2,)),
            dma((2,)),
            V((feats, width), BF16),
            V((rows, shard), BF16),
            V((width, qkvw), BF16),
            V((rolls, slots, 2 * HD), BF16),
            V((rows, shard), BF16),
            dma((5,)),
            V((rows, shard), F32),
            V((rolls, model), F32),
            V((rank, piece), F32),
            V((rank, piece), F32),
            dma,
            dma((3,)),
        ]
        + [dma((2,))] * 8,
        compiler_params=pltpu.CompilerParams(
            collective_id=0, has_side_effects=True, vmem_limit_bytes=64815104
        ),
    )(
        hidden,
        attention_norm_gain.reshape(model // 128, 128),
        query_key_value_weight[:, 0, :],
        key_value_cache[:, :, 0, :],
        cache_fill_lengths,
        output_weight_frozen[0],
        adapter_down_transposed[:, 0, :],
        adapter_up_matrix[:, 0, :],
        attention_rows,
        upstream,
        rewards,
        prompt_group_index,
        completion_live_lengths,
    )
    return dec, out, ga[:, None, :], gb[:, None, :]


def shards(
    hidden,
    attention_norm_gain,
    query_key_value_weight,
    key_value_cache,
    cache_fill_lengths,
    output_weight_frozen,
    adapter_down_transposed,
    adapter_up_matrix,
    attention_rows,
    upstream,
    rewards,
    prompt_group_index,
    completion_live_lengths,
):
    a_piece, b_piece = (
        lax.all_gather(adapter_down_transposed, "dp", axis=2, tiled=True),
        lax.all_gather(adapter_up_matrix, "dp", axis=2, tiled=True),
    )
    b_whole = lax.all_gather(b_piece, "tp", axis=1, tiled=True)
    up_matrix_flat = b_whole.reshape(b_whole.shape[0], -1).astype(jnp.float32)
    a_local = a_piece[:, 0, :]
    up_matrix_columns = b_piece[:, 0, :]
    w_rows = query_key_value_weight[:, 0, :].astype(jnp.float32)
    w_cols = output_weight_frozen[0]
    query_width = HEADS_TP * HD
    local_rolls = hidden.shape[0]
    decode_state = hidden.astype(jnp.float32)
    keys_new = []
    values_new = []
    for step in range(2):
        normed = rms_norm(decode_state, attention_norm_gain)
        spread = lax.all_to_all(normed, "dp", split_axis=1, concat_axis=0, tiled=True)
        partial_value = jnp.dot(spread, w_rows, precision=lax.Precision.HIGHEST)
        qkv = lax.psum_scatter(partial_value, "dp", scatter_dimension=0, tiled=True)
        query = qkv[:, :query_width].reshape(local_rolls, HEADS_TP, HD)
        keys_new.append(qkv[:, query_width : query_width + HD])
        values_new.append(qkv[:, query_width + HD :])
        attended = attend(
            query,
            key_value_cache[:, :, 0, :],
            cache_fill_lengths,
            jnp.stack(keys_new, axis=1),
            jnp.stack(values_new, axis=1),
        )
        columns = jnp.dot(
            lax.all_gather(attended, "dp", axis=0, tiled=True),
            w_cols,
            preferred_element_type=jnp.float32,
        )
        returned_values = lax.all_to_all(columns, "dp", split_axis=0, concat_axis=1, tiled=True)
        low_rank_decode = jnp.dot(attended, a_local.T, preferred_element_type=jnp.float32)
        state_update = returned_values + adapter_scale * jnp.dot(
            low_rank_decode, up_matrix_flat, precision=lax.Precision.HIGHEST
        )
        decode_state = decode_state + lax.psum(state_update, "tp")
    groups = local_rolls * lax.axis_size("dp") // GROUP
    onehot = (prompt_group_index[:, None] == jnp.arange(groups, dtype=jnp.int32)[None, :]).astype(
        jnp.float32
    )
    totals, squares = lax.psum(
        (
            jnp.sum(onehot * rewards[:, None], axis=0),
            jnp.sum(onehot * (rewards * rewards)[:, None], axis=0),
        ),
        "dp",
    )
    mean = totals / GROUP
    std = jnp.sqrt(jnp.maximum(squares / GROUP - mean * mean, 0.09))
    advantage = (rewards - jnp.sum(onehot * mean[None, :], axis=1)) / jnp.sum(
        onehot * std[None, :], axis=1
    )
    per_roll = advantage / completion_live_lengths.astype(jnp.float32)
    rows = attention_rows.shape[0]
    slot = jnp.arange(rows, dtype=jnp.int32) % COMP
    limit = jnp.repeat(completion_live_lengths, COMP)
    row_w = jnp.where(slot < limit, jnp.repeat(per_roll, COMP), 0.0)
    whole_rows = jnp.dot(
        attention_rows,
        lax.all_gather(output_weight_frozen, "dp", axis=2, tiled=True)[0],
        preferred_element_type=jnp.float32,
    )
    frozen_output_rows = lax.psum_scatter(whole_rows, "tp", scatter_dimension=1, tiled=True)
    low_sum = lax.psum(jnp.dot(attention_rows, a_local.T, preferred_element_type=jnp.float32), "tp")
    low_rank_rows = low_sum.astype(jnp.bfloat16)
    adapted_output_rows = frozen_output_rows + adapter_scale * jnp.dot(
        low_rank_rows, up_matrix_columns, preferred_element_type=jnp.float32
    )
    advantage_weighted = (row_w[:, None] * upstream.astype(jnp.float32)).astype(jnp.bfloat16)
    backward_result = lax.psum(
        jnp.dot(advantage_weighted, up_matrix_columns.T, preferred_element_type=jnp.float32), "tp"
    ).astype(jnp.bfloat16)
    down_gradient = adapter_scale * lax.dot_general(
        backward_result,
        attention_rows,
        (((0,), (0,)), ((), ())),
        preferred_element_type=jnp.float32,
    )
    up_gradient = adapter_scale * lax.dot_general(
        low_rank_rows,
        advantage_weighted,
        (((0,), (0,)), ((), ())),
        preferred_element_type=jnp.float32,
    )
    grad_a_part, grad_b_part = (
        lax.psum_scatter(down_gradient[:, None, :], "dp", scatter_dimension=2, tiled=True),
        lax.psum_scatter(up_gradient[:, None, :], "dp", scatter_dimension=2, tiled=True),
    )
    return (decode_state, adapted_output_rows, grad_a_part, grad_b_part)


def solution(mesh):
    placed = (
        P("dp", None),
        P(),
        P("dp", "tp", None),
        P("dp", None, "tp", None),
        P("dp"),
        P("tp", None, "dp"),
        P(None, "tp", "dp"),
        P(None, "tp", "dp"),
        P("dp", "tp"),
        P("dp", "tp"),
        P("dp"),
        P("dp"),
        P("dp"),
    )
    ndp, ntp = mesh.shape["dp"], mesh.shape["tp"]

    def body(*args):
        width = args[5].shape[2]
        piece = args[6].shape[2]
        if ntp == 4 and ndp == 8 and piece % 128 == 0 and width % CHUNK == 0:
            return fused_shards(ndp, ntp, *args)
        return shards(*args)

    return jax.shard_map(
        body,
        mesh=mesh,
        in_specs=placed,
        out_specs=(P("dp", None), P("dp", "tp"), P(None, "tp", "dp"), P(None, "tp", "dp")),
        check_vma=False,
    )
```

```python
import math

import jax
import jax.numpy as jnp
from jax import lax
from jax.experimental import pallas as pl
from jax.experimental.pallas import tpu as pltpu
from jax.sharding import PartitionSpec as P

HD = 128
HEADS_TP = 8
GROUP = 4
COMP = 256


adapter_scale = 2.0


def rms_norm(decode_state, gain):
    scale = lax.rsqrt(jnp.mean(decode_state * decode_state, axis=-1, keepdims=True) + 1e-05)
    return decode_state * scale * gain.astype(jnp.float32)


def attend(query, cache, lengths, new_keys, new_values):
    head = query.shape[-1]
    slots = cache.shape[1]
    factor = 1.0 / math.sqrt(head)
    keys = cache[:, :, :head].astype(jnp.float32)
    values = cache[:, :, head:]
    scores = jnp.einsum("bhd,bcd->bhc", query, keys, precision=lax.Precision.HIGHEST) * factor
    valid = jnp.arange(slots, dtype=jnp.int32)[None, None, :] < lengths[:, None, None]
    scores = jnp.where(valid, scores, -1e30)
    extra = jnp.einsum("bhd,bed->bhe", query, new_keys, precision=lax.Precision.HIGHEST) * factor
    joined = jnp.concatenate([scores, extra], axis=-1)
    top = jnp.max(joined, axis=-1, keepdims=True)
    expo = jnp.exp(joined - top)
    probs = (expo / jnp.sum(expo, axis=-1, keepdims=True)).astype(jnp.bfloat16)
    out = jnp.einsum("bhc,bcd->bhd", probs[..., :slots], values, preferred_element_type=jnp.float32)
    out = out + jnp.einsum(
        "bhe,bed->bhd",
        probs[..., slots:].astype(jnp.float32),
        new_values,
        precision=lax.Precision.HIGHEST,
    )
    return out.astype(jnp.bfloat16).reshape(query.shape[0], -1)


MESH = pl.DeviceIdType.MESH
F32 = jnp.float32
BF16 = jnp.bfloat16
NT = (((1,), (1,)), ((), ()))
TN = (((0,), (0,)), ((), ()))
CHUNK = 256
SEGS = 4
ROW_PARTS = 8


def split3(v):
    hi = v.astype(BF16)
    rest = v - hi.astype(F32)
    mid = rest.astype(BF16)
    lo = (rest - mid.astype(F32)).astype(BF16)
    return jnp.concatenate([hi, mid, lo], axis=0)


def exact_dot(v, w, dims=(((1,), (0,)), ((), ()))):
    n = v.shape[0]
    r = lax.dot_general(split3(v), w, dims, preferred_element_type=F32)
    return r[:n] + r[n : 2 * n] + r[2 * n :]


def rows_of(ref, n):
    return jnp.concatenate([ref[i] for i in range(n)], axis=0)


def lanes_of(ref, n):
    return jnp.concatenate([ref[i] for i in range(n)], axis=1)


def fused_kernel(
    ndp,
    ntp,
    h_ref,
    gain_ref,
    wqkv_in,
    cache_in,
    lens_ref,
    wo_in,
    a_ref,
    b_ref,
    x_in,
    up_in,
    rew_ref,
    idx_ref,
    live_ref,
    dec_out,
    rows_out,
    ga_out,
    gb_out,
    hsend,
    stats_ref,
    hbuf,
    abuf,
    bdbuf,
    statbuf,
    qsend,
    qside,
    qline,
    qrecv,
    asend,
    arecv,
    usend,
    urecv,
    fsend,
    frecv,
    lbsend,
    lbhalf,
    lbfull,
    gown,
    gsend,
    grecv,
    gzsend,
    gzrecv,
    wt_ref,
    xbuf,
    wbuf,
    pbuf,
    prcv,
    ds_s,
    ds_r,
    ts_s,
    ts_r,
    bd_s,
    bd_r,
    xs_s,
    xs_r,
    wl_s,
    wl_r,
    ps_s,
    ps_r,
    gy_s,
    gy_r,
    gz_s,
    gz_r,
    lb_s,
    lb_r,
    ab_s,
    ab_r,
    wo_ref,
    x_ref,
    wqkv_ref,
    cache_ref,
    up_ref,
    in_s,
    out_ref,
    dec_ref,
    ga_ref,
    gb_ref,
    out_s,
    fin_s,
    acc,
    qy_s,
    qy_r,
    qz_s,
    qz_r,
    ay_s,
    ay_r,
    az_s,
    az_r,
):
    d = lax.axis_index("dp")
    t = lax.axis_index("tp")
    z, y = d // 2, d % 2
    x, c = t // 2, t % 2
    nz = ndp // 2
    rolls, model = h_ref.shape
    width = model // ndp
    rank = a_ref.shape[0]
    piece = a_ref.shape[1]
    chunks = wo_ref.shape[1] // CHUNK
    qkvw = wqkv_ref.shape[1]
    rows = x_ref.shape[0]
    mate = 2 * x + (1 - c)
    other_y = 2 * z + (1 - y)

    def fetch(k):
        src, dst = (
            (wo_in, wo_ref),
            (x_in, x_ref),
            (wqkv_in, wqkv_ref),
            (cache_in, cache_ref),
            (up_in, up_ref),
        )[k]
        return pltpu.make_async_copy(src, dst, in_s.at[k])

    for k in range(5):
        fetch(k).start()
    barrier = pltpu.get_barrier_semaphore()
    for i in range(ndp):
        for j in range(ntp):
            if i or j:
                pl.semaphore_signal(
                    barrier,
                    inc=1,
                    device_id=((d + i) % ndp, (t + j) % ntp),
                    device_id_type=MESH,
                )
    pl.semaphore_wait(barrier, ndp * ntp - 1)

    sent = []

    def send(src, dst, s, r, dev):
        cp = pltpu.make_async_remote_copy(
            src_ref=src, dst_ref=dst, send_sem=s, recv_sem=r, device_id=dev, device_id_type=MESH
        )
        return cp

    def dp_start(e, src, dst):
        for off in range(1, ndp):
            peer = (d + off) % ndp
            send(src(peer), dst.at[d], ds_s.at[e], ds_r.at[e], (peer, t)).start()
        whole = dst.at[pl.ds(0, ndp - 1)]
        sent.append(send(whole, whole, ds_s.at[e], ds_r.at[e], (d, (t + 1) % ntp)))

    def dp_wait(e, dst):
        whole = dst.at[pl.ds(0, ndp - 1)]
        send(whole, whole, ds_s.at[e], ds_r.at[e], (d, (t + 1) % ntp)).wait_recv()

    def tp_start(e, src, dst):
        for off in range(1, ntp):
            peer = (t + off) % ntp
            send(src, dst.at[t], ts_s.at[e], ts_r.at[e], (d, peer)).start()
        whole = dst.at[pl.ds(0, ntp - 1)]
        sent.append(send(whole, whole, ts_s.at[e], ts_r.at[e], (d, (t + 1) % ntp)))

    def tp_wait(e, dst):
        whole = dst.at[pl.ds(0, ntp - 1)]
        send(whole, whole, ts_s.at[e], ts_r.at[e], (d, (t + 1) % ntp)).wait_recv()

    for i in range(ndp):
        hsend[i] = h_ref[:, i * width : (i + 1) * width]
    lane = lax.broadcasted_iota(jnp.int32, (1, 128), 1)
    ones = [jnp.where(lane == idx_ref[r], 1.0, 0.0) for r in range(rolls)]
    stats_ref[...] = jnp.zeros_like(stats_ref)
    for r in range(rolls):
        stats_ref[0:1] += ones[r] * rew_ref[r]
        stats_ref[1:2] += ones[r] * (rew_ref[r] * rew_ref[r])

    dp_start(0, lambda p: hsend.at[p], hbuf)
    hbuf[d] = hsend[d]
    abuf[y, z, 0] = a_ref[...]
    abuf[y, z, 1] = b_ref[...]
    for k, ref in enumerate((a_ref, b_ref)):
        for off in range(1, nz):
            peer = 2 * ((z + off) % nz) + y
            send(ref, abuf.at[y, z, k], ab_s.at[0], ab_r.at[0], (peer, t)).start()
    others = abuf.at[0, pl.ds(0, nz - 1)]
    sent.append(send(others, others, ab_s.at[0], ab_r.at[0], (other_y, t)))
    dp_start(1, lambda p: stats_ref, statbuf)
    statbuf[d] = stats_ref[...]
    per = width // piece
    half = ndp // per
    src_t = d // half

    def up_block(tj):
        return send(bdbuf, bdbuf, bd_s, bd_r, (d, tj))

    fetch(0).wait()
    fetch(1).wait()
    xcp = send(x_ref, xbuf.at[y, c], xs_s.at[0], xs_r.at[0], (d, mate))
    xcp.start()
    sent.append(xcp)
    xbuf[y, c] = x_ref[...]

    def row_send(k):
        part = rows // ROW_PARTS
        if k >= ROW_PARTS:
            return
        seg = pl.ds(k * part, part)
        send(
            x_ref.at[seg], xbuf.at[y, c, seg], xs_s.at[1], xs_r.at[1], (other_y, t)
        ).start()

    def rows_whole():
        return send(x_ref, xbuf.at[1 - y, c], xs_s.at[1], xs_r.at[1], (other_y, t))

    def relay(dst_core):
        return send(
            xbuf.at[1 - y, c], xbuf.at[1 - y, dst_core], xs_s.at[2], xs_r.at[2], (d, mate)
        )

    feats = wo_ref.shape[0]
    pieces = chunks * SEGS
    near, far = z // 2, 1 - z // 2
    end = jnp.logical_or(z == 0, z == nz - 1)
    role_m = jnp.logical_and(jnp.logical_not(end), c == z // 2)
    role_2 = jnp.logical_and(jnp.logical_not(end), c != z // 2)
    lead = jnp.where(c == near, far, near)
    trail = 1 - lead
    z_up, z_dn = jnp.minimum(z + 1, nz - 1), jnp.maximum(z - 1, 0)
    z_in = jnp.where(z < 2, z_up, z_dn)
    z_out = jnp.where(z < 2, z_dn, z_up)

    cuts = [(ch, 0, CHUNK) for ch in range(chunks - 1)]
    cuts += [(chunks - 1, h * 128, 128) for h in range(CHUNK // 128)]

    def seg_of(k):
        ch, part = k // SEGS, k % SEGS
        if ch < chunks - 1:
            size = feats // SEGS
            return ch, pl.ds(part * size, size), 0, CHUNK
        halves = CHUNK // 128
        size = feats * halves // SEGS
        per_half = SEGS // halves
        return ch, pl.ds((part % per_half) * size, size), (part // per_half) * 128, 128

    def own(k, which, zt):
        ch, seg, off, num = seg_of(k)
        return send(
            wo_ref.at[seg, pl.ds(ch * CHUNK + off, num)],
            wbuf.at[z // 2, c, ch, seg, pl.ds(off, num)],
            wl_s.at[which],
            wl_r.at[z // 2, c, k],
            (2 * zt + y, 2 * x + z % 2),
        )

    def hop(blk, j, which, zt):
        k, cc = j // 2, j % 2
        ch, seg, off, num = seg_of(k)
        ref = wbuf.at[blk, cc, ch, seg, pl.ds(off, num)]
        return send(ref, ref, wl_s.at[which], wl_r.at[blk, cc, k], (2 * zt + y, t))

    def own_tick(k):
        @pl.when(z < nz - 1)
        def _():
            own(k, 0, z_up).start()

        @pl.when(z > 0)
        def _():
            own(k, 1, z_dn).start()

        @pl.when(z % 2 != c)
        def _():
            own(k, 2, z).start()

    waited = {"near": 0, "far_m": 0, "far_2": 0}

    def arrive(name, blk, upto):
        for j in range(waited[name], upto):
            hop(blk, j, 3, z_in).wait_recv()
        waited[name] = max(waited[name], upto)

    def relay_tick(name, blk, lo, hi, which, zt):
        hi = min(hi, 2 * pieces)
        arrive(name, blk, hi)
        for j in range(lo, hi):
            hop(blk, j, which, zt).start()

    clock = [0]
    ticks = 3 * pieces

    def tick():
        n = clock[0]
        if n >= ticks:
            return
        clock[0] += 1
        if n < pieces:
            own_tick(n)
            row_send(n)
            return
        m = n - pieces

        @pl.when(role_m)
        def _():
            if m < pieces:
                relay_tick("near", near, 2 * m, 2 * m + 2, 3, z_in)
                relay_tick("far_m", far, 2 * m, 2 * m + 2, 4, z_out)

        if m >= pieces:

            @pl.when(role_2)
            def _():
                relay_tick("far_2", far, 2 * (m - pieces), 2 * (m - pieces) + 2, 4, z_out)

    def pump(n):
        for _ in range(n):
            tick()

    pump(2)

    @pl.when(z % 2 == c)
    def _():
        for ch in range(chunks):
            wbuf[z // 2, c, ch] = wo_ref[:, ch * CHUNK : (ch + 1) * CHUNK]

    def q_side(step):
        return send(qsend.at[step, 1 - y], qside.at[step], qy_s.at[step], qy_r.at[step], (other_y, t))

    def q_lines(step):
        whole = qrecv.at[step, pl.ds(0, nz - 1)]
        return send(whole, whole, qz_s.at[step], qz_r.at[step], (other_y, t))

    def a_side(step, yy):
        ref = arecv.at[step, yy]
        return send(ref, ref, ay_s.at[step], ay_r.at[step], (other_y, t))

    def a_lines(step):
        whole = arecv.at[step, 0, pl.ds(0, nz - 1)]
        return send(whole, whole, az_s.at[step], az_r.at[step], (other_y, t))

    def ab_side(yy):
        return send(abuf.at[yy], abuf.at[yy], ab_s.at[1], ab_r.at[1], (other_y, t))

    def lb_core():
        return send(lbsend.at[1 - c], lbhalf.at[2], lb_s.at[0], lb_r.at[0], (d, mate))

    def lb_chip():
        return send(lbhalf.at[0], lbhalf.at[1], lb_s.at[1], lb_r.at[1], (d, 2 * (1 - x) + c))

    def lb_back(core):
        return send(lbfull.at[core], lbfull.at[core], lb_s.at[2], lb_r.at[2], (d, mate))

    def g_side():
        return send(gsend.at[1 - y], grecv, gy_s, gy_r, (other_y, t))

    def g_line(off):
        zt = (z + off) % nz
        return send(gzsend.at[zt], gzrecv.at[z], gz_s, gz_r, (2 * zt + y, t))

    def g_lines():
        whole = gzrecv.at[pl.ds(0, nz - 1)]
        return send(whole, whole, gz_s, gz_r, (other_y, t))

    def share(dx, dy, u):
        zz = jnp.where(dx == 1, 1 - x, x)
        yy = jnp.where(dy == 1, 1 - y, y)
        ch, off, num = cuts[u]
        cols = pl.ds(off, num)
        return send(
            pbuf.at[2 * dx + dy, ch, :, cols],
            prcv.at[2 * dx + dy, ch, :, cols],
            ps_s,
            ps_r.at[u],
            (2 * z + yy, 2 * zz + c),
        )

    def rows_in():
        rows_whole().wait_recv()
        relay(c).start()

    def rows_ready():
        send(x_ref, xbuf.at[y, 1 - c], xs_s.at[0], xs_r.at[0], (d, mate)).wait_recv()
        relay(1 - c).wait_recv()

    def columns(yy, u):
        ch, off, num = cuts[u]
        return pl.ds(pl.multiple_of((yy * chunks + ch) * CHUNK + off, 128), num)

    def final(k):
        src, dst = ((dec_ref, dec_out), (ga_ref, ga_out), (gb_ref, gb_out))[k]
        return pltpu.make_async_copy(src, dst, fin_s.at[k])

    def emit(dy, u):
        cols = columns((y + dy) % 2, u)
        return pltpu.make_async_copy(out_ref.at[:, cols], rows_out.at[:, cols], out_s)

    def unit(blk, u):
        ch, off, num = cuts[u]
        cols = pl.ds(off, num)
        own_ks = [k for k in range(pieces) if seg_of(k)[0] == ch and seg_of(k)[2] == off]
        upto = 2 * (max(own_ks) + 1)
        leads = blk is lead

        @pl.when(role_m)
        def _():
            arrive("far_m" if leads else "near", blk, upto)

        if not leads:

            @pl.when(role_2)
            def _():
                arrive("far_2", blk, upto)

        others = jnp.logical_not(role_m) if leads else end
        parts = [(k, cc) for k in own_ks for cc in range(2)]

        def landed(todo):
            for cc in range(2):
                mine = jnp.logical_and(c + 2 * blk == z, c == cc)
                ks = [k for k, core in todo if core == cc]

                if ks:

                    @pl.when(jnp.logical_and(others, jnp.logical_not(mine)))
                    def _():
                        for k in ks:
                            hop(blk, 2 * k + cc, 3, z_in).wait_recv()

        dx = jnp.where(blk == x, 0, 1)

        def put(dy, p):
            if dy == 1:
                pbuf[2 * dx + 1, ch, :, cols] = p.astype(BF16)
                share(dx, 1, u).start()
            else:

                @pl.when(dx == 1)
                def _():
                    pbuf[2, ch, :, cols] = p.astype(BF16)
                    share(1, 0, u).start()

                @pl.when(dx == 0)
                def _():
                    out_ref[:, columns(y, u)] += p

        if leads or u < len(cuts) - 1:
            landed(parts)
            for dy in (1, 0):
                yy = (y + dy) % 2
                p = jnp.dot(xbuf[yy, 0], wbuf[blk, 0, ch, :, cols], preferred_element_type=F32)
                p = p + jnp.dot(xbuf[yy, 1], wbuf[blk, 1, ch, :, cols], preferred_element_type=F32)
                put(dy, p)
            return
        for i, (k, cc) in enumerate(parts):
            landed([(k, cc)])
            seg = seg_of(k)[1]
            for dy in (1, 0):
                yy = (y + dy) % 2
                p = jnp.dot(
                    xbuf[yy, cc, :, seg], wbuf[blk, cc, ch, seg, cols], preferred_element_type=F32
                )
                if i:
                    p = p + acc[dy]
                if i < len(parts) - 1:
                    acc[dy] = p
                else:
                    put(dy, p)

    dp_wait(0, hbuf)
    state = jnp.concatenate([hbuf[i].astype(F32) for i in range(ndp)], axis=0)
    gains = gain_ref[...].astype(F32)
    line = lax.broadcasted_iota(jnp.int32, gains.shape, 0)
    gain = jnp.concatenate(
        [
            jnp.sum(jnp.where(line == d * (width // 128) + i, gains, 0.0), axis=0, keepdims=True)
            for i in range(width // 128)
        ],
        axis=1,
    )
    fetch(2).wait()
    new_k, new_v = [], []
    factor = 1.0 / math.sqrt(HD)

    for step in range(2):
        squares = jnp.sum(state * state, axis=-1, keepdims=True)
        part = exact_dot(state * gain, wqkv_ref[...])
        both = jnp.concatenate([part, jnp.broadcast_to(squares, (ndp * rolls, 128))], axis=1)
        for i in range(ndp):
            qsend[step, i % 2, i // 2] = both[i * rolls : (i + 1) * rolls]
        q_side(step).start()
        pump(1)
        if step == 1:
            lb_chip().wait_recv()
            lbfull[c] = (lbhalf[0] + lbhalf[1]).astype(BF16)
            lb_back(c).start()
        if step == 0:
            send(others, others, ab_s.at[0], ab_r.at[0], (other_y, t)).wait_recv()
            ab_side(y).start()
            dp_wait(1, statbuf)
            tot = statbuf[0]
            for i in range(1, ndp):
                tot = tot + statbuf[i]
            mean = tot[0:1] / GROUP
            std = jnp.sqrt(jnp.maximum(tot[1:2] / GROUP - mean * mean, 0.09))
            fetch(4).wait()
            for r in range(rolls):
                one, rew = ones[r], rew_ref[r]
                live = live_ref[r].astype(F32)
                adv = (rew - jnp.sum(one * mean, axis=1, keepdims=True)) / jnp.sum(
                    one * std, axis=1, keepdims=True
                )
                slot = lax.broadcasted_iota(jnp.int32, (COMP, 1), 0).astype(F32)
                row_w = jnp.where(slot < live, adv / live, 0.0)
                seg = pl.ds(r * COMP, COMP)
                wt_ref[seg, :] = (row_w * up_ref[seg, :].astype(F32)).astype(BF16)
        q_side(step).wait_recv()
        for i in range(nz):
            qline[step, i] = qsend[step, y, i] + qside[step, i]
        for off in range(1, nz):
            zt = (z + off) % nz
            src, dst = qline.at[step, zt], qrecv.at[step, z]
            send(src, dst, qz_s.at[step], qz_r.at[step], (2 * zt + y, t)).start()
        pump(2)
        q_lines(step).wait_recv()
        total = qline[step, z]
        for off in range(1, nz):
            total = total + qrecv[step, (z + off) % nz]
        qkv = total[:, :qkvw] * lax.rsqrt(total[:, qkvw : qkvw + 1] / model + 1e-05)
        new_k.append(qkv[:, HEADS_TP * HD : HEADS_TP * HD + HD])
        new_v.append(qkv[:, HEADS_TP * HD + HD :])
        if step == 0:
            fetch(3).wait()
        heads = []
        for b in range(rolls):
            q = jnp.concatenate(
                [qkv[b : b + 1, h * HD : (h + 1) * HD] for h in range(HEADS_TP)], axis=0
            )
            scores = exact_dot(q, cache_ref[b, :, :HD], NT) * factor
            pos = lax.broadcasted_iota(jnp.int32, scores.shape, 1)
            scores = jnp.where(pos < lens_ref[b], scores, -1e30)
            extra = [
                jnp.sum(q * k[b : b + 1], axis=-1, keepdims=True) * factor for k in new_k
            ]
            top = jnp.max(scores, axis=-1, keepdims=True)
            for e in extra:
                top = jnp.maximum(top, e)
            expo = jnp.exp(scores - top)
            ee = [jnp.exp(e - top) for e in extra]
            den = jnp.sum(expo, axis=-1, keepdims=True)
            for e in ee:
                den = den + e
            att = jnp.dot(
                (expo / den).astype(BF16), cache_ref[b, :, HD:], preferred_element_type=F32
            )
            for e, v in zip(ee, new_v):
                att = att + (e / den).astype(BF16).astype(F32) * v[b : b + 1]
            heads.append(jnp.concatenate([att[h : h + 1] for h in range(HEADS_TP)], axis=1))
        asend[step] = jnp.concatenate(heads, axis=0).astype(BF16)
        for off in range(1, nz):
            zt = (z + off) % nz
            send(
                asend.at[step], arecv.at[step, y, z], az_s.at[step], az_r.at[step], (2 * zt + y, t)
            ).start()
        pump(1)
        arecv[step, y, z] = asend[step]
        if step == 0:
            ab_side(1 - y).wait_recv()
            at, bt = (
                jnp.concatenate([abuf[i % 2, i // 2, k] for i in range(ndp)], axis=1)
                for k in range(2)
            )

            @pl.when(t == src_t)
            def _():
                for j in range(per):
                    bdbuf[j] = abuf[j % 2, (d % half) * (per // 2) + j // 2, 1]
                for off in range(1, ntp):
                    up_block((t + off) % ntp).start()

            for k, (m, v) in enumerate(((at, x_ref), (bt, wt_ref))):
                lb = lax.dot_general(m, v[...], NT, preferred_element_type=F32)
                for i in range(2):
                    lbsend[i, k] = lb[:, i * (rows // 2) : (i + 1) * (rows // 2)]
            lb_core().start()
        else:
            lb_back(c).wait_send()
            lb_back(1 - c).wait_recv()
            low_t, back_t = lanes_of(lbfull.at[:, 0], 2), lanes_of(lbfull.at[:, 1], 2)
            ga = adapter_scale * jnp.dot(back_t, x_ref[...], preferred_element_type=F32)
            gb = adapter_scale * jnp.dot(low_t, wt_ref[...], preferred_element_type=F32)
            for i in range(ndp):
                for k, g in enumerate((ga, gb)):
                    part = g[:, i * piece : (i + 1) * piece]
                    gown[i % 2, i // 2, k] = part
                    gsend[i % 2, i // 2, k] = part.astype(BF16)
            g_side().start()
            out_ref[...] = adapter_scale * lax.dot_general(
                low_t, bt, TN, preferred_element_type=F32
            )
        a_lines(step).wait_recv()
        a_side(step, y).start()
        pump(1)
        a_side(step, 1 - y).wait_recv()
        attended = jnp.concatenate(
            [arecv[step, i % 2, i // 2].astype(F32) for i in range(ndp)], axis=0
        ).astype(BF16)
        usend[step, :, :width] = jnp.dot(attended, wo_ref[...], preferred_element_type=F32)
        usend[step, :, width:] = jnp.concatenate(
            [
                lax.dot_general(attended, at, NT, preferred_element_type=F32),
                jnp.zeros((ndp * rolls, 128 - rank), F32),
            ],
            axis=1,
        )
        tp_start(step, usend.at[step], urecv.at[step])
        pump(2)
        urecv[step, t] = usend[step]
        if step == 0:
            lb_core().wait_recv()
            lbhalf[0] = lbsend[c] + lbhalf[2]
            lb_chip().start()

            @pl.when(t != src_t)
            def _():
                up_block(src_t).wait_recv()

            bd = lanes_of(bdbuf, per)
        tp_wait(step, urecv.at[step])
        upd = urecv[step, 0]
        for i in range(1, ntp):
            upd = upd + urecv[step, i]
        state = state + (
            upd[:, :width] + adapter_scale * exact_dot(upd[:, width : width + rank], bd)
        )

    for i in range(ndp):
        fsend[i] = state[i * rolls : (i + 1) * rolls]
    dp_start(2, lambda p: fsend.at[p], frecv)
    frecv[d] = fsend[d]
    rows_in()
    g_side().wait_recv()
    for i in range(nz):
        gzsend[i] = (gown[y, i] + grecv[i].astype(F32)).astype(BF16)
    pump(2)
    rows_ready()
    for u in range(len(cuts)):
        unit(lead, u)
        pump(2)
    dp_wait(2, frecv)
    for i in range(ndp):
        dec_ref[:, i * width : (i + 1) * width] = frecv[i]
    final(0).start()
    for cp in sent:
        cp.wait_send()
    while clock[0] < 2 * pieces + pieces // 2:
        pump(1)
    unit(trail, 0)
    pump(ticks)
    unit(trail, 1)
    for off in range(1, nz):
        g_line(off).start()
    for u in range(2, len(cuts)):
        unit(trail, u)
    for u in range(len(cuts)):
        ch, off, num = cuts[u]
        three = prcv.at[pl.ds(1, 3), ch, :, pl.ds(off, num)]
        send(three, three, ps_s, ps_r.at[u], (d, mate)).wait_recv()
        for dx, dy in ((1, 0), (0, 1), (1, 1)):
            got = prcv[2 * dx + dy, ch, :, pl.ds(off, num)].astype(F32)
            out_ref[:, columns((y + dy) % 2, u)] += got
        for dy in range(2):
            emit(dy, u).start()

    g = gown[y, z] + grecv[z].astype(F32)
    g_lines().wait_recv()
    for off in range(1, nz):
        g = g + gzrecv[(z + nz - off) % nz].astype(F32)
    ga_ref[...] = g[0]
    gb_ref[...] = g[1]
    final(1).start()
    final(2).start()
    pltpu.make_async_copy(out_ref, rows_out, out_s).wait()
    for k in range(3):
        final(k).wait()

    def drain(which, full):
        send(full, full, wl_s.at[which], wl_r.at[0, 0, 0], (d, mate)).wait_send()

    @pl.when(z < nz - 1)
    def _():
        drain(0, wbuf.at[0, 0])

    @pl.when(z > 0)
    def _():
        drain(1, wbuf.at[0, 0])

    @pl.when(z % 2 != c)
    def _():
        drain(2, wbuf.at[0, 0])

    @pl.when(role_m)
    def _():
        drain(3, wbuf.at[0])

    @pl.when(jnp.logical_not(end))
    def _():
        drain(4, wbuf.at[0])

    three = pbuf.at[pl.ds(1, 3)]
    send(three, three, ps_s, ps_r.at[0], (d, mate)).wait_send()
    rows_whole().wait_send()
    relay(c).wait_send()
    g_side().wait_send()
    for step in range(2):
        q_side(step).wait_send()
        q_lines(step).wait_send()
        a_side(step, y).wait_send()
        a_lines(step).wait_send()
    lb_core().wait_send()
    lb_chip().wait_send()
    ab_side(y).wait_send()
    g_lines().wait_send()

    @pl.when(t == src_t)
    def _():
        copies = wo_ref.at[pl.ds(0, (ntp - 1) * rank)]
        send(copies, copies, bd_s, bd_r, (d, mate)).wait_send()


def fused_shards(
    ndp,
    ntp,
    hidden,
    attention_norm_gain,
    query_key_value_weight,
    key_value_cache,
    cache_fill_lengths,
    output_weight_frozen,
    adapter_down_transposed,
    adapter_up_matrix,
    attention_rows,
    upstream,
    rewards,
    prompt_group_index,
    completion_live_lengths,
):
    rolls, model = hidden.shape
    slots = key_value_cache.shape[1]
    width = model // ndp
    rank, _, piece = adapter_down_transposed.shape
    rows, shard = attention_rows.shape
    qkvw = query_key_value_weight.shape[2]
    feats = output_weight_frozen.shape[1]
    chunks = width // CHUNK
    vm = pl.BlockSpec(memory_space=pltpu.VMEM)
    sm = pl.BlockSpec(memory_space=pltpu.SMEM)
    hbm = pl.BlockSpec(memory_space=pltpu.HBM)
    dma = pltpu.SemaphoreType.DMA
    V = pltpu.VMEM
    dec, out, ga, gb = pl.pallas_call(
        lambda *refs: fused_kernel(ndp, ntp, *refs),
        out_shape=(
            pltpu.VMEM((rolls, model), F32),
            pltpu.VMEM((rows, shard), F32),
            pltpu.VMEM((rank, piece), F32),
            pltpu.VMEM((rank, piece), F32),
        ),
        in_specs=[vm, vm, hbm, hbm, sm, hbm, vm, vm, hbm, hbm, sm, sm, sm],
        out_specs=(pl.BlockSpec(memory_space=pl.ANY),) * 4,
        scratch_shapes=[
            V((ndp, rolls, width), BF16),
            V((2, 128), F32),
            V((ndp, rolls, width), BF16),
            V((2, ndp // 2, 2, rank, piece), BF16),
            V((width // piece, rank, piece), BF16),
            V((ndp, 2, 128), F32),
            V((2, 2, ndp // 2, rolls, qkvw + 128), F32),
            V((2, ndp // 2, rolls, qkvw + 128), F32),
            V((2, ndp // 2, rolls, qkvw + 128), F32),
            V((2, ndp // 2, rolls, qkvw + 128), F32),
            V((2, rolls, feats), BF16),
            V((2, 2, ndp // 2, rolls, feats), BF16),
            V((2, ndp * rolls, width + 128), F32),
            V((2, ntp, ndp * rolls, width + 128), F32),
            V((ndp, rolls, width), F32),
            V((ndp, rolls, width), F32),
            V((2, 2, rank, rows // 2), F32),
            V((3, 2, rank, rows // 2), F32),
            V((2, 2, rank, rows // 2), BF16),
            V((2, ndp // 2, 2, rank, piece), F32),
            V((2, ndp // 2, 2, rank, piece), BF16),
            V((ndp // 2, 2, rank, piece), BF16),
            V((ndp // 2, 2, rank, piece), BF16),
            V((ndp // 2, 2, rank, piece), BF16),
            V((rows, shard), BF16),
            V((2, 2, rows, shard), BF16),
            V((2, 2, chunks, feats, CHUNK), BF16),
            V((4, chunks, rows, CHUNK), BF16),
            V((4, chunks, rows, CHUNK), BF16),
            dma((3,)),
            dma((3,)),
            dma((2,)),
            dma((2,)),
            dma,
            dma,
            dma((3,)),
            dma((3,)),
            dma((5,)),
            dma((2, 2, chunks * SEGS)),
            dma,
            dma((chunks - 1 + CHUNK // 128,)),
            dma,
            dma,
            dma,
            dma,
            dma((3,)),
            dma((3,)),
            dma((2,)),
            dma((2,)),
            V((feats, width), BF16),
            V((rows, shard), BF16),
            V((width, qkvw), BF16),
            V((rolls, slots, 2 * HD), BF16),
            V((rows, shard), BF16),
            dma((5,)),
            V((rows, shard), F32),
            V((rolls, model), F32),
            V((rank, piece), F32),
            V((rank, piece), F32),
            dma,
            dma((3,)),
            V((2, rows, 128), F32),
        ]
        + [dma((2,))] * 8,
        compiler_params=pltpu.CompilerParams(
            collective_id=0, has_side_effects=True, vmem_limit_bytes=64815104
        ),
    )(
        hidden,
        attention_norm_gain.reshape(model // 128, 128),
        query_key_value_weight[:, 0, :],
        key_value_cache[:, :, 0, :],
        cache_fill_lengths,
        output_weight_frozen[0],
        adapter_down_transposed[:, 0, :],
        adapter_up_matrix[:, 0, :],
        attention_rows,
        upstream,
        rewards,
        prompt_group_index,
        completion_live_lengths,
    )
    return dec, out, ga[:, None, :], gb[:, None, :]


def shards(
    hidden,
    attention_norm_gain,
    query_key_value_weight,
    key_value_cache,
    cache_fill_lengths,
    output_weight_frozen,
    adapter_down_transposed,
    adapter_up_matrix,
    attention_rows,
    upstream,
    rewards,
    prompt_group_index,
    completion_live_lengths,
):
    a_piece, b_piece = (
        lax.all_gather(adapter_down_transposed, "dp", axis=2, tiled=True),
        lax.all_gather(adapter_up_matrix, "dp", axis=2, tiled=True),
    )
    b_whole = lax.all_gather(b_piece, "tp", axis=1, tiled=True)
    up_matrix_flat = b_whole.reshape(b_whole.shape[0], -1).astype(jnp.float32)
    a_local = a_piece[:, 0, :]
    up_matrix_columns = b_piece[:, 0, :]
    w_rows = query_key_value_weight[:, 0, :].astype(jnp.float32)
    w_cols = output_weight_frozen[0]
    query_width = HEADS_TP * HD
    local_rolls = hidden.shape[0]
    decode_state = hidden.astype(jnp.float32)
    keys_new = []
    values_new = []
    for step in range(2):
        normed = rms_norm(decode_state, attention_norm_gain)
        spread = lax.all_to_all(normed, "dp", split_axis=1, concat_axis=0, tiled=True)
        partial_value = jnp.dot(spread, w_rows, precision=lax.Precision.HIGHEST)
        qkv = lax.psum_scatter(partial_value, "dp", scatter_dimension=0, tiled=True)
        query = qkv[:, :query_width].reshape(local_rolls, HEADS_TP, HD)
        keys_new.append(qkv[:, query_width : query_width + HD])
        values_new.append(qkv[:, query_width + HD :])
        attended = attend(
            query,
            key_value_cache[:, :, 0, :],
            cache_fill_lengths,
            jnp.stack(keys_new, axis=1),
            jnp.stack(values_new, axis=1),
        )
        columns = jnp.dot(
            lax.all_gather(attended, "dp", axis=0, tiled=True),
            w_cols,
            preferred_element_type=jnp.float32,
        )
        returned_values = lax.all_to_all(columns, "dp", split_axis=0, concat_axis=1, tiled=True)
        low_rank_decode = jnp.dot(attended, a_local.T, preferred_element_type=jnp.float32)
        state_update = returned_values + adapter_scale * jnp.dot(
            low_rank_decode, up_matrix_flat, precision=lax.Precision.HIGHEST
        )
        decode_state = decode_state + lax.psum(state_update, "tp")
    groups = local_rolls * lax.axis_size("dp") // GROUP
    onehot = (prompt_group_index[:, None] == jnp.arange(groups, dtype=jnp.int32)[None, :]).astype(
        jnp.float32
    )
    totals, squares = lax.psum(
        (
            jnp.sum(onehot * rewards[:, None], axis=0),
            jnp.sum(onehot * (rewards * rewards)[:, None], axis=0),
        ),
        "dp",
    )
    mean = totals / GROUP
    std = jnp.sqrt(jnp.maximum(squares / GROUP - mean * mean, 0.09))
    advantage = (rewards - jnp.sum(onehot * mean[None, :], axis=1)) / jnp.sum(
        onehot * std[None, :], axis=1
    )
    per_roll = advantage / completion_live_lengths.astype(jnp.float32)
    rows = attention_rows.shape[0]
    slot = jnp.arange(rows, dtype=jnp.int32) % COMP
    limit = jnp.repeat(completion_live_lengths, COMP)
    row_w = jnp.where(slot < limit, jnp.repeat(per_roll, COMP), 0.0)
    whole_rows = jnp.dot(
        attention_rows,
        lax.all_gather(output_weight_frozen, "dp", axis=2, tiled=True)[0],
        preferred_element_type=jnp.float32,
    )
    frozen_output_rows = lax.psum_scatter(whole_rows, "tp", scatter_dimension=1, tiled=True)
    low_sum = lax.psum(jnp.dot(attention_rows, a_local.T, preferred_element_type=jnp.float32), "tp")
    low_rank_rows = low_sum.astype(jnp.bfloat16)
    adapted_output_rows = frozen_output_rows + adapter_scale * jnp.dot(
        low_rank_rows, up_matrix_columns, preferred_element_type=jnp.float32
    )
    advantage_weighted = (row_w[:, None] * upstream.astype(jnp.float32)).astype(jnp.bfloat16)
    backward_result = lax.psum(
        jnp.dot(advantage_weighted, up_matrix_columns.T, preferred_element_type=jnp.float32), "tp"
    ).astype(jnp.bfloat16)
    down_gradient = adapter_scale * lax.dot_general(
        backward_result,
        attention_rows,
        (((0,), (0,)), ((), ())),
        preferred_element_type=jnp.float32,
    )
    up_gradient = adapter_scale * lax.dot_general(
        low_rank_rows,
        advantage_weighted,
        (((0,), (0,)), ((), ())),
        preferred_element_type=jnp.float32,
    )
    grad_a_part, grad_b_part = (
        lax.psum_scatter(down_gradient[:, None, :], "dp", scatter_dimension=2, tiled=True),
        lax.psum_scatter(up_gradient[:, None, :], "dp", scatter_dimension=2, tiled=True),
    )
    return (decode_state, adapted_output_rows, grad_a_part, grad_b_part)


def solution(mesh):
    placed = (
        P("dp", None),
        P(),
        P("dp", "tp", None),
        P("dp", None, "tp", None),
        P("dp"),
        P("tp", None, "dp"),
        P(None, "tp", "dp"),
        P(None, "tp", "dp"),
        P("dp", "tp"),
        P("dp", "tp"),
        P("dp"),
        P("dp"),
        P("dp"),
    )
    ndp, ntp = mesh.shape["dp"], mesh.shape["tp"]

    def body(*args):
        width = args[5].shape[2]
        piece = args[6].shape[2]
        if ntp == 4 and ndp == 8 and piece % 128 == 0 and width % CHUNK == 0:
            return fused_shards(ndp, ntp, *args)
        return shards(*args)

    return jax.shard_map(
        body,
        mesh=mesh,
        in_specs=placed,
        out_specs=(P("dp", None), P("dp", "tp"), P(None, "tp", "dp"), P(None, "tp", "dp")),
        check_vma=False,
    )
```

```python
import math

import jax
import jax.numpy as jnp
from jax import lax
from jax.experimental import pallas as pl
from jax.experimental.pallas import tpu as pltpu
from jax.sharding import PartitionSpec as P

HD = 128
HEADS_TP = 8
GROUP = 4
COMP = 256


adapter_scale = 2.0


def rms_norm(decode_state, gain):
    scale = lax.rsqrt(jnp.mean(decode_state * decode_state, axis=-1, keepdims=True) + 1e-05)
    return decode_state * scale * gain.astype(jnp.float32)


def attend(query, cache, lengths, new_keys, new_values):
    head = query.shape[-1]
    slots = cache.shape[1]
    factor = 1.0 / math.sqrt(head)
    keys = cache[:, :, :head].astype(jnp.float32)
    values = cache[:, :, head:]
    scores = jnp.einsum("bhd,bcd->bhc", query, keys, precision=lax.Precision.HIGHEST) * factor
    valid = jnp.arange(slots, dtype=jnp.int32)[None, None, :] < lengths[:, None, None]
    scores = jnp.where(valid, scores, -1e30)
    extra = jnp.einsum("bhd,bed->bhe", query, new_keys, precision=lax.Precision.HIGHEST) * factor
    joined = jnp.concatenate([scores, extra], axis=-1)
    top = jnp.max(joined, axis=-1, keepdims=True)
    expo = jnp.exp(joined - top)
    probs = (expo / jnp.sum(expo, axis=-1, keepdims=True)).astype(jnp.bfloat16)
    out = jnp.einsum("bhc,bcd->bhd", probs[..., :slots], values, preferred_element_type=jnp.float32)
    out = out + jnp.einsum(
        "bhe,bed->bhd",
        probs[..., slots:].astype(jnp.float32),
        new_values,
        precision=lax.Precision.HIGHEST,
    )
    return out.astype(jnp.bfloat16).reshape(query.shape[0], -1)


MESH = pl.DeviceIdType.MESH
F32 = jnp.float32
BF16 = jnp.bfloat16
NT = (((1,), (1,)), ((), ()))
TN = (((0,), (0,)), ((), ()))
CHUNK = 256
SEGS = 4
ROW_PARTS = 8


def split3(v):
    hi = v.astype(BF16)
    rest = v - hi.astype(F32)
    mid = rest.astype(BF16)
    lo = (rest - mid.astype(F32)).astype(BF16)
    return jnp.concatenate([hi, mid, lo], axis=0)


def exact_dot(v, w, dims=(((1,), (0,)), ((), ()))):
    n = v.shape[0]
    r = lax.dot_general(split3(v), w, dims, preferred_element_type=F32)
    return r[:n] + r[n : 2 * n] + r[2 * n :]


def rows_of(ref, n):
    return jnp.concatenate([ref[i] for i in range(n)], axis=0)


def lanes_of(ref, n):
    return jnp.concatenate([ref[i] for i in range(n)], axis=1)


def fused_kernel(
    ndp,
    ntp,
    h_ref,
    gain_ref,
    wqkv_in,
    cache_in,
    lens_ref,
    wo_in,
    a_ref,
    b_ref,
    x_in,
    up_in,
    rew_ref,
    idx_ref,
    live_ref,
    dec_out,
    rows_out,
    ga_out,
    gb_out,
    hsend,
    stats_ref,
    hbuf,
    abuf,
    bdbuf,
    statbuf,
    qsend,
    qside,
    qline,
    qrecv,
    asend,
    arecv,
    usend,
    urecv,
    fsend,
    frecv,
    lbsend,
    lbhalf,
    lbfull,
    gown,
    gsend,
    grecv,
    gzsend,
    gzrecv,
    wt_ref,
    xbuf,
    wbuf,
    pbuf,
    prcv,
    ds_s,
    ds_r,
    ts_s,
    ts_r,
    bd_s,
    bd_r,
    xs_s,
    xs_r,
    wl_s,
    wl_r,
    ps_s,
    ps_r,
    gy_s,
    gy_r,
    gz_s,
    gz_r,
    lb_s,
    lb_r,
    ab_s,
    ab_r,
    wo_ref,
    x_ref,
    wqkv_ref,
    cache_ref,
    up_ref,
    in_s,
    out_ref,
    dec_ref,
    ga_ref,
    gb_ref,
    out_s,
    fin_s,
    acc,
    qy_s,
    qy_r,
    qz_s,
    qz_r,
    ay_s,
    ay_r,
    az_s,
    az_r,
):
    d = lax.axis_index("dp")
    t = lax.axis_index("tp")
    z, y = d // 2, d % 2
    x, c = t // 2, t % 2
    nz = ndp // 2
    rolls, model = h_ref.shape
    width = model // ndp
    rank = a_ref.shape[0]
    piece = a_ref.shape[1]
    chunks = wo_ref.shape[1] // CHUNK
    qkvw = wqkv_ref.shape[1]
    rows = x_ref.shape[0]
    mate = 2 * x + (1 - c)
    other_y = 2 * z + (1 - y)

    def fetch(k):
        src, dst = (
            (wo_in, wo_ref),
            (x_in, x_ref),
            (wqkv_in, wqkv_ref),
            (cache_in, cache_ref),
            (up_in, up_ref),
        )[k]
        return pltpu.make_async_copy(src, dst, in_s.at[k])

    for k in range(5):
        fetch(k).start()
    barrier = pltpu.get_barrier_semaphore()
    for i in range(ndp):
        for j in range(ntp):
            if i or j:
                pl.semaphore_signal(
                    barrier,
                    inc=1,
                    device_id=((d + i) % ndp, (t + j) % ntp),
                    device_id_type=MESH,
                )
    pl.semaphore_wait(barrier, ndp * ntp - 1)

    sent = []

    def send(src, dst, s, r, dev):
        cp = pltpu.make_async_remote_copy(
            src_ref=src, dst_ref=dst, send_sem=s, recv_sem=r, device_id=dev, device_id_type=MESH
        )
        return cp

    def dp_start(e, src, dst):
        for off in range(1, ndp):
            peer = (d + off) % ndp
            send(src(peer), dst.at[d], ds_s.at[e], ds_r.at[e], (peer, t)).start()
        whole = dst.at[pl.ds(0, ndp - 1)]
        sent.append(send(whole, whole, ds_s.at[e], ds_r.at[e], (d, (t + 1) % ntp)))

    def dp_wait(e, dst):
        whole = dst.at[pl.ds(0, ndp - 1)]
        send(whole, whole, ds_s.at[e], ds_r.at[e], (d, (t + 1) % ntp)).wait_recv()

    def tp_start(e, src, dst):
        for off in range(1, ntp):
            peer = (t + off) % ntp
            send(src, dst.at[t], ts_s.at[e], ts_r.at[e], (d, peer)).start()
        whole = dst.at[pl.ds(0, ntp - 1)]
        sent.append(send(whole, whole, ts_s.at[e], ts_r.at[e], (d, (t + 1) % ntp)))

    def tp_wait(e, dst):
        whole = dst.at[pl.ds(0, ntp - 1)]
        send(whole, whole, ts_s.at[e], ts_r.at[e], (d, (t + 1) % ntp)).wait_recv()

    for i in range(ndp):
        hsend[i] = h_ref[:, i * width : (i + 1) * width]
    lane = lax.broadcasted_iota(jnp.int32, (1, 128), 1)
    ones = [jnp.where(lane == idx_ref[r], 1.0, 0.0) for r in range(rolls)]
    stats_ref[...] = jnp.zeros_like(stats_ref)
    for r in range(rolls):
        stats_ref[0:1] += ones[r] * rew_ref[r]
        stats_ref[1:2] += ones[r] * (rew_ref[r] * rew_ref[r])

    dp_start(0, lambda p: hsend.at[p], hbuf)
    hbuf[d] = hsend[d]
    abuf[y, z, 0] = a_ref[...]
    abuf[y, z, 1] = b_ref[...]
    for k, ref in enumerate((a_ref, b_ref)):
        for off in range(1, nz):
            peer = 2 * ((z + off) % nz) + y
            send(ref, abuf.at[y, z, k], ab_s.at[0], ab_r.at[0], (peer, t)).start()
    others = abuf.at[0, pl.ds(0, nz - 1)]
    sent.append(send(others, others, ab_s.at[0], ab_r.at[0], (other_y, t)))
    dp_start(1, lambda p: stats_ref, statbuf)
    statbuf[d] = stats_ref[...]
    per = width // piece
    half = ndp // per
    src_t = d // half

    def up_block(tj):
        return send(bdbuf, bdbuf, bd_s, bd_r, (d, tj))

    fetch(0).wait()
    fetch(1).wait()
    xcp = send(x_ref, xbuf.at[y, c], xs_s.at[0], xs_r.at[0], (d, mate))
    xcp.start()
    sent.append(xcp)
    xbuf[y, c] = x_ref[...]

    def row_send(k):
        part = rows // ROW_PARTS
        if k >= ROW_PARTS:
            return
        seg = pl.ds(k * part, part)
        send(
            x_ref.at[seg], xbuf.at[y, c, seg], xs_s.at[1], xs_r.at[1], (other_y, t)
        ).start()

    def rows_whole():
        return send(x_ref, xbuf.at[1 - y, c], xs_s.at[1], xs_r.at[1], (other_y, t))

    def relay(dst_core):
        return send(
            xbuf.at[1 - y, c], xbuf.at[1 - y, dst_core], xs_s.at[2], xs_r.at[2], (d, mate)
        )

    feats = wo_ref.shape[0]
    pieces = chunks * SEGS
    near, far = z // 2, 1 - z // 2
    end = jnp.logical_or(z == 0, z == nz - 1)
    role_m = jnp.logical_and(jnp.logical_not(end), c == z // 2)
    role_2 = jnp.logical_and(jnp.logical_not(end), c != z // 2)
    lead = jnp.where(c == near, far, near)
    trail = 1 - lead
    z_up, z_dn = jnp.minimum(z + 1, nz - 1), jnp.maximum(z - 1, 0)
    z_in = jnp.where(z < 2, z_up, z_dn)
    z_out = jnp.where(z < 2, z_dn, z_up)

    cuts = [(ch, 0, CHUNK) for ch in range(chunks - 1)]
    cuts += [(chunks - 1, h * 128, 128) for h in range(CHUNK // 128)]

    def seg_of(k):
        ch, part = k // SEGS, k % SEGS
        if ch < chunks - 1:
            size = feats // SEGS
            return ch, pl.ds(part * size, size), 0, CHUNK
        halves = CHUNK // 128
        size = feats * halves // SEGS
        per_half = SEGS // halves
        return ch, pl.ds((part % per_half) * size, size), (part // per_half) * 128, 128

    def own(k, which, zt):
        ch, seg, off, num = seg_of(k)
        return send(
            wo_ref.at[seg, pl.ds(ch * CHUNK + off, num)],
            wbuf.at[z // 2, c, ch, seg, pl.ds(off, num)],
            wl_s.at[which],
            wl_r.at[z // 2, c, k],
            (2 * zt + y, 2 * x + z % 2),
        )

    def hop(blk, j, which, zt):
        k, cc = j // 2, j % 2
        ch, seg, off, num = seg_of(k)
        ref = wbuf.at[blk, cc, ch, seg, pl.ds(off, num)]
        return send(ref, ref, wl_s.at[which], wl_r.at[blk, cc, k], (2 * zt + y, t))

    def own_tick(k):
        @pl.when(z < nz - 1)
        def _():
            own(k, 0, z_up).start()

        @pl.when(z > 0)
        def _():
            own(k, 1, z_dn).start()

        @pl.when(z % 2 != c)
        def _():
            own(k, 2, z).start()

    waited = {"near": 0, "far_m": 0, "far_2": 0}

    def arrive(name, blk, upto):
        for j in range(waited[name], upto):
            hop(blk, j, 3, z_in).wait_recv()
        waited[name] = max(waited[name], upto)

    def relay_tick(name, blk, lo, hi, which, zt):
        hi = min(hi, 2 * pieces)
        arrive(name, blk, hi)
        for j in range(lo, hi):
            hop(blk, j, which, zt).start()

    clock = [0]
    ticks = 3 * pieces

    def tick():
        n = clock[0]
        if n >= ticks:
            return
        clock[0] += 1
        if n < pieces:
            own_tick(n)
            row_send(n)
            return
        m = n - pieces

        @pl.when(role_m)
        def _():
            if m < pieces:
                relay_tick("near", near, 2 * m, 2 * m + 2, 3, z_in)
                relay_tick("far_m", far, 2 * m, 2 * m + 2, 4, z_out)

        if m >= pieces:

            @pl.when(role_2)
            def _():
                relay_tick("far_2", far, 2 * (m - pieces), 2 * (m - pieces) + 2, 4, z_out)

    def pump(n):
        for _ in range(n):
            tick()

    pump(2)

    @pl.when(z % 2 == c)
    def _():
        for ch in range(chunks):
            wbuf[z // 2, c, ch] = wo_ref[:, ch * CHUNK : (ch + 1) * CHUNK]

    def q_side(step):
        return send(qsend.at[step, 1 - y], qside.at[step], qy_s.at[step], qy_r.at[step], (other_y, t))

    def q_lines(step):
        whole = qrecv.at[step, pl.ds(0, nz - 1)]
        return send(whole, whole, qz_s.at[step], qz_r.at[step], (other_y, t))

    def a_side(step, yy):
        ref = arecv.at[step, yy]
        return send(ref, ref, ay_s.at[step], ay_r.at[step], (other_y, t))

    def a_lines(step):
        whole = arecv.at[step, 0, pl.ds(0, nz - 1)]
        return send(whole, whole, az_s.at[step], az_r.at[step], (other_y, t))

    def ab_side(yy):
        return send(abuf.at[yy], abuf.at[yy], ab_s.at[1], ab_r.at[1], (other_y, t))

    def lb_core():
        return send(lbsend.at[1 - c], lbhalf.at[2], lb_s.at[0], lb_r.at[0], (d, mate))

    def lb_chip():
        return send(lbhalf.at[0], lbhalf.at[1], lb_s.at[1], lb_r.at[1], (d, 2 * (1 - x) + c))

    def lb_back(core):
        return send(lbfull.at[core], lbfull.at[core], lb_s.at[2], lb_r.at[2], (d, mate))

    def g_side():
        return send(gsend.at[1 - y], grecv, gy_s, gy_r, (other_y, t))

    def g_line(off):
        zt = (z + off) % nz
        return send(gzsend.at[zt], gzrecv.at[z], gz_s, gz_r, (2 * zt + y, t))

    def g_lines():
        whole = gzrecv.at[pl.ds(0, nz - 1)]
        return send(whole, whole, gz_s, gz_r, (other_y, t))

    def share(dx, dy, u):
        zz = jnp.where(dx == 1, 1 - x, x)
        yy = jnp.where(dy == 1, 1 - y, y)
        ch, off, num = cuts[u]
        cols = pl.ds(off, num)
        return send(
            pbuf.at[2 * dx + dy, ch, :, cols],
            prcv.at[2 * dx + dy, ch, :, cols],
            ps_s,
            ps_r.at[u],
            (2 * z + yy, 2 * zz + c),
        )

    def rows_in():
        rows_whole().wait_recv()
        relay(c).start()

    def rows_ready():
        send(x_ref, xbuf.at[y, 1 - c], xs_s.at[0], xs_r.at[0], (d, mate)).wait_recv()
        relay(1 - c).wait_recv()

    def columns(yy, u):
        ch, off, num = cuts[u]
        return pl.ds(pl.multiple_of((yy * chunks + ch) * CHUNK + off, 128), num)

    def final(k):
        src, dst = ((dec_ref, dec_out), (ga_ref, ga_out), (gb_ref, gb_out))[k]
        return pltpu.make_async_copy(src, dst, fin_s.at[k])

    def emit(dy, u):
        cols = columns((y + dy) % 2, u)
        return pltpu.make_async_copy(out_ref.at[:, cols], rows_out.at[:, cols], out_s)

    def unit(blk, u):
        ch, off, num = cuts[u]
        cols = pl.ds(off, num)
        own_ks = [k for k in range(pieces) if seg_of(k)[0] == ch and seg_of(k)[2] == off]
        upto = 2 * (max(own_ks) + 1)
        leads = blk is lead

        @pl.when(role_m)
        def _():
            arrive("far_m" if leads else "near", blk, upto)

        if not leads:

            @pl.when(role_2)
            def _():
                arrive("far_2", blk, upto)

        others = jnp.logical_not(role_m) if leads else end
        parts = [(k, cc) for k in own_ks for cc in range(2)]

        def landed(todo):
            for cc in range(2):
                mine = jnp.logical_and(c + 2 * blk == z, c == cc)
                ks = [k for k, core in todo if core == cc]

                if ks:

                    @pl.when(jnp.logical_and(others, jnp.logical_not(mine)))
                    def _():
                        for k in ks:
                            hop(blk, 2 * k + cc, 3, z_in).wait_recv()

        dx = jnp.where(blk == x, 0, 1)

        def put(dy, p):
            if dy == 1:
                pbuf[2 * dx + 1, ch, :, cols] = p.astype(BF16)
                share(dx, 1, u).start()
            else:

                @pl.when(dx == 1)
                def _():
                    pbuf[2, ch, :, cols] = p.astype(BF16)
                    share(1, 0, u).start()

                @pl.when(dx == 0)
                def _():
                    out_ref[:, columns(y, u)] += p

        if leads or u < len(cuts) - 1:
            landed(parts)
            for dy in (1, 0):
                yy = (y + dy) % 2
                p = jnp.dot(xbuf[yy, 0], wbuf[blk, 0, ch, :, cols], preferred_element_type=F32)
                p = p + jnp.dot(xbuf[yy, 1], wbuf[blk, 1, ch, :, cols], preferred_element_type=F32)
                put(dy, p)
            return
        for i, (k, cc) in enumerate(parts):
            landed([(k, cc)])
            seg = seg_of(k)[1]
            for dy in (1, 0):
                yy = (y + dy) % 2
                p = jnp.dot(
                    xbuf[yy, cc, :, seg], wbuf[blk, cc, ch, seg, cols], preferred_element_type=F32
                )
                if i:
                    p = p + acc[dy]
                if i < len(parts) - 1:
                    acc[dy] = p
                else:
                    put(dy, p)

    dp_wait(0, hbuf)
    state = jnp.concatenate([hbuf[i].astype(F32) for i in range(ndp)], axis=0)
    gains = gain_ref[...].astype(F32)
    line = lax.broadcasted_iota(jnp.int32, gains.shape, 0)
    gain = jnp.concatenate(
        [
            jnp.sum(jnp.where(line == d * (width // 128) + i, gains, 0.0), axis=0, keepdims=True)
            for i in range(width // 128)
        ],
        axis=1,
    )
    fetch(2).wait()
    new_k, new_v = [], []
    factor = 1.0 / math.sqrt(HD)

    for step in range(2):
        squares = jnp.sum(state * state, axis=-1, keepdims=True)
        part = exact_dot(state * gain, wqkv_ref[...])
        both = jnp.concatenate([part, jnp.broadcast_to(squares, (ndp * rolls, 128))], axis=1)
        for i in range(ndp):
            qsend[step, i % 2, i // 2] = both[i * rolls : (i + 1) * rolls]
        q_side(step).start()
        pump(1)
        if step == 1:
            lb_chip().wait_recv()
            lbfull[c] = (lbhalf[0] + lbhalf[1]).astype(BF16)
            lb_back(c).start()
        if step == 0:
            send(others, others, ab_s.at[0], ab_r.at[0], (other_y, t)).wait_recv()
            ab_side(y).start()
            dp_wait(1, statbuf)
            tot = statbuf[0]
            for i in range(1, ndp):
                tot = tot + statbuf[i]
            mean = tot[0:1] / GROUP
            std = jnp.sqrt(jnp.maximum(tot[1:2] / GROUP - mean * mean, 0.09))
            fetch(4).wait()
            for r in range(rolls):
                one, rew = ones[r], rew_ref[r]
                live = live_ref[r].astype(F32)
                adv = (rew - jnp.sum(one * mean, axis=1, keepdims=True)) / jnp.sum(
                    one * std, axis=1, keepdims=True
                )
                slot = lax.broadcasted_iota(jnp.int32, (COMP, 1), 0).astype(F32)
                row_w = jnp.where(slot < live, adv / live, 0.0)
                seg = pl.ds(r * COMP, COMP)
                wt_ref[seg, :] = (row_w * up_ref[seg, :].astype(F32)).astype(BF16)
        q_side(step).wait_recv()
        for i in range(nz):
            qline[step, i] = qsend[step, y, i] + qside[step, i]
        for off in range(1, nz):
            zt = (z + off) % nz
            src, dst = qline.at[step, zt], qrecv.at[step, z]
            send(src, dst, qz_s.at[step], qz_r.at[step], (2 * zt + y, t)).start()
        pump(2)
        q_lines(step).wait_recv()
        total = qline[step, z]
        for off in range(1, nz):
            total = total + qrecv[step, (z + off) % nz]
        qkv = total[:, :qkvw] * lax.rsqrt(total[:, qkvw : qkvw + 1] / model + 1e-05)
        new_k.append(qkv[:, HEADS_TP * HD : HEADS_TP * HD + HD])
        new_v.append(qkv[:, HEADS_TP * HD + HD :])
        if step == 0:
            fetch(3).wait()
        heads = []
        for b in range(rolls):
            q = jnp.concatenate(
                [qkv[b : b + 1, h * HD : (h + 1) * HD] for h in range(HEADS_TP)], axis=0
            )
            scores = exact_dot(q, cache_ref[b, :, :HD], NT) * factor
            pos = lax.broadcasted_iota(jnp.int32, scores.shape, 1)
            scores = jnp.where(pos < lens_ref[b], scores, -1e30)
            extra = [
                jnp.sum(q * k[b : b + 1], axis=-1, keepdims=True) * factor for k in new_k
            ]
            top = jnp.max(scores, axis=-1, keepdims=True)
            for e in extra:
                top = jnp.maximum(top, e)
            expo = jnp.exp(scores - top)
            ee = [jnp.exp(e - top) for e in extra]
            den = jnp.sum(expo, axis=-1, keepdims=True)
            for e in ee:
                den = den + e
            att = jnp.dot(
                (expo / den).astype(BF16), cache_ref[b, :, HD:], preferred_element_type=F32
            )
            for e, v in zip(ee, new_v):
                att = att + (e / den).astype(BF16).astype(F32) * v[b : b + 1]
            heads.append(jnp.concatenate([att[h : h + 1] for h in range(HEADS_TP)], axis=1))
        asend[step] = jnp.concatenate(heads, axis=0).astype(BF16)
        for off in range(1, nz):
            zt = (z + off) % nz
            send(
                asend.at[step], arecv.at[step, y, z], az_s.at[step], az_r.at[step], (2 * zt + y, t)
            ).start()
        pump(1)
        arecv[step, y, z] = asend[step]
        if step == 0:
            ab_side(1 - y).wait_recv()
            at, bt = (
                jnp.concatenate([abuf[i % 2, i // 2, k] for i in range(ndp)], axis=1)
                for k in range(2)
            )

            @pl.when(t == src_t)
            def _():
                for j in range(per):
                    bdbuf[j] = abuf[j % 2, (d % half) * (per // 2) + j // 2, 1]
                for off in range(1, ntp):
                    up_block((t + off) % ntp).start()

            for k, (m, v) in enumerate(((at, x_ref), (bt, wt_ref))):
                lb = lax.dot_general(m, v[...], NT, preferred_element_type=F32)
                for i in range(2):
                    lbsend[i, k] = lb[:, i * (rows // 2) : (i + 1) * (rows // 2)]
            lb_core().start()
        else:
            lb_back(c).wait_send()
            lb_back(1 - c).wait_recv()
            low_t, back_t = lanes_of(lbfull.at[:, 0], 2), lanes_of(lbfull.at[:, 1], 2)
            ga = adapter_scale * jnp.dot(back_t, x_ref[...], preferred_element_type=F32)
            gb = adapter_scale * jnp.dot(low_t, wt_ref[...], preferred_element_type=F32)
            for i in range(ndp):
                for k, g in enumerate((ga, gb)):
                    part = g[:, i * piece : (i + 1) * piece]
                    gown[i % 2, i // 2, k] = part
                    gsend[i % 2, i // 2, k] = part.astype(BF16)
            g_side().start()
            out_ref[...] = adapter_scale * lax.dot_general(
                low_t, bt, TN, preferred_element_type=F32
            )
        a_lines(step).wait_recv()
        a_side(step, y).start()
        pump(1)
        a_side(step, 1 - y).wait_recv()
        attended = jnp.concatenate(
            [arecv[step, i % 2, i // 2].astype(F32) for i in range(ndp)], axis=0
        ).astype(BF16)
        usend[step, :, :width] = jnp.dot(attended, wo_ref[...], preferred_element_type=F32)
        usend[step, :, width:] = jnp.concatenate(
            [
                lax.dot_general(attended, at, NT, preferred_element_type=F32),
                jnp.zeros((ndp * rolls, 128 - rank), F32),
            ],
            axis=1,
        )
        tp_start(step, usend.at[step], urecv.at[step])
        pump(2)
        urecv[step, t] = usend[step]
        if step == 0:
            lb_core().wait_recv()
            lbhalf[0] = lbsend[c] + lbhalf[2]
            lb_chip().start()

            @pl.when(t != src_t)
            def _():
                up_block(src_t).wait_recv()

            bd = lanes_of(bdbuf, per)
        tp_wait(step, urecv.at[step])
        upd = urecv[step, 0]
        for i in range(1, ntp):
            upd = upd + urecv[step, i]
        state = state + (
            upd[:, :width] + adapter_scale * exact_dot(upd[:, width : width + rank], bd)
        )

    for i in range(ndp):
        fsend[i] = state[i * rolls : (i + 1) * rolls]
    dp_start(2, lambda p: fsend.at[p], frecv)
    frecv[d] = fsend[d]
    rows_in()
    g_side().wait_recv()
    for i in range(nz):
        gzsend[i] = (gown[y, i] + grecv[i].astype(F32)).astype(BF16)
    pump(2)
    rows_ready()
    for u in range(len(cuts)):
        unit(lead, u)
        pump(2)
    dp_wait(2, frecv)
    for i in range(ndp):
        dec_ref[:, i * width : (i + 1) * width] = frecv[i]
    final(0).start()
    for cp in sent:
        cp.wait_send()
    while clock[0] < 2 * pieces + pieces // 2:
        pump(1)
    unit(trail, 0)
    pump(ticks)
    unit(trail, 1)
    for off in range(1, nz):
        g_line(off).start()
    for u in range(2, len(cuts)):
        unit(trail, u)
    for u in range(len(cuts)):
        ch, off, num = cuts[u]
        three = prcv.at[pl.ds(1, 3), ch, :, pl.ds(off, num)]
        send(three, three, ps_s, ps_r.at[u], (d, mate)).wait_recv()
        for dx, dy in ((1, 0), (0, 1), (1, 1)):
            got = prcv[2 * dx + dy, ch, :, pl.ds(off, num)].astype(F32)
            out_ref[:, columns((y + dy) % 2, u)] += got
        for dy in range(2):
            emit(dy, u).start()

    g = gown[y, z] + grecv[z].astype(F32)
    g_lines().wait_recv()
    for off in range(1, nz):
        g = g + gzrecv[(z + nz - off) % nz].astype(F32)
    ga_ref[...] = g[0]
    gb_ref[...] = g[1]
    final(1).start()
    final(2).start()
    pltpu.make_async_copy(out_ref, rows_out, out_s).wait()
    for k in range(3):
        final(k).wait()

    def drain(which, full):
        send(full, full, wl_s.at[which], wl_r.at[0, 0, 0], (d, mate)).wait_send()

    @pl.when(z < nz - 1)
    def _():
        drain(0, wbuf.at[0, 0])

    @pl.when(z > 0)
    def _():
        drain(1, wbuf.at[0, 0])

    @pl.when(z % 2 != c)
    def _():
        drain(2, wbuf.at[0, 0])

    @pl.when(role_m)
    def _():
        drain(3, wbuf.at[0])

    @pl.when(jnp.logical_not(end))
    def _():
        drain(4, wbuf.at[0])

    three = pbuf.at[pl.ds(1, 3)]
    send(three, three, ps_s, ps_r.at[0], (d, mate)).wait_send()
    rows_whole().wait_send()
    relay(c).wait_send()
    g_side().wait_send()
    for step in range(2):
        q_side(step).wait_send()
        q_lines(step).wait_send()
        a_side(step, y).wait_send()
        a_lines(step).wait_send()
    lb_core().wait_send()
    lb_chip().wait_send()
    ab_side(y).wait_send()
    g_lines().wait_send()

    @pl.when(t == src_t)
    def _():
        copies = wo_ref.at[pl.ds(0, (ntp - 1) * rank)]
        send(copies, copies, bd_s, bd_r, (d, mate)).wait_send()


def finish_kernel(*refs):
    n = len(refs) // 2
    copies = [pltpu.make_async_copy(refs[i], refs[n + i], refs[-1].at[i]) for i in range(n)]
    for cp in copies:
        cp.start()
    for cp in copies:
        cp.wait()


def fused_shards(
    ndp,
    ntp,
    hidden,
    attention_norm_gain,
    query_key_value_weight,
    key_value_cache,
    cache_fill_lengths,
    output_weight_frozen,
    adapter_down_transposed,
    adapter_up_matrix,
    attention_rows,
    upstream,
    rewards,
    prompt_group_index,
    completion_live_lengths,
):
    rolls, model = hidden.shape
    slots = key_value_cache.shape[1]
    width = model // ndp
    rank, _, piece = adapter_down_transposed.shape
    rows, shard = attention_rows.shape
    qkvw = query_key_value_weight.shape[2]
    feats = output_weight_frozen.shape[1]
    chunks = width // CHUNK
    vm = pl.BlockSpec(memory_space=pltpu.VMEM)
    sm = pl.BlockSpec(memory_space=pltpu.SMEM)
    hbm = pl.BlockSpec(memory_space=pltpu.HBM)
    dma = pltpu.SemaphoreType.DMA
    V = pltpu.VMEM
    dec, out, ga, gb = pl.pallas_call(
        lambda *refs: fused_kernel(ndp, ntp, *refs),
        out_shape=(
            pltpu.VMEM((rolls, model), F32),
            pltpu.VMEM((rows, shard), F32),
            pltpu.VMEM((rank, piece), F32),
            pltpu.VMEM((rank, piece), F32),
        ),
        in_specs=[vm, vm, hbm, hbm, sm, hbm, vm, vm, hbm, hbm, sm, sm, sm],
        out_specs=(pl.BlockSpec(memory_space=pl.ANY),) * 4,
        scratch_shapes=[
            V((ndp, rolls, width), BF16),
            V((2, 128), F32),
            V((ndp, rolls, width), BF16),
            V((2, ndp // 2, 2, rank, piece), BF16),
            V((width // piece, rank, piece), BF16),
            V((ndp, 2, 128), F32),
            V((2, 2, ndp // 2, rolls, qkvw + 128), F32),
            V((2, ndp // 2, rolls, qkvw + 128), F32),
            V((2, ndp // 2, rolls, qkvw + 128), F32),
            V((2, ndp // 2, rolls, qkvw + 128), F32),
            V((2, rolls, feats), BF16),
            V((2, 2, ndp // 2, rolls, feats), BF16),
            V((2, ndp * rolls, width + 128), F32),
            V((2, ntp, ndp * rolls, width + 128), F32),
            V((ndp, rolls, width), F32),
            V((ndp, rolls, width), F32),
            V((2, 2, rank, rows // 2), F32),
            V((3, 2, rank, rows // 2), F32),
            V((2, 2, rank, rows // 2), BF16),
            V((2, ndp // 2, 2, rank, piece), F32),
            V((2, ndp // 2, 2, rank, piece), BF16),
            V((ndp // 2, 2, rank, piece), BF16),
            V((ndp // 2, 2, rank, piece), BF16),
            V((ndp // 2, 2, rank, piece), BF16),
            V((rows, shard), BF16),
            V((2, 2, rows, shard), BF16),
            V((2, 2, chunks, feats, CHUNK), BF16),
            V((4, chunks, rows, CHUNK), BF16),
            V((4, chunks, rows, CHUNK), BF16),
            dma((3,)),
            dma((3,)),
            dma((2,)),
            dma((2,)),
            dma,
            dma,
            dma((3,)),
            dma((3,)),
            dma((5,)),
            dma((2, 2, chunks * SEGS)),
            dma,
            dma((chunks - 1 + CHUNK // 128,)),
            dma,
            dma,
            dma,
            dma,
            dma((3,)),
            dma((3,)),
            dma((2,)),
            dma((2,)),
            V((feats, width), BF16),
            V((rows, shard), BF16),
            V((width, qkvw), BF16),
            V((rolls, slots, 2 * HD), BF16),
            V((rows, shard), BF16),
            dma((5,)),
            V((rows, shard), F32),
            V((rolls, model), F32),
            V((rank, piece), F32),
            V((rank, piece), F32),
            dma,
            dma((3,)),
            V((2, rows, 128), F32),
        ]
        + [dma((2,))] * 8,
        compiler_params=pltpu.CompilerParams(
            collective_id=0, has_side_effects=True, vmem_limit_bytes=64815104
        ),
    )(
        hidden,
        attention_norm_gain.reshape(model // 128, 128),
        query_key_value_weight[:, 0, :],
        key_value_cache[:, :, 0, :],
        cache_fill_lengths,
        output_weight_frozen[0],
        adapter_down_transposed[:, 0, :],
        adapter_up_matrix[:, 0, :],
        attention_rows,
        upstream,
        rewards,
        prompt_group_index,
        completion_live_lengths,
    )
    parts = (dec, out, ga[:, None, :], gb[:, None, :])
    anywhere = (pl.BlockSpec(memory_space=pl.ANY),) * len(parts)
    return pl.pallas_call(
        finish_kernel,
        out_shape=tuple(jax.ShapeDtypeStruct(p.shape, F32) for p in parts),
        in_specs=[vm] * len(parts),
        out_specs=anywhere,
        scratch_shapes=[dma((len(parts),))],
        compiler_params=pltpu.CompilerParams(vmem_limit_bytes=2**20),
    )(*[pltpu.with_memory_space_constraint(p, pltpu.VMEM) for p in parts])


def shards(
    hidden,
    attention_norm_gain,
    query_key_value_weight,
    key_value_cache,
    cache_fill_lengths,
    output_weight_frozen,
    adapter_down_transposed,
    adapter_up_matrix,
    attention_rows,
    upstream,
    rewards,
    prompt_group_index,
    completion_live_lengths,
):
    a_piece, b_piece = (
        lax.all_gather(adapter_down_transposed, "dp", axis=2, tiled=True),
        lax.all_gather(adapter_up_matrix, "dp", axis=2, tiled=True),
    )
    b_whole = lax.all_gather(b_piece, "tp", axis=1, tiled=True)
    up_matrix_flat = b_whole.reshape(b_whole.shape[0], -1).astype(jnp.float32)
    a_local = a_piece[:, 0, :]
    up_matrix_columns = b_piece[:, 0, :]
    w_rows = query_key_value_weight[:, 0, :].astype(jnp.float32)
    w_cols = output_weight_frozen[0]
    query_width = HEADS_TP * HD
    local_rolls = hidden.shape[0]
    decode_state = hidden.astype(jnp.float32)
    keys_new = []
    values_new = []
    for step in range(2):
        normed = rms_norm(decode_state, attention_norm_gain)
        spread = lax.all_to_all(normed, "dp", split_axis=1, concat_axis=0, tiled=True)
        partial_value = jnp.dot(spread, w_rows, precision=lax.Precision.HIGHEST)
        qkv = lax.psum_scatter(partial_value, "dp", scatter_dimension=0, tiled=True)
        query = qkv[:, :query_width].reshape(local_rolls, HEADS_TP, HD)
        keys_new.append(qkv[:, query_width : query_width + HD])
        values_new.append(qkv[:, query_width + HD :])
        attended = attend(
            query,
            key_value_cache[:, :, 0, :],
            cache_fill_lengths,
            jnp.stack(keys_new, axis=1),
            jnp.stack(values_new, axis=1),
        )
        columns = jnp.dot(
            lax.all_gather(attended, "dp", axis=0, tiled=True),
            w_cols,
            preferred_element_type=jnp.float32,
        )
        returned_values = lax.all_to_all(columns, "dp", split_axis=0, concat_axis=1, tiled=True)
        low_rank_decode = jnp.dot(attended, a_local.T, preferred_element_type=jnp.float32)
        state_update = returned_values + adapter_scale * jnp.dot(
            low_rank_decode, up_matrix_flat, precision=lax.Precision.HIGHEST
        )
        decode_state = decode_state + lax.psum(state_update, "tp")
    groups = local_rolls * lax.axis_size("dp") // GROUP
    onehot = (prompt_group_index[:, None] == jnp.arange(groups, dtype=jnp.int32)[None, :]).astype(
        jnp.float32
    )
    totals, squares = lax.psum(
        (
            jnp.sum(onehot * rewards[:, None], axis=0),
            jnp.sum(onehot * (rewards * rewards)[:, None], axis=0),
        ),
        "dp",
    )
    mean = totals / GROUP
    std = jnp.sqrt(jnp.maximum(squares / GROUP - mean * mean, 0.09))
    advantage = (rewards - jnp.sum(onehot * mean[None, :], axis=1)) / jnp.sum(
        onehot * std[None, :], axis=1
    )
    per_roll = advantage / completion_live_lengths.astype(jnp.float32)
    rows = attention_rows.shape[0]
    slot = jnp.arange(rows, dtype=jnp.int32) % COMP
    limit = jnp.repeat(completion_live_lengths, COMP)
    row_w = jnp.where(slot < limit, jnp.repeat(per_roll, COMP), 0.0)
    whole_rows = jnp.dot(
        attention_rows,
        lax.all_gather(output_weight_frozen, "dp", axis=2, tiled=True)[0],
        preferred_element_type=jnp.float32,
    )
    frozen_output_rows = lax.psum_scatter(whole_rows, "tp", scatter_dimension=1, tiled=True)
    low_sum = lax.psum(jnp.dot(attention_rows, a_local.T, preferred_element_type=jnp.float32), "tp")
    low_rank_rows = low_sum.astype(jnp.bfloat16)
    adapted_output_rows = frozen_output_rows + adapter_scale * jnp.dot(
        low_rank_rows, up_matrix_columns, preferred_element_type=jnp.float32
    )
    advantage_weighted = (row_w[:, None] * upstream.astype(jnp.float32)).astype(jnp.bfloat16)
    backward_result = lax.psum(
        jnp.dot(advantage_weighted, up_matrix_columns.T, preferred_element_type=jnp.float32), "tp"
    ).astype(jnp.bfloat16)
    down_gradient = adapter_scale * lax.dot_general(
        backward_result,
        attention_rows,
        (((0,), (0,)), ((), ())),
        preferred_element_type=jnp.float32,
    )
    up_gradient = adapter_scale * lax.dot_general(
        low_rank_rows,
        advantage_weighted,
        (((0,), (0,)), ((), ())),
        preferred_element_type=jnp.float32,
    )
    grad_a_part, grad_b_part = (
        lax.psum_scatter(down_gradient[:, None, :], "dp", scatter_dimension=2, tiled=True),
        lax.psum_scatter(up_gradient[:, None, :], "dp", scatter_dimension=2, tiled=True),
    )
    return (decode_state, adapted_output_rows, grad_a_part, grad_b_part)


def solution(mesh):
    placed = (
        P("dp", None),
        P(),
        P("dp", "tp", None),
        P("dp", None, "tp", None),
        P("dp"),
        P("tp", None, "dp"),
        P(None, "tp", "dp"),
        P(None, "tp", "dp"),
        P("dp", "tp"),
        P("dp", "tp"),
        P("dp"),
        P("dp"),
        P("dp"),
    )
    ndp, ntp = mesh.shape["dp"], mesh.shape["tp"]

    def body(*args):
        width = args[5].shape[2]
        piece = args[6].shape[2]
        if ntp == 4 and ndp == 8 and piece % 128 == 0 and width % CHUNK == 0:
            return fused_shards(ndp, ntp, *args)
        return shards(*args)

    return jax.shard_map(
        body,
        mesh=mesh,
        in_specs=placed,
        out_specs=(P("dp", None), P("dp", "tp"), P(None, "tp", "dp"), P(None, "tp", "dp")),
        check_vma=False,
    )
```

```python
import math

import jax
import jax.numpy as jnp
from jax import lax
from jax.experimental import pallas as pl
from jax.experimental.pallas import tpu as pltpu
from jax.sharding import PartitionSpec as P

HD = 128
HEADS_TP = 8
GROUP = 4
COMP = 256


adapter_scale = 2.0


def rms_norm(decode_state, gain):
    scale = lax.rsqrt(jnp.mean(decode_state * decode_state, axis=-1, keepdims=True) + 1e-05)
    return decode_state * scale * gain.astype(jnp.float32)


def attend(query, cache, lengths, new_keys, new_values):
    head = query.shape[-1]
    slots = cache.shape[1]
    factor = 1.0 / math.sqrt(head)
    keys = cache[:, :, :head].astype(jnp.float32)
    values = cache[:, :, head:]
    scores = jnp.einsum("bhd,bcd->bhc", query, keys, precision=lax.Precision.HIGHEST) * factor
    valid = jnp.arange(slots, dtype=jnp.int32)[None, None, :] < lengths[:, None, None]
    scores = jnp.where(valid, scores, -1e30)
    extra = jnp.einsum("bhd,bed->bhe", query, new_keys, precision=lax.Precision.HIGHEST) * factor
    joined = jnp.concatenate([scores, extra], axis=-1)
    top = jnp.max(joined, axis=-1, keepdims=True)
    expo = jnp.exp(joined - top)
    probs = (expo / jnp.sum(expo, axis=-1, keepdims=True)).astype(jnp.bfloat16)
    out = jnp.einsum("bhc,bcd->bhd", probs[..., :slots], values, preferred_element_type=jnp.float32)
    out = out + jnp.einsum(
        "bhe,bed->bhd",
        probs[..., slots:].astype(jnp.float32),
        new_values,
        precision=lax.Precision.HIGHEST,
    )
    return out.astype(jnp.bfloat16).reshape(query.shape[0], -1)


MESH = pl.DeviceIdType.MESH
F32 = jnp.float32
BF16 = jnp.bfloat16
NT = (((1,), (1,)), ((), ()))
TN = (((0,), (0,)), ((), ()))
CHUNK = 256
SEGS = 4
ROW_PARTS = 8


def split3(v):
    hi = v.astype(BF16)
    rest = v - hi.astype(F32)
    mid = rest.astype(BF16)
    lo = (rest - mid.astype(F32)).astype(BF16)
    return jnp.concatenate([hi, mid, lo], axis=0)


def exact_dot(v, w, dims=(((1,), (0,)), ((), ()))):
    n = v.shape[0]
    r = lax.dot_general(split3(v), w, dims, preferred_element_type=F32)
    return r[:n] + r[n : 2 * n] + r[2 * n :]


def rows_of(ref, n):
    return jnp.concatenate([ref[i] for i in range(n)], axis=0)


def lanes_of(ref, n):
    return jnp.concatenate([ref[i] for i in range(n)], axis=1)


def fused_kernel(
    ndp,
    ntp,
    h_in,
    gain_in,
    wqkv_in,
    cache_in,
    lens_in,
    wo_in,
    a_in,
    b_in,
    x_in,
    up_in,
    rew_in,
    idx_in,
    live_in,
    dec_out,
    rows_out,
    ga_out,
    gb_out,
    hsend,
    stats_ref,
    hbuf,
    abuf,
    bdbuf,
    statbuf,
    qsend,
    qside,
    qline,
    qrecv,
    asend,
    arecv,
    usend,
    urecv,
    fsend,
    frecv,
    lbsend,
    lbhalf,
    lbfull,
    gown,
    gsend,
    grecv,
    gus,
    gur,
    gds,
    gdr,
    wt_ref,
    xbuf,
    wbuf,
    pbuf,
    prcv,
    ds_s,
    ds_r,
    ts_s,
    ts_r,
    bd_s,
    bd_r,
    xs_s,
    xs_r,
    wl_s,
    wl_r,
    ps_s,
    ps_r,
    gy_s,
    gy_r,
    gu_s,
    gu_r,
    gd_s,
    gd_r,
    lb_s,
    lb_r,
    ab_s,
    ab_r,
    wo_ref,
    x_ref,
    wqkv_ref,
    cache_ref,
    up_ref,
    in_s,
    out_ref,
    dec_ref,
    ga_ref,
    gb_ref,
    out_s,
    fin_s,
    acc,
    qy_s,
    qy_r,
    qz_s,
    qz_r,
    ay_s,
    ay_r,
    az_s,
    az_r,
    h_ref,
    gain_ref,
    a_ref,
    b_ref,
    lens_ref,
    rew_ref,
    idx_ref,
    live_ref,
):
    d = lax.axis_index("dp")
    t = lax.axis_index("tp")
    z, y = d // 2, d % 2
    x, c = t // 2, t % 2
    nz = ndp // 2
    rolls, model = h_ref.shape
    width = model // ndp
    rank = a_ref.shape[0]
    piece = a_ref.shape[1]
    chunks = wo_ref.shape[1] // CHUNK
    qkvw = wqkv_ref.shape[1]
    rows = x_ref.shape[0]
    mate = 2 * x + (1 - c)
    other_y = 2 * z + (1 - y)

    def fetch(k):
        src, dst = (
            (wo_in, wo_ref),
            (x_in, x_ref),
            (wqkv_in, wqkv_ref),
            (cache_in, cache_ref),
            (up_in, up_ref),
            (h_in, h_ref),
            (a_in, a_ref),
            (b_in, b_ref),
            (idx_in, idx_ref),
            (rew_in, rew_ref),
            (gain_in, gain_ref),
            (live_in, live_ref),
            (lens_in, lens_ref),
        )[k]
        return pltpu.make_async_copy(src, dst, in_s.at[k])

    barrier = pltpu.get_barrier_semaphore()
    for i in range(ndp):
        for j in range(ntp):
            if i or j:
                pl.semaphore_signal(
                    barrier,
                    inc=1,
                    device_id=((d + i) % ndp, (t + j) % ntp),
                    device_id_type=MESH,
                )
    for k in (5, 6, 7, 8, 9, 0, 1, 2, 3, 4, 10, 11, 12):
        fetch(k).start()
    pl.semaphore_wait(barrier, ndp * ntp - 1)
    for k in (5, 6, 7, 8, 9, 10, 11, 12):
        fetch(k).wait()

    sent = []

    def send(src, dst, s, r, dev):
        cp = pltpu.make_async_remote_copy(
            src_ref=src, dst_ref=dst, send_sem=s, recv_sem=r, device_id=dev, device_id_type=MESH
        )
        return cp

    def dp_start(e, src, dst):
        for off in range(1, ndp):
            peer = (d + off) % ndp
            send(src(peer), dst.at[d], ds_s.at[e], ds_r.at[e], (peer, t)).start()
        whole = dst.at[pl.ds(0, ndp - 1)]
        sent.append(send(whole, whole, ds_s.at[e], ds_r.at[e], (d, (t + 1) % ntp)))

    def dp_wait(e, dst):
        whole = dst.at[pl.ds(0, ndp - 1)]
        send(whole, whole, ds_s.at[e], ds_r.at[e], (d, (t + 1) % ntp)).wait_recv()

    def tp_start(e, src, dst):
        for off in range(1, ntp):
            peer = (t + off) % ntp
            send(src, dst.at[t], ts_s.at[e], ts_r.at[e], (d, peer)).start()
        whole = dst.at[pl.ds(0, ntp - 1)]
        sent.append(send(whole, whole, ts_s.at[e], ts_r.at[e], (d, (t + 1) % ntp)))

    def tp_wait(e, dst):
        whole = dst.at[pl.ds(0, ntp - 1)]
        send(whole, whole, ts_s.at[e], ts_r.at[e], (d, (t + 1) % ntp)).wait_recv()

    for i in range(ndp):
        hsend[i] = h_ref[:, i * width : (i + 1) * width]
    lane = lax.broadcasted_iota(jnp.int32, (1, 128), 1)
    ones = [jnp.where(lane == idx_ref[r], 1.0, 0.0) for r in range(rolls)]
    stats_ref[...] = jnp.zeros_like(stats_ref)
    for r in range(rolls):
        stats_ref[0:1] += ones[r] * rew_ref[r]
        stats_ref[1:2] += ones[r] * (rew_ref[r] * rew_ref[r])

    dp_start(0, lambda p: hsend.at[p], hbuf)
    hbuf[d] = hsend[d]
    abuf[y, z, 0] = a_ref[...]
    abuf[y, z, 1] = b_ref[...]
    for k, ref in enumerate((a_ref, b_ref)):
        for off in range(1, nz):
            peer = 2 * ((z + off) % nz) + y
            send(ref, abuf.at[y, z, k], ab_s.at[0], ab_r.at[0], (peer, t)).start()
    others = abuf.at[0, pl.ds(0, nz - 1)]
    sent.append(send(others, others, ab_s.at[0], ab_r.at[0], (other_y, t)))
    dp_start(1, lambda p: stats_ref, statbuf)
    statbuf[d] = stats_ref[...]
    per = width // piece
    half = ndp // per
    src_t = d // half

    def up_block(tj):
        return send(bdbuf, bdbuf, bd_s, bd_r, (d, tj))

    fetch(0).wait()
    fetch(1).wait()
    xcp = send(x_ref, xbuf.at[y, c], xs_s.at[0], xs_r.at[0], (d, mate))
    xcp.start()
    sent.append(xcp)
    xbuf[y, c] = x_ref[...]

    def row_send(k):
        part = rows // ROW_PARTS
        if k >= ROW_PARTS:
            return
        seg = pl.ds(k * part, part)
        send(
            x_ref.at[seg], xbuf.at[y, c, seg], xs_s.at[1], xs_r.at[1], (other_y, t)
        ).start()

    def rows_whole():
        return send(x_ref, xbuf.at[1 - y, c], xs_s.at[1], xs_r.at[1], (other_y, t))

    def relay(dst_core):
        return send(
            xbuf.at[1 - y, c], xbuf.at[1 - y, dst_core], xs_s.at[2], xs_r.at[2], (d, mate)
        )

    feats = wo_ref.shape[0]
    pieces = chunks * SEGS
    near, far = z // 2, 1 - z // 2
    end = jnp.logical_or(z == 0, z == nz - 1)
    role_m = jnp.logical_and(jnp.logical_not(end), c == z // 2)
    role_2 = jnp.logical_and(jnp.logical_not(end), c != z // 2)
    lead = jnp.where(c == near, far, near)
    trail = 1 - lead
    z_up, z_dn = jnp.minimum(z + 1, nz - 1), jnp.maximum(z - 1, 0)
    z_in = jnp.where(z < 2, z_up, z_dn)
    z_out = jnp.where(z < 2, z_dn, z_up)

    cuts = [(ch, 0, CHUNK) for ch in range(chunks - 1)]
    cuts += [(chunks - 1, h * 128, 128) for h in range(CHUNK // 128)]

    def seg_of(k):
        ch, part = k // SEGS, k % SEGS
        if ch < chunks - 1:
            size = feats // SEGS
            return ch, pl.ds(part * size, size), 0, CHUNK
        halves = CHUNK // 128
        size = feats * halves // SEGS
        per_half = SEGS // halves
        return ch, pl.ds((part % per_half) * size, size), (part // per_half) * 128, 128

    def own(k, which, zt):
        ch, seg, off, num = seg_of(k)
        return send(
            wo_ref.at[seg, pl.ds(ch * CHUNK + off, num)],
            wbuf.at[z // 2, c, ch, seg, pl.ds(off, num)],
            wl_s.at[which],
            wl_r.at[z // 2, c, k],
            (2 * zt + y, 2 * x + z % 2),
        )

    def hop(blk, j, which, zt):
        k, cc = j // 2, j % 2
        ch, seg, off, num = seg_of(k)
        ref = wbuf.at[blk, cc, ch, seg, pl.ds(off, num)]
        return send(ref, ref, wl_s.at[which], wl_r.at[blk, cc, k], (2 * zt + y, t))

    def own_tick(k):
        @pl.when(z < nz - 1)
        def _():
            own(k, 0, z_up).start()

        @pl.when(z > 0)
        def _():
            own(k, 1, z_dn).start()

        @pl.when(z % 2 != c)
        def _():
            own(k, 2, z).start()

    waited = {"near": 0, "far_m": 0, "far_2": 0}

    def arrive(name, blk, upto):
        for j in range(waited[name], upto):
            hop(blk, j, 3, z_in).wait_recv()
        waited[name] = max(waited[name], upto)

    def relay_tick(name, blk, lo, hi, which, zt):
        hi = min(hi, 2 * pieces)
        arrive(name, blk, hi)
        for j in range(lo, hi):
            hop(blk, j, which, zt).start()

    clock = [0]
    ticks = 3 * pieces

    def tick():
        n = clock[0]
        if n >= ticks:
            return
        clock[0] += 1
        if n < pieces:
            own_tick(n)
            row_send(n)
            return
        m = n - pieces

        @pl.when(role_m)
        def _():
            if m < pieces:
                relay_tick("near", near, 2 * m, 2 * m + 2, 3, z_in)
                relay_tick("far_m", far, 2 * m, 2 * m + 2, 4, z_out)

        if m >= pieces:

            @pl.when(role_2)
            def _():
                relay_tick("far_2", far, 2 * (m - pieces), 2 * (m - pieces) + 2, 4, z_out)

    def pump(n):
        for _ in range(n):
            tick()

    pump(2)

    @pl.when(z % 2 == c)
    def _():
        for ch in range(chunks):
            wbuf[z // 2, c, ch] = wo_ref[:, ch * CHUNK : (ch + 1) * CHUNK]

    def q_side(step):
        return send(qsend.at[step, 1 - y], qside.at[step], qy_s.at[step], qy_r.at[step], (other_y, t))

    def q_lines(step):
        whole = qrecv.at[step, pl.ds(0, nz - 1)]
        return send(whole, whole, qz_s.at[step], qz_r.at[step], (other_y, t))

    def a_side(step, yy):
        ref = arecv.at[step, yy]
        return send(ref, ref, ay_s.at[step], ay_r.at[step], (other_y, t))

    def a_lines(step):
        whole = arecv.at[step, 0, pl.ds(0, nz - 1)]
        return send(whole, whole, az_s.at[step], az_r.at[step], (other_y, t))

    def ab_side(yy):
        return send(abuf.at[yy], abuf.at[yy], ab_s.at[1], ab_r.at[1], (other_y, t))

    def lb_core():
        return send(lbsend.at[1 - c], lbhalf.at[2], lb_s.at[0], lb_r.at[0], (d, mate))

    def lb_chip():
        return send(lbhalf.at[0], lbhalf.at[1], lb_s.at[1], lb_r.at[1], (d, 2 * (1 - x) + c))

    def lb_back(core):
        return send(lbfull.at[core], lbfull.at[core], lb_s.at[2], lb_r.at[2], (d, mate))

    def g_side():
        return send(gsend.at[1 - y], grecv, gy_s, gy_r, (other_y, t))

    def g_own(i):
        return gown[y, i] + grecv[i].astype(F32)

    def g_up(zz):
        part = pl.ds(zz + 1, nz - 1 - zz)
        return send(gus.at[part], gur.at[part], gu_s, gu_r, (2 * (zz + 1) + y, t))

    def g_down(zz):
        part = pl.ds(0, zz)
        return send(gds.at[part], gdr.at[part], gd_s, gd_r, (2 * (zz - 1) + y, t))

    def g_step(ph):
        @pl.when(z == ph)
        def _():
            if ph:
                g_up(ph - 1).wait_recv()
            for i in range(ph + 1, nz):
                gus[i] = (g_own(i) + gur[i].astype(F32) if ph else g_own(i)).astype(BF16)
            g_up(ph).start()

        top = nz - 1 - ph

        @pl.when(z == top)
        def _():
            if ph:
                g_down(top + 1).wait_recv()
            for i in range(top):
                gds[i] = (g_own(i) + gdr[i].astype(F32) if ph else g_own(i)).astype(BF16)
            g_down(top).start()

    def share(dx, dy, u):
        zz = jnp.where(dx == 1, 1 - x, x)
        yy = jnp.where(dy == 1, 1 - y, y)
        ch, off, num = cuts[u]
        cols = pl.ds(off, num)
        return send(
            pbuf.at[2 * dx + dy, ch, :, cols],
            prcv.at[2 * dx + dy, ch, :, cols],
            ps_s,
            ps_r.at[u],
            (2 * z + yy, 2 * zz + c),
        )

    def rows_in():
        rows_whole().wait_recv()
        relay(c).start()

    def rows_ready():
        send(x_ref, xbuf.at[y, 1 - c], xs_s.at[0], xs_r.at[0], (d, mate)).wait_recv()
        relay(1 - c).wait_recv()

    def columns(yy, u):
        ch, off, num = cuts[u]
        return pl.ds(pl.multiple_of((yy * chunks + ch) * CHUNK + off, 128), num)

    def final(k):
        src, dst = ((dec_ref, dec_out), (ga_ref, ga_out), (gb_ref, gb_out))[k]
        return pltpu.make_async_copy(src, dst, fin_s.at[k])

    def emit(dy, u):
        cols = columns((y + dy) % 2, u)
        return pltpu.make_async_copy(out_ref.at[:, cols], rows_out.at[:, cols], out_s)

    def unit(blk, u):
        ch, off, num = cuts[u]
        cols = pl.ds(off, num)
        own_ks = [k for k in range(pieces) if seg_of(k)[0] == ch and seg_of(k)[2] == off]
        upto = 2 * (max(own_ks) + 1)
        leads = blk is lead

        @pl.when(role_m)
        def _():
            arrive("far_m" if leads else "near", blk, upto)

        if not leads:

            @pl.when(role_2)
            def _():
                arrive("far_2", blk, upto)

        others = jnp.logical_not(role_m) if leads else end
        parts = [(k, cc) for k in own_ks for cc in range(2)]

        def landed(todo):
            for cc in range(2):
                mine = jnp.logical_and(c + 2 * blk == z, c == cc)
                ks = [k for k, core in todo if core == cc]

                if ks:

                    @pl.when(jnp.logical_and(others, jnp.logical_not(mine)))
                    def _():
                        for k in ks:
                            hop(blk, 2 * k + cc, 3, z_in).wait_recv()

        dx = jnp.where(blk == x, 0, 1)

        def put(dy, p):
            if dy == 1:
                pbuf[2 * dx + 1, ch, :, cols] = p.astype(BF16)
                share(dx, 1, u).start()
            else:

                @pl.when(dx == 1)
                def _():
                    pbuf[2, ch, :, cols] = p.astype(BF16)
                    share(1, 0, u).start()

                @pl.when(dx == 0)
                def _():
                    out_ref[:, columns(y, u)] += p

        if leads or u < len(cuts) - 1:
            landed(parts)
            for dy in (1, 0):
                yy = (y + dy) % 2
                p = jnp.dot(xbuf[yy, 0], wbuf[blk, 0, ch, :, cols], preferred_element_type=F32)
                p = p + jnp.dot(xbuf[yy, 1], wbuf[blk, 1, ch, :, cols], preferred_element_type=F32)
                put(dy, p)
            return
        for i, (k, cc) in enumerate(parts):
            landed([(k, cc)])
            seg = seg_of(k)[1]
            for dy in (1, 0):
                yy = (y + dy) % 2
                p = jnp.dot(
                    xbuf[yy, cc, :, seg], wbuf[blk, cc, ch, seg, cols], preferred_element_type=F32
                )
                if i:
                    p = p + acc[dy]
                if i < len(parts) - 1:
                    acc[dy] = p
                else:
                    put(dy, p)

    dp_wait(0, hbuf)
    state = jnp.concatenate([hbuf[i].astype(F32) for i in range(ndp)], axis=0)
    gains = gain_ref[...].astype(F32)
    line = lax.broadcasted_iota(jnp.int32, gains.shape, 0)
    gain = jnp.concatenate(
        [
            jnp.sum(jnp.where(line == d * (width // 128) + i, gains, 0.0), axis=0, keepdims=True)
            for i in range(width // 128)
        ],
        axis=1,
    )
    fetch(2).wait()
    new_k, new_v = [], []
    factor = 1.0 / math.sqrt(HD)

    for step in range(2):
        squares = jnp.sum(state * state, axis=-1, keepdims=True)
        part = exact_dot(state * gain, wqkv_ref[...])
        both = jnp.concatenate([part, jnp.broadcast_to(squares, (ndp * rolls, 128))], axis=1)
        for i in range(ndp):
            qsend[step, i % 2, i // 2] = both[i * rolls : (i + 1) * rolls]
        q_side(step).start()
        pump(1)
        if step == 1:
            lb_chip().wait_recv()
            lbfull[c] = (lbhalf[0] + lbhalf[1]).astype(BF16)
            lb_back(c).start()
        if step == 0:
            send(others, others, ab_s.at[0], ab_r.at[0], (other_y, t)).wait_recv()
            ab_side(y).start()
            dp_wait(1, statbuf)
            tot = statbuf[0]
            for i in range(1, ndp):
                tot = tot + statbuf[i]
            mean = tot[0:1] / GROUP
            std = jnp.sqrt(jnp.maximum(tot[1:2] / GROUP - mean * mean, 0.09))
            fetch(4).wait()
            for r in range(rolls):
                one, rew = ones[r], rew_ref[r]
                live = live_ref[r].astype(F32)
                adv = (rew - jnp.sum(one * mean, axis=1, keepdims=True)) / jnp.sum(
                    one * std, axis=1, keepdims=True
                )
                slot = lax.broadcasted_iota(jnp.int32, (COMP, 1), 0).astype(F32)
                row_w = jnp.where(slot < live, adv / live, 0.0)
                seg = pl.ds(r * COMP, COMP)
                wt_ref[seg, :] = (row_w * up_ref[seg, :].astype(F32)).astype(BF16)
        q_side(step).wait_recv()
        for i in range(nz):
            qline[step, i] = qsend[step, y, i] + qside[step, i]
        for off in range(1, nz):
            zt = (z + off) % nz
            src, dst = qline.at[step, zt], qrecv.at[step, z]
            send(src, dst, qz_s.at[step], qz_r.at[step], (2 * zt + y, t)).start()
        pump(2)
        q_lines(step).wait_recv()
        total = qline[step, z]
        for off in range(1, nz):
            total = total + qrecv[step, (z + off) % nz]
        qkv = total[:, :qkvw] * lax.rsqrt(total[:, qkvw : qkvw + 1] / model + 1e-05)
        new_k.append(qkv[:, HEADS_TP * HD : HEADS_TP * HD + HD])
        new_v.append(qkv[:, HEADS_TP * HD + HD :])
        if step == 0:
            fetch(3).wait()
        heads = []
        for b in range(rolls):
            q = jnp.concatenate(
                [qkv[b : b + 1, h * HD : (h + 1) * HD] for h in range(HEADS_TP)], axis=0
            )
            scores = exact_dot(q, cache_ref[b, :, :HD], NT) * factor
            pos = lax.broadcasted_iota(jnp.int32, scores.shape, 1)
            scores = jnp.where(pos < lens_ref[b], scores, -1e30)
            extra = [
                jnp.sum(q * k[b : b + 1], axis=-1, keepdims=True) * factor for k in new_k
            ]
            top = jnp.max(scores, axis=-1, keepdims=True)
            for e in extra:
                top = jnp.maximum(top, e)
            expo = jnp.exp(scores - top)
            ee = [jnp.exp(e - top) for e in extra]
            den = jnp.sum(expo, axis=-1, keepdims=True)
            for e in ee:
                den = den + e
            att = jnp.dot(
                (expo / den).astype(BF16), cache_ref[b, :, HD:], preferred_element_type=F32
            )
            for e, v in zip(ee, new_v):
                att = att + (e / den).astype(BF16).astype(F32) * v[b : b + 1]
            heads.append(jnp.concatenate([att[h : h + 1] for h in range(HEADS_TP)], axis=1))
        asend[step] = jnp.concatenate(heads, axis=0).astype(BF16)
        for off in range(1, nz):
            zt = (z + off) % nz
            send(
                asend.at[step], arecv.at[step, y, z], az_s.at[step], az_r.at[step], (2 * zt + y, t)
            ).start()
        pump(1)
        arecv[step, y, z] = asend[step]
        if step == 0:
            ab_side(1 - y).wait_recv()
            at, bt = (
                jnp.concatenate([abuf[i % 2, i // 2, k] for i in range(ndp)], axis=1)
                for k in range(2)
            )

            @pl.when(t == src_t)
            def _():
                for j in range(per):
                    bdbuf[j] = abuf[j % 2, (d % half) * (per // 2) + j // 2, 1]
                for off in range(1, ntp):
                    up_block((t + off) % ntp).start()

            for k, (m, v) in enumerate(((at, x_ref), (bt, wt_ref))):
                lb = lax.dot_general(m, v[...], NT, preferred_element_type=F32)
                for i in range(2):
                    lbsend[i, k] = lb[:, i * (rows // 2) : (i + 1) * (rows // 2)]
            lb_core().start()
        else:
            lb_back(c).wait_send()
            lb_back(1 - c).wait_recv()
            low_t, back_t = lanes_of(lbfull.at[:, 0], 2), lanes_of(lbfull.at[:, 1], 2)
            ga = adapter_scale * jnp.dot(back_t, x_ref[...], preferred_element_type=F32)
            gb = adapter_scale * jnp.dot(low_t, wt_ref[...], preferred_element_type=F32)
            for i in range(ndp):
                for k, g in enumerate((ga, gb)):
                    part = g[:, i * piece : (i + 1) * piece]
                    gown[i % 2, i // 2, k] = part
                    gsend[i % 2, i // 2, k] = part.astype(BF16)
            g_side().start()
            out_ref[...] = adapter_scale * lax.dot_general(
                low_t, bt, TN, preferred_element_type=F32
            )
        a_lines(step).wait_recv()
        a_side(step, y).start()
        pump(1)
        a_side(step, 1 - y).wait_recv()
        attended = jnp.concatenate(
            [arecv[step, i % 2, i // 2].astype(F32) for i in range(ndp)], axis=0
        ).astype(BF16)
        usend[step, :, :width] = jnp.dot(attended, wo_ref[...], preferred_element_type=F32)
        usend[step, :, width:] = jnp.concatenate(
            [
                lax.dot_general(attended, at, NT, preferred_element_type=F32),
                jnp.zeros((ndp * rolls, 128 - rank), F32),
            ],
            axis=1,
        )
        tp_start(step, usend.at[step], urecv.at[step])
        pump(2)
        urecv[step, t] = usend[step]
        if step == 0:
            lb_core().wait_recv()
            lbhalf[0] = lbsend[c] + lbhalf[2]
            lb_chip().start()

            @pl.when(t != src_t)
            def _():
                up_block(src_t).wait_recv()

            bd = lanes_of(bdbuf, per)
        tp_wait(step, urecv.at[step])
        upd = urecv[step, 0]
        for i in range(1, ntp):
            upd = upd + urecv[step, i]
        state = state + (
            upd[:, :width] + adapter_scale * exact_dot(upd[:, width : width + rank], bd)
        )

    for i in range(ndp):
        fsend[i] = state[i * rolls : (i + 1) * rolls]
    dp_start(2, lambda p: fsend.at[p], frecv)
    frecv[d] = fsend[d]
    rows_in()
    g_side().wait_recv()
    g_step(0)
    pump(2)
    rows_ready()
    for u in range(len(cuts)):
        unit(lead, u)
        if 0 < u < nz - 1:
            g_step(u)
        pump(2)
    dp_wait(2, frecv)
    for i in range(ndp):
        dec_ref[:, i * width : (i + 1) * width] = frecv[i]
    final(0).start()
    for cp in sent:
        cp.wait_send()
    while clock[0] < 2 * pieces + pieces // 2:
        pump(1)
    unit(trail, 0)
    pump(ticks)
    unit(trail, 1)
    for u in range(2, len(cuts)):
        unit(trail, u)
    for u in range(len(cuts)):
        ch, off, num = cuts[u]
        three = prcv.at[pl.ds(1, 3), ch, :, pl.ds(off, num)]
        send(three, three, ps_s, ps_r.at[u], (d, mate)).wait_recv()
        for dx, dy in ((1, 0), (0, 1), (1, 1)):
            got = prcv[2 * dx + dy, ch, :, pl.ds(off, num)].astype(F32)
            out_ref[:, columns((y + dy) % 2, u)] += got
        for dy in range(2):
            emit(dy, u).start()

    @pl.when(z == 0)
    def _():
        g_down(1).wait_recv()
        gur[0] = jnp.zeros_like(gur[0])

    @pl.when(z == nz - 1)
    def _():
        g_up(nz - 2).wait_recv()
        gdr[nz - 1] = jnp.zeros_like(gdr[0])

    g = g_own(z) + gur[z].astype(F32) + gdr[z].astype(F32)
    ga_ref[...] = g[0]
    gb_ref[...] = g[1]
    final(1).start()
    final(2).start()
    pltpu.make_async_copy(out_ref, rows_out, out_s).wait()
    for k in range(3):
        final(k).wait()

    def drain(which, full):
        send(full, full, wl_s.at[which], wl_r.at[0, 0, 0], (d, mate)).wait_send()

    @pl.when(z < nz - 1)
    def _():
        drain(0, wbuf.at[0, 0])

    @pl.when(z > 0)
    def _():
        drain(1, wbuf.at[0, 0])

    @pl.when(z % 2 != c)
    def _():
        drain(2, wbuf.at[0, 0])

    @pl.when(role_m)
    def _():
        drain(3, wbuf.at[0])

    @pl.when(jnp.logical_not(end))
    def _():
        drain(4, wbuf.at[0])

    three = pbuf.at[pl.ds(1, 3)]
    send(three, three, ps_s, ps_r.at[0], (d, mate)).wait_send()
    rows_whole().wait_send()
    relay(c).wait_send()
    g_side().wait_send()
    for step in range(2):
        q_side(step).wait_send()
        q_lines(step).wait_send()
        a_side(step, y).wait_send()
        a_lines(step).wait_send()
    lb_core().wait_send()
    lb_chip().wait_send()
    ab_side(y).wait_send()
    for zz in range(nz):

        @pl.when(z == zz)
        def _():
            if zz < nz - 1:
                g_up(zz).wait_send()
            if zz:
                g_down(zz).wait_send()


    @pl.when(t == src_t)
    def _():
        copies = wo_ref.at[pl.ds(0, (ntp - 1) * rank)]
        send(copies, copies, bd_s, bd_r, (d, mate)).wait_send()


def finish_kernel(*refs):
    n = len(refs) // 2
    copies = [pltpu.make_async_copy(refs[i], refs[n + i], refs[-1].at[i]) for i in range(n)]
    for cp in copies:
        cp.start()
    for cp in copies:
        cp.wait()


def fused_shards(
    ndp,
    ntp,
    hidden,
    attention_norm_gain,
    query_key_value_weight,
    key_value_cache,
    cache_fill_lengths,
    output_weight_frozen,
    adapter_down_transposed,
    adapter_up_matrix,
    attention_rows,
    upstream,
    rewards,
    prompt_group_index,
    completion_live_lengths,
):
    rolls, model = hidden.shape
    slots = key_value_cache.shape[1]
    width = model // ndp
    rank, _, piece = adapter_down_transposed.shape
    rows, shard = attention_rows.shape
    qkvw = query_key_value_weight.shape[2]
    feats = output_weight_frozen.shape[1]
    chunks = width // CHUNK
    vm = pl.BlockSpec(memory_space=pltpu.VMEM)
    hbm = pl.BlockSpec(memory_space=pltpu.HBM)
    dma = pltpu.SemaphoreType.DMA
    V = pltpu.VMEM
    dec, out, ga, gb = pl.pallas_call(
        lambda *refs: fused_kernel(ndp, ntp, *refs),
        out_shape=(
            pltpu.VMEM((rolls, model), F32),
            pltpu.VMEM((rows, shard), F32),
            pltpu.VMEM((rank, piece), F32),
            pltpu.VMEM((rank, piece), F32),
        ),
        in_specs=[hbm] * 13,
        out_specs=(pl.BlockSpec(memory_space=pl.ANY),) * 4,
        scratch_shapes=[
            V((ndp, rolls, width), BF16),
            V((2, 128), F32),
            V((ndp, rolls, width), BF16),
            V((2, ndp // 2, 2, rank, piece), BF16),
            V((width // piece, rank, piece), BF16),
            V((ndp, 2, 128), F32),
            V((2, 2, ndp // 2, rolls, qkvw + 128), F32),
            V((2, ndp // 2, rolls, qkvw + 128), F32),
            V((2, ndp // 2, rolls, qkvw + 128), F32),
            V((2, ndp // 2, rolls, qkvw + 128), F32),
            V((2, rolls, feats), BF16),
            V((2, 2, ndp // 2, rolls, feats), BF16),
            V((2, ndp * rolls, width + 128), F32),
            V((2, ntp, ndp * rolls, width + 128), F32),
            V((ndp, rolls, width), F32),
            V((ndp, rolls, width), F32),
            V((2, 2, rank, rows // 2), F32),
            V((3, 2, rank, rows // 2), F32),
            V((2, 2, rank, rows // 2), BF16),
            V((2, ndp // 2, 2, rank, piece), F32),
            V((2, ndp // 2, 2, rank, piece), BF16),
            V((ndp // 2, 2, rank, piece), BF16),
            V((ndp // 2, 2, rank, piece), BF16),
            V((ndp // 2, 2, rank, piece), BF16),
            V((ndp // 2, 2, rank, piece), BF16),
            V((ndp // 2, 2, rank, piece), BF16),
            V((rows, shard), BF16),
            V((2, 2, rows, shard), BF16),
            V((2, 2, chunks, feats, CHUNK), BF16),
            V((4, chunks, rows, CHUNK), BF16),
            V((4, chunks, rows, CHUNK), BF16),
            dma((3,)),
            dma((3,)),
            dma((2,)),
            dma((2,)),
            dma,
            dma,
            dma((3,)),
            dma((3,)),
            dma((5,)),
            dma((2, 2, chunks * SEGS)),
            dma,
            dma((chunks - 1 + CHUNK // 128,)),
            dma,
            dma,
            dma,
            dma,
            dma,
            dma,
            dma((3,)),
            dma((3,)),
            dma((2,)),
            dma((2,)),
            V((feats, width), BF16),
            V((rows, shard), BF16),
            V((width, qkvw), BF16),
            V((rolls, slots, 2 * HD), BF16),
            V((rows, shard), BF16),
            dma((13,)),
            V((rows, shard), F32),
            V((rolls, model), F32),
            V((rank, piece), F32),
            V((rank, piece), F32),
            dma,
            dma((3,)),
            V((2, rows, 128), F32),
        ]
        + [dma((2,))] * 8
        + [V((rolls, model), BF16), V((model // 128, 128), BF16)]
        + [V((rank, piece), BF16)] * 2
        + [pltpu.SMEM((rolls,), t) for t in (jnp.int32, F32, jnp.int32, jnp.int32)],
        compiler_params=pltpu.CompilerParams(
            collective_id=0, has_side_effects=True, vmem_limit_bytes=64815104
        ),
    )(
        hidden,
        attention_norm_gain.reshape(model // 128, 128),
        query_key_value_weight[:, 0, :],
        key_value_cache[:, :, 0, :],
        cache_fill_lengths,
        output_weight_frozen[0],
        adapter_down_transposed[:, 0, :],
        adapter_up_matrix[:, 0, :],
        attention_rows,
        upstream,
        rewards,
        prompt_group_index,
        completion_live_lengths,
    )
    parts = (dec, out, ga[:, None, :], gb[:, None, :])
    anywhere = (pl.BlockSpec(memory_space=pl.ANY),) * len(parts)
    return pl.pallas_call(
        finish_kernel,
        out_shape=tuple(jax.ShapeDtypeStruct(p.shape, F32) for p in parts),
        in_specs=[vm] * len(parts),
        out_specs=anywhere,
        scratch_shapes=[dma((len(parts),))],
        compiler_params=pltpu.CompilerParams(vmem_limit_bytes=2**20),
    )(*[pltpu.with_memory_space_constraint(p, pltpu.VMEM) for p in parts])


def shards(
    hidden,
    attention_norm_gain,
    query_key_value_weight,
    key_value_cache,
    cache_fill_lengths,
    output_weight_frozen,
    adapter_down_transposed,
    adapter_up_matrix,
    attention_rows,
    upstream,
    rewards,
    prompt_group_index,
    completion_live_lengths,
):
    a_piece, b_piece = (
        lax.all_gather(adapter_down_transposed, "dp", axis=2, tiled=True),
        lax.all_gather(adapter_up_matrix, "dp", axis=2, tiled=True),
    )
    b_whole = lax.all_gather(b_piece, "tp", axis=1, tiled=True)
    up_matrix_flat = b_whole.reshape(b_whole.shape[0], -1).astype(jnp.float32)
    a_local = a_piece[:, 0, :]
    up_matrix_columns = b_piece[:, 0, :]
    w_rows = query_key_value_weight[:, 0, :].astype(jnp.float32)
    w_cols = output_weight_frozen[0]
    query_width = HEADS_TP * HD
    local_rolls = hidden.shape[0]
    decode_state = hidden.astype(jnp.float32)
    keys_new = []
    values_new = []
    for step in range(2):
        normed = rms_norm(decode_state, attention_norm_gain)
        spread = lax.all_to_all(normed, "dp", split_axis=1, concat_axis=0, tiled=True)
        partial_value = jnp.dot(spread, w_rows, precision=lax.Precision.HIGHEST)
        qkv = lax.psum_scatter(partial_value, "dp", scatter_dimension=0, tiled=True)
        query = qkv[:, :query_width].reshape(local_rolls, HEADS_TP, HD)
        keys_new.append(qkv[:, query_width : query_width + HD])
        values_new.append(qkv[:, query_width + HD :])
        attended = attend(
            query,
            key_value_cache[:, :, 0, :],
            cache_fill_lengths,
            jnp.stack(keys_new, axis=1),
            jnp.stack(values_new, axis=1),
        )
        columns = jnp.dot(
            lax.all_gather(attended, "dp", axis=0, tiled=True),
            w_cols,
            preferred_element_type=jnp.float32,
        )
        returned_values = lax.all_to_all(columns, "dp", split_axis=0, concat_axis=1, tiled=True)
        low_rank_decode = jnp.dot(attended, a_local.T, preferred_element_type=jnp.float32)
        state_update = returned_values + adapter_scale * jnp.dot(
            low_rank_decode, up_matrix_flat, precision=lax.Precision.HIGHEST
        )
        decode_state = decode_state + lax.psum(state_update, "tp")
    groups = local_rolls * lax.axis_size("dp") // GROUP
    onehot = (prompt_group_index[:, None] == jnp.arange(groups, dtype=jnp.int32)[None, :]).astype(
        jnp.float32
    )
    totals, squares = lax.psum(
        (
            jnp.sum(onehot * rewards[:, None], axis=0),
            jnp.sum(onehot * (rewards * rewards)[:, None], axis=0),
        ),
        "dp",
    )
    mean = totals / GROUP
    std = jnp.sqrt(jnp.maximum(squares / GROUP - mean * mean, 0.09))
    advantage = (rewards - jnp.sum(onehot * mean[None, :], axis=1)) / jnp.sum(
        onehot * std[None, :], axis=1
    )
    per_roll = advantage / completion_live_lengths.astype(jnp.float32)
    rows = attention_rows.shape[0]
    slot = jnp.arange(rows, dtype=jnp.int32) % COMP
    limit = jnp.repeat(completion_live_lengths, COMP)
    row_w = jnp.where(slot < limit, jnp.repeat(per_roll, COMP), 0.0)
    whole_rows = jnp.dot(
        attention_rows,
        lax.all_gather(output_weight_frozen, "dp", axis=2, tiled=True)[0],
        preferred_element_type=jnp.float32,
    )
    frozen_output_rows = lax.psum_scatter(whole_rows, "tp", scatter_dimension=1, tiled=True)
    low_sum = lax.psum(jnp.dot(attention_rows, a_local.T, preferred_element_type=jnp.float32), "tp")
    low_rank_rows = low_sum.astype(jnp.bfloat16)
    adapted_output_rows = frozen_output_rows + adapter_scale * jnp.dot(
        low_rank_rows, up_matrix_columns, preferred_element_type=jnp.float32
    )
    advantage_weighted = (row_w[:, None] * upstream.astype(jnp.float32)).astype(jnp.bfloat16)
    backward_result = lax.psum(
        jnp.dot(advantage_weighted, up_matrix_columns.T, preferred_element_type=jnp.float32), "tp"
    ).astype(jnp.bfloat16)
    down_gradient = adapter_scale * lax.dot_general(
        backward_result,
        attention_rows,
        (((0,), (0,)), ((), ())),
        preferred_element_type=jnp.float32,
    )
    up_gradient = adapter_scale * lax.dot_general(
        low_rank_rows,
        advantage_weighted,
        (((0,), (0,)), ((), ())),
        preferred_element_type=jnp.float32,
    )
    grad_a_part, grad_b_part = (
        lax.psum_scatter(down_gradient[:, None, :], "dp", scatter_dimension=2, tiled=True),
        lax.psum_scatter(up_gradient[:, None, :], "dp", scatter_dimension=2, tiled=True),
    )
    return (decode_state, adapted_output_rows, grad_a_part, grad_b_part)


def solution(mesh):
    placed = (
        P("dp", None),
        P(),
        P("dp", "tp", None),
        P("dp", None, "tp", None),
        P("dp"),
        P("tp", None, "dp"),
        P(None, "tp", "dp"),
        P(None, "tp", "dp"),
        P("dp", "tp"),
        P("dp", "tp"),
        P("dp"),
        P("dp"),
        P("dp"),
    )
    ndp, ntp = mesh.shape["dp"], mesh.shape["tp"]

    def body(*args):
        width = args[5].shape[2]
        piece = args[6].shape[2]
        if ntp == 4 and ndp == 8 and piece % 128 == 0 and width % CHUNK == 0:
            return fused_shards(ndp, ntp, *args)
        return shards(*args)

    return jax.shard_map(
        body,
        mesh=mesh,
        in_specs=placed,
        out_specs=(P("dp", None), P("dp", "tp"), P(None, "tp", "dp"), P(None, "tp", "dp")),
        check_vma=False,
    )
```

```python
import math

import jax
import jax.numpy as jnp
from jax import lax
from jax.experimental import pallas as pl
from jax.experimental.pallas import tpu as pltpu
from jax.sharding import PartitionSpec as P

HD = 128
HEADS_TP = 8
GROUP = 4
COMP = 256


adapter_scale = 2.0


def rms_norm(decode_state, gain):
    scale = lax.rsqrt(jnp.mean(decode_state * decode_state, axis=-1, keepdims=True) + 1e-05)
    return decode_state * scale * gain.astype(jnp.float32)


def attend(query, cache, lengths, new_keys, new_values):
    head = query.shape[-1]
    slots = cache.shape[1]
    factor = 1.0 / math.sqrt(head)
    keys = cache[:, :, :head].astype(jnp.float32)
    values = cache[:, :, head:]
    scores = jnp.einsum("bhd,bcd->bhc", query, keys, precision=lax.Precision.HIGHEST) * factor
    valid = jnp.arange(slots, dtype=jnp.int32)[None, None, :] < lengths[:, None, None]
    scores = jnp.where(valid, scores, -1e30)
    extra = jnp.einsum("bhd,bed->bhe", query, new_keys, precision=lax.Precision.HIGHEST) * factor
    joined = jnp.concatenate([scores, extra], axis=-1)
    top = jnp.max(joined, axis=-1, keepdims=True)
    expo = jnp.exp(joined - top)
    probs = (expo / jnp.sum(expo, axis=-1, keepdims=True)).astype(jnp.bfloat16)
    out = jnp.einsum("bhc,bcd->bhd", probs[..., :slots], values, preferred_element_type=jnp.float32)
    out = out + jnp.einsum(
        "bhe,bed->bhd",
        probs[..., slots:].astype(jnp.float32),
        new_values,
        precision=lax.Precision.HIGHEST,
    )
    return out.astype(jnp.bfloat16).reshape(query.shape[0], -1)


MESH = pl.DeviceIdType.MESH
F32 = jnp.float32
BF16 = jnp.bfloat16
NT = (((1,), (1,)), ((), ()))
TN = (((0,), (0,)), ((), ()))
CHUNK = 256
SEGS = 4
ROW_PARTS = 8


def split3(v):
    hi = v.astype(BF16)
    rest = v - hi.astype(F32)
    mid = rest.astype(BF16)
    lo = (rest - mid.astype(F32)).astype(BF16)
    return jnp.concatenate([hi, mid, lo], axis=0)


def exact_dot(v, w, dims=(((1,), (0,)), ((), ()))):
    n = v.shape[0]
    r = lax.dot_general(split3(v), w, dims, preferred_element_type=F32)
    return r[:n] + r[n : 2 * n] + r[2 * n :]


def rows_of(ref, n):
    return jnp.concatenate([ref[i] for i in range(n)], axis=0)


def lanes_of(ref, n):
    return jnp.concatenate([ref[i] for i in range(n)], axis=1)


def fused_kernel(
    ndp,
    ntp,
    h_in,
    gain_in,
    wqkv_in,
    cache_in,
    lens_in,
    wo_in,
    a_in,
    b_in,
    x_in,
    up_in,
    rew_in,
    idx_in,
    live_in,
    dec_ref,
    out_ref,
    ga_ref,
    gb_ref,
    hsend,
    stats_ref,
    hbuf,
    abuf,
    bdbuf,
    statbuf,
    qsend,
    qside,
    qline,
    qrecv,
    asend,
    arecv,
    usend,
    urecv,
    fsend,
    frecv,
    lbsend,
    lbhalf,
    lbfull,
    gown,
    grecv,
    gus,
    gur,
    gds,
    gdr,
    wt_ref,
    xbuf,
    wbuf,
    pbuf,
    prcv,
    ds_s,
    ds_r,
    ts_s,
    ts_r,
    bd_s,
    bd_r,
    xs_s,
    xs_r,
    wl_s,
    wl_r,
    ps_s,
    ps_r,
    gy_s,
    gy_r,
    gu_s,
    gu_r,
    gd_s,
    gd_r,
    lb_s,
    lb_r,
    ab_s,
    ab_r,
    wo_ref,
    x_ref,
    wqkv_ref,
    cache_ref,
    up_ref,
    in_s,
    acc,
    qy_s,
    qy_r,
    qz_s,
    qz_r,
    ay_s,
    ay_r,
    az_s,
    az_r,
    h_ref,
    gain_ref,
    a_ref,
    b_ref,
    lens_ref,
    rew_ref,
    idx_ref,
    live_ref,
):
    d = lax.axis_index("dp")
    t = lax.axis_index("tp")
    z, y = d // 2, d % 2
    x, c = t // 2, t % 2
    nz = ndp // 2
    rolls, model = h_ref.shape
    width = model // ndp
    rank = a_ref.shape[0]
    piece = a_ref.shape[1]
    chunks = wo_ref.shape[1] // CHUNK
    qkvw = wqkv_ref.shape[1]
    rows = x_ref.shape[0]
    mate = 2 * x + (1 - c)
    other_y = 2 * z + (1 - y)

    def fetch(k):
        src, dst = (
            (wo_in, wo_ref),
            (x_in, x_ref),
            (wqkv_in, wqkv_ref),
            (cache_in, cache_ref),
            (up_in, up_ref),
            (h_in, h_ref),
            (a_in, a_ref),
            (b_in, b_ref),
            (idx_in, idx_ref),
            (rew_in, rew_ref),
            (gain_in, gain_ref),
            (live_in, live_ref),
            (lens_in, lens_ref),
        )[k]
        return pltpu.make_async_copy(src, dst, in_s.at[k])

    barrier = pltpu.get_barrier_semaphore()
    for i in range(ndp):
        for j in range(ntp):
            if i or j:
                pl.semaphore_signal(
                    barrier,
                    inc=1,
                    device_id=((d + i) % ndp, (t + j) % ntp),
                    device_id_type=MESH,
                )
    for k in (5, 6, 7, 8, 9, 0, 1, 2, 3, 4, 10, 11, 12):
        fetch(k).start()
    pl.semaphore_wait(barrier, ndp * ntp - 1)
    for k in (5, 6, 7, 8, 9, 10, 11, 12):
        fetch(k).wait()

    sent = []

    def send(src, dst, s, r, dev):
        cp = pltpu.make_async_remote_copy(
            src_ref=src, dst_ref=dst, send_sem=s, recv_sem=r, device_id=dev, device_id_type=MESH
        )
        return cp

    def dp_start(e, src, dst):
        for off in range(1, ndp):
            peer = (d + off) % ndp
            send(src(peer), dst.at[d], ds_s.at[e], ds_r.at[e], (peer, t)).start()
        whole = dst.at[pl.ds(0, ndp - 1)]
        sent.append(send(whole, whole, ds_s.at[e], ds_r.at[e], (d, (t + 1) % ntp)))

    def dp_wait(e, dst):
        whole = dst.at[pl.ds(0, ndp - 1)]
        send(whole, whole, ds_s.at[e], ds_r.at[e], (d, (t + 1) % ntp)).wait_recv()

    def tp_start(e, src, dst):
        for off in range(1, ntp):
            peer = (t + off) % ntp
            send(src, dst.at[t], ts_s.at[e], ts_r.at[e], (d, peer)).start()
        whole = dst.at[pl.ds(0, ntp - 1)]
        sent.append(send(whole, whole, ts_s.at[e], ts_r.at[e], (d, (t + 1) % ntp)))

    def tp_wait(e, dst):
        whole = dst.at[pl.ds(0, ntp - 1)]
        send(whole, whole, ts_s.at[e], ts_r.at[e], (d, (t + 1) % ntp)).wait_recv()

    for i in range(ndp):
        hsend[i] = h_ref[:, i * width : (i + 1) * width]
    lane = lax.broadcasted_iota(jnp.int32, (1, 128), 1)
    ones = [jnp.where(lane == idx_ref[r], 1.0, 0.0) for r in range(rolls)]
    stats_ref[...] = jnp.zeros_like(stats_ref)
    for r in range(rolls):
        stats_ref[0:1] += ones[r] * rew_ref[r]
        stats_ref[1:2] += ones[r] * (rew_ref[r] * rew_ref[r])

    dp_start(0, lambda p: hsend.at[p], hbuf)
    hbuf[d] = hsend[d]
    abuf[y, z, 0] = a_ref[...]
    abuf[y, z, 1] = b_ref[...]
    for k, ref in enumerate((a_ref, b_ref)):
        for off in range(1, nz):
            peer = 2 * ((z + off) % nz) + y
            send(ref, abuf.at[y, z, k], ab_s.at[0], ab_r.at[0], (peer, t)).start()
    others = abuf.at[0, pl.ds(0, nz - 1)]
    sent.append(send(others, others, ab_s.at[0], ab_r.at[0], (other_y, t)))
    dp_start(1, lambda p: stats_ref, statbuf)
    statbuf[d] = stats_ref[...]
    per = width // piece
    half = ndp // per
    src_t = d // half

    def up_block(tj):
        return send(bdbuf, bdbuf, bd_s, bd_r, (d, tj))

    fetch(0).wait()
    fetch(1).wait()
    xcp = send(x_ref, xbuf.at[y, c], xs_s.at[0], xs_r.at[0], (d, mate))
    xcp.start()
    sent.append(xcp)
    xbuf[y, c] = x_ref[...]

    def row_send(k):
        part = rows // ROW_PARTS
        if k >= ROW_PARTS:
            return
        seg = pl.ds(k * part, part)
        send(
            x_ref.at[seg], xbuf.at[y, c, seg], xs_s.at[1], xs_r.at[1], (other_y, t)
        ).start()

    def rows_whole():
        return send(x_ref, xbuf.at[1 - y, c], xs_s.at[1], xs_r.at[1], (other_y, t))

    def relay(dst_core):
        return send(
            xbuf.at[1 - y, c], xbuf.at[1 - y, dst_core], xs_s.at[2], xs_r.at[2], (d, mate)
        )

    feats = wo_ref.shape[0]
    pieces = chunks * SEGS
    near, far = z // 2, 1 - z // 2
    end = jnp.logical_or(z == 0, z == nz - 1)
    role_m = jnp.logical_and(jnp.logical_not(end), c == z // 2)
    role_2 = jnp.logical_and(jnp.logical_not(end), c != z // 2)
    lead = jnp.where(c == near, far, near)
    trail = 1 - lead
    z_up, z_dn = jnp.minimum(z + 1, nz - 1), jnp.maximum(z - 1, 0)
    z_in = jnp.where(z < 2, z_up, z_dn)
    z_out = jnp.where(z < 2, z_dn, z_up)

    cuts = [(ch, 0, CHUNK) for ch in range(chunks - 1)]
    cuts += [(chunks - 1, h * 128, 128) for h in range(CHUNK // 128)]

    def seg_of(k):
        ch, part = k // SEGS, k % SEGS
        if ch < chunks - 1:
            size = feats // SEGS
            return ch, pl.ds(part * size, size), 0, CHUNK
        halves = CHUNK // 128
        size = feats * halves // SEGS
        per_half = SEGS // halves
        return ch, pl.ds((part % per_half) * size, size), (part // per_half) * 128, 128

    def own(k, which, zt):
        ch, seg, off, num = seg_of(k)
        return send(
            wo_ref.at[seg, pl.ds(ch * CHUNK + off, num)],
            wbuf.at[z // 2, c, ch, seg, pl.ds(off, num)],
            wl_s.at[which],
            wl_r.at[z // 2, c, k],
            (2 * zt + y, 2 * x + z % 2),
        )

    def hop(blk, j, which, zt):
        k, cc = j // 2, j % 2
        ch, seg, off, num = seg_of(k)
        ref = wbuf.at[blk, cc, ch, seg, pl.ds(off, num)]
        return send(ref, ref, wl_s.at[which], wl_r.at[blk, cc, k], (2 * zt + y, t))

    def own_tick(k):
        @pl.when(z < nz - 1)
        def _():
            own(k, 0, z_up).start()

        @pl.when(z > 0)
        def _():
            own(k, 1, z_dn).start()

        @pl.when(z % 2 != c)
        def _():
            own(k, 2, z).start()

    waited = {"near": 0, "far_m": 0, "far_2": 0}

    def arrive(name, blk, upto):
        for j in range(waited[name], upto):
            hop(blk, j, 3, z_in).wait_recv()
        waited[name] = max(waited[name], upto)

    def relay_tick(name, blk, lo, hi, which, zt):
        hi = min(hi, 2 * pieces)
        arrive(name, blk, hi)
        for j in range(lo, hi):
            hop(blk, j, which, zt).start()

    clock = [0]
    ticks = 3 * pieces

    def tick():
        n = clock[0]
        if n >= ticks:
            return
        clock[0] += 1
        if n < pieces:
            own_tick(n)
            row_send(n)
            return
        m = n - pieces

        @pl.when(role_m)
        def _():
            if m < pieces:
                relay_tick("near", near, 2 * m, 2 * m + 2, 3, z_in)
                relay_tick("far_m", far, 2 * m, 2 * m + 2, 4, z_out)

        if m >= pieces:

            @pl.when(role_2)
            def _():
                relay_tick("far_2", far, 2 * (m - pieces), 2 * (m - pieces) + 2, 4, z_out)

    def pump(n):
        for _ in range(n):
            tick()

    pump(2)

    @pl.when(z % 2 == c)
    def _():
        for ch in range(chunks):
            wbuf[z // 2, c, ch] = wo_ref[:, ch * CHUNK : (ch + 1) * CHUNK]

    def q_side(step):
        return send(qsend.at[step, 1 - y], qside.at[step], qy_s.at[step], qy_r.at[step], (other_y, t))

    def q_lines(step):
        whole = qrecv.at[step, pl.ds(0, nz - 1)]
        return send(whole, whole, qz_s.at[step], qz_r.at[step], (other_y, t))

    def a_side(step, yy):
        ref = arecv.at[step, yy]
        return send(ref, ref, ay_s.at[step], ay_r.at[step], (other_y, t))

    def a_lines(step):
        whole = arecv.at[step, 0, pl.ds(0, nz - 1)]
        return send(whole, whole, az_s.at[step], az_r.at[step], (other_y, t))

    def ab_side(yy):
        return send(abuf.at[yy], abuf.at[yy], ab_s.at[1], ab_r.at[1], (other_y, t))

    def lb_core():
        return send(lbsend.at[1 - c], lbhalf.at[2], lb_s.at[0], lb_r.at[0], (d, mate))

    def lb_chip():
        return send(lbhalf.at[0], lbhalf.at[1], lb_s.at[1], lb_r.at[1], (d, 2 * (1 - x) + c))

    def lb_back(core):
        return send(lbfull.at[core], lbfull.at[core], lb_s.at[2], lb_r.at[2], (d, mate))

    def g_side():
        return send(gown.at[1 - y], grecv, gy_s, gy_r, (other_y, t))

    def g_own(i):
        return gown[y, i] + grecv[i]

    def g_up(zz):
        part = pl.ds(zz + 1, nz - 1 - zz)
        return send(gus.at[part], gur.at[part], gu_s, gu_r, (2 * (zz + 1) + y, t))

    def g_down(zz):
        part = pl.ds(0, zz)
        return send(gds.at[part], gdr.at[part], gd_s, gd_r, (2 * (zz - 1) + y, t))

    def g_step(ph):
        @pl.when(z == ph)
        def _():
            if ph:
                g_up(ph - 1).wait_recv()
            for i in range(ph + 1, nz):
                gus[i] = (g_own(i) + gur[i].astype(F32) if ph else g_own(i)).astype(BF16)
            g_up(ph).start()

        top = nz - 1 - ph

        @pl.when(z == top)
        def _():
            if ph:
                g_down(top + 1).wait_recv()
            for i in range(top):
                gds[i] = (g_own(i) + gdr[i].astype(F32) if ph else g_own(i)).astype(BF16)
            g_down(top).start()

    def share(dx, dy, u):
        zz = jnp.where(dx == 1, 1 - x, x)
        yy = jnp.where(dy == 1, 1 - y, y)
        ch, off, num = cuts[u]
        cols = pl.ds(off, num)
        return send(
            pbuf.at[2 * dx + dy, ch, :, cols],
            prcv.at[2 * dx + dy, ch, :, cols],
            ps_s,
            ps_r.at[u],
            (2 * z + yy, 2 * zz + c),
        )

    def rows_in():
        rows_whole().wait_recv()
        relay(c).start()

    def rows_ready():
        send(x_ref, xbuf.at[y, 1 - c], xs_s.at[0], xs_r.at[0], (d, mate)).wait_recv()
        relay(1 - c).wait_recv()

    def columns(yy, u):
        ch, off, num = cuts[u]
        return pl.ds(pl.multiple_of((yy * chunks + ch) * CHUNK + off, 128), num)

    def unit(blk, u):
        ch, off, num = cuts[u]
        cols = pl.ds(off, num)
        own_ks = [k for k in range(pieces) if seg_of(k)[0] == ch and seg_of(k)[2] == off]
        upto = 2 * (max(own_ks) + 1)
        leads = blk is lead

        @pl.when(role_m)
        def _():
            arrive("far_m" if leads else "near", blk, upto)

        if not leads:

            @pl.when(role_2)
            def _():
                arrive("far_2", blk, upto)

        others = jnp.logical_not(role_m) if leads else end
        parts = [(k, cc) for k in own_ks for cc in range(2)]

        def landed(todo):
            for cc in range(2):
                mine = jnp.logical_and(c + 2 * blk == z, c == cc)
                ks = [k for k, core in todo if core == cc]

                if ks:

                    @pl.when(jnp.logical_and(others, jnp.logical_not(mine)))
                    def _():
                        for k in ks:
                            hop(blk, 2 * k + cc, 3, z_in).wait_recv()

        dx = jnp.where(blk == x, 0, 1)

        def put(dy, p):
            if dy == 1:
                pbuf[2 * dx + 1, ch, :, cols] = p.astype(BF16)
                share(dx, 1, u).start()
            else:

                @pl.when(dx == 1)
                def _():
                    pbuf[2, ch, :, cols] = p.astype(BF16)
                    share(1, 0, u).start()

                @pl.when(dx == 0)
                def _():
                    out_ref[:, columns(y, u)] += p

        if leads or u < len(cuts) - 1:
            landed(parts)
            for dy in (1, 0):
                yy = (y + dy) % 2
                p = jnp.dot(xbuf[yy, 0], wbuf[blk, 0, ch, :, cols], preferred_element_type=F32)
                p = p + jnp.dot(xbuf[yy, 1], wbuf[blk, 1, ch, :, cols], preferred_element_type=F32)
                put(dy, p)
            return
        for i, (k, cc) in enumerate(parts):
            landed([(k, cc)])
            seg = seg_of(k)[1]
            for dy in (1, 0):
                yy = (y + dy) % 2
                p = jnp.dot(
                    xbuf[yy, cc, :, seg], wbuf[blk, cc, ch, seg, cols], preferred_element_type=F32
                )
                if i:
                    p = p + acc[dy]
                if i < len(parts) - 1:
                    acc[dy] = p
                else:
                    put(dy, p)

    dp_wait(0, hbuf)
    state = jnp.concatenate([hbuf[i].astype(F32) for i in range(ndp)], axis=0)
    gains = gain_ref[...].astype(F32)
    line = lax.broadcasted_iota(jnp.int32, gains.shape, 0)
    gain = jnp.concatenate(
        [
            jnp.sum(jnp.where(line == d * (width // 128) + i, gains, 0.0), axis=0, keepdims=True)
            for i in range(width // 128)
        ],
        axis=1,
    )
    fetch(2).wait()
    new_k, new_v = [], []
    factor = 1.0 / math.sqrt(HD)

    for step in range(2):
        squares = jnp.sum(state * state, axis=-1, keepdims=True)
        part = exact_dot(state * gain, wqkv_ref[...])
        both = jnp.concatenate([part, jnp.broadcast_to(squares, (ndp * rolls, 128))], axis=1)
        for i in range(ndp):
            qsend[step, i % 2, i // 2] = both[i * rolls : (i + 1) * rolls]
        q_side(step).start()
        pump(1)
        if step == 1:
            lb_chip().wait_recv()
            lbfull[c] = (lbhalf[0] + lbhalf[1]).astype(BF16)
            lb_back(c).start()
        if step == 0:
            send(others, others, ab_s.at[0], ab_r.at[0], (other_y, t)).wait_recv()
            ab_side(y).start()
            dp_wait(1, statbuf)
            tot = statbuf[0]
            for i in range(1, ndp):
                tot = tot + statbuf[i]
            mean = tot[0:1] / GROUP
            std = jnp.sqrt(jnp.maximum(tot[1:2] / GROUP - mean * mean, 0.09))
            fetch(4).wait()
            for r in range(rolls):
                one, rew = ones[r], rew_ref[r]
                live = live_ref[r].astype(F32)
                adv = (rew - jnp.sum(one * mean, axis=1, keepdims=True)) / jnp.sum(
                    one * std, axis=1, keepdims=True
                )
                slot = lax.broadcasted_iota(jnp.int32, (COMP, 1), 0).astype(F32)
                row_w = jnp.where(slot < live, adv / live, 0.0)
                seg = pl.ds(r * COMP, COMP)
                wt_ref[seg, :] = (row_w * up_ref[seg, :].astype(F32)).astype(BF16)
        q_side(step).wait_recv()
        for i in range(nz):
            qline[step, i] = qsend[step, y, i] + qside[step, i]
        for off in range(1, nz):
            zt = (z + off) % nz
            src, dst = qline.at[step, zt], qrecv.at[step, z]
            send(src, dst, qz_s.at[step], qz_r.at[step], (2 * zt + y, t)).start()
        pump(2)
        q_lines(step).wait_recv()
        total = qline[step, z]
        for off in range(1, nz):
            total = total + qrecv[step, (z + off) % nz]
        qkv = total[:, :qkvw] * lax.rsqrt(total[:, qkvw : qkvw + 1] / model + 1e-05)
        new_k.append(qkv[:, HEADS_TP * HD : HEADS_TP * HD + HD])
        new_v.append(qkv[:, HEADS_TP * HD + HD :])
        if step == 0:
            fetch(3).wait()
        heads = []
        for b in range(rolls):
            q = jnp.concatenate(
                [qkv[b : b + 1, h * HD : (h + 1) * HD] for h in range(HEADS_TP)], axis=0
            )
            scores = exact_dot(q, cache_ref[b, :, :HD], NT) * factor
            pos = lax.broadcasted_iota(jnp.int32, scores.shape, 1)
            scores = jnp.where(pos < lens_ref[b], scores, -1e30)
            extra = [
                jnp.sum(q * k[b : b + 1], axis=-1, keepdims=True) * factor for k in new_k
            ]
            top = jnp.max(scores, axis=-1, keepdims=True)
            for e in extra:
                top = jnp.maximum(top, e)
            expo = jnp.exp(scores - top)
            ee = [jnp.exp(e - top) for e in extra]
            den = jnp.sum(expo, axis=-1, keepdims=True)
            for e in ee:
                den = den + e
            att = jnp.dot(
                (expo / den).astype(BF16), cache_ref[b, :, HD:], preferred_element_type=F32
            )
            for e, v in zip(ee, new_v):
                att = att + (e / den).astype(BF16).astype(F32) * v[b : b + 1]
            heads.append(jnp.concatenate([att[h : h + 1] for h in range(HEADS_TP)], axis=1))
        asend[step] = jnp.concatenate(heads, axis=0).astype(BF16)
        for off in range(1, nz):
            zt = (z + off) % nz
            send(
                asend.at[step], arecv.at[step, y, z], az_s.at[step], az_r.at[step], (2 * zt + y, t)
            ).start()
        pump(1)
        arecv[step, y, z] = asend[step]
        if step == 0:
            ab_side(1 - y).wait_recv()
            at, bt = (
                jnp.concatenate([abuf[i % 2, i // 2, k] for i in range(ndp)], axis=1)
                for k in range(2)
            )

            @pl.when(t == src_t)
            def _():
                for j in range(per):
                    bdbuf[j] = abuf[j % 2, (d % half) * (per // 2) + j // 2, 1]
                for off in range(1, ntp):
                    up_block((t + off) % ntp).start()

            for k, (m, v) in enumerate(((at, x_ref), (bt, wt_ref))):
                lb = lax.dot_general(m, v[...], NT, preferred_element_type=F32)
                for i in range(2):
                    lbsend[i, k] = lb[:, i * (rows // 2) : (i + 1) * (rows // 2)]
            lb_core().start()
        else:
            lb_back(c).wait_send()
            lb_back(1 - c).wait_recv()
            low_t, back_t = lanes_of(lbfull.at[:, 0], 2), lanes_of(lbfull.at[:, 1], 2)
            ga = adapter_scale * jnp.dot(back_t, x_ref[...], preferred_element_type=F32)
            gb = adapter_scale * jnp.dot(low_t, wt_ref[...], preferred_element_type=F32)
            for i in range(ndp):
                for k, g in enumerate((ga, gb)):
                    gown[i % 2, i // 2, k] = g[:, i * piece : (i + 1) * piece]
            out_ref[...] = adapter_scale * lax.dot_general(
                low_t, bt, TN, preferred_element_type=F32
            )
        a_lines(step).wait_recv()
        a_side(step, y).start()
        if step == 1:
            g_side().start()
        pump(1)
        a_side(step, 1 - y).wait_recv()
        attended = jnp.concatenate(
            [arecv[step, i % 2, i // 2].astype(F32) for i in range(ndp)], axis=0
        ).astype(BF16)
        usend[step, :, :width] = jnp.dot(attended, wo_ref[...], preferred_element_type=F32)
        usend[step, :, width:] = jnp.concatenate(
            [
                lax.dot_general(attended, at, NT, preferred_element_type=F32),
                jnp.zeros((ndp * rolls, 128 - rank), F32),
            ],
            axis=1,
        )
        tp_start(step, usend.at[step], urecv.at[step])
        pump(2)
        urecv[step, t] = usend[step]
        if step == 0:
            lb_core().wait_recv()
            lbhalf[0] = lbsend[c] + lbhalf[2]
            lb_chip().start()

            @pl.when(t != src_t)
            def _():
                up_block(src_t).wait_recv()

            bd = lanes_of(bdbuf, per)
        tp_wait(step, urecv.at[step])
        upd = urecv[step, 0]
        for i in range(1, ntp):
            upd = upd + urecv[step, i]
        state = state + (
            upd[:, :width] + adapter_scale * exact_dot(upd[:, width : width + rank], bd)
        )

    for i in range(ndp):
        fsend[i] = state[i * rolls : (i + 1) * rolls]
    dp_start(2, lambda p: fsend.at[p], frecv)
    frecv[d] = fsend[d]
    rows_in()
    g_side().wait_recv()
    g_step(0)
    pump(2)
    rows_ready()
    for u in range(len(cuts)):
        unit(lead, u)
        if 0 < u < nz - 1:
            g_step(u)
        pump(2)
    dp_wait(2, frecv)
    for i in range(ndp):
        dec_ref[:, i * width : (i + 1) * width] = frecv[i]
    for cp in sent:
        cp.wait_send()
    while clock[0] < 2 * pieces + pieces // 2:
        pump(1)
    unit(trail, 0)
    pump(ticks)
    unit(trail, 1)
    for u in range(2, len(cuts)):
        unit(trail, u)
    for u in range(len(cuts)):
        ch, off, num = cuts[u]
        three = prcv.at[pl.ds(1, 3), ch, :, pl.ds(off, num)]
        send(three, three, ps_s, ps_r.at[u], (d, mate)).wait_recv()
        for dx, dy in ((1, 0), (0, 1), (1, 1)):
            got = prcv[2 * dx + dy, ch, :, pl.ds(off, num)].astype(F32)
            out_ref[:, columns((y + dy) % 2, u)] += got

    @pl.when(z == 0)
    def _():
        g_down(1).wait_recv()
        gur[0] = jnp.zeros_like(gur[0])

    @pl.when(z == nz - 1)
    def _():
        g_up(nz - 2).wait_recv()
        gdr[nz - 1] = jnp.zeros_like(gdr[0])

    g = g_own(z) + gur[z].astype(F32) + gdr[z].astype(F32)
    ga_ref[...] = g[0]
    gb_ref[...] = g[1]

    def drain(which, full):
        send(full, full, wl_s.at[which], wl_r.at[0, 0, 0], (d, mate)).wait_send()

    @pl.when(z < nz - 1)
    def _():
        drain(0, wbuf.at[0, 0])

    @pl.when(z > 0)
    def _():
        drain(1, wbuf.at[0, 0])

    @pl.when(z % 2 != c)
    def _():
        drain(2, wbuf.at[0, 0])

    @pl.when(role_m)
    def _():
        drain(3, wbuf.at[0])

    @pl.when(jnp.logical_not(end))
    def _():
        drain(4, wbuf.at[0])

    three = pbuf.at[pl.ds(1, 3)]
    send(three, three, ps_s, ps_r.at[0], (d, mate)).wait_send()
    rows_whole().wait_send()
    relay(c).wait_send()
    g_side().wait_send()
    for step in range(2):
        q_side(step).wait_send()
        q_lines(step).wait_send()
        a_side(step, y).wait_send()
        a_lines(step).wait_send()
    lb_core().wait_send()
    lb_chip().wait_send()
    ab_side(y).wait_send()
    for zz in range(nz):

        @pl.when(z == zz)
        def _():
            if zz < nz - 1:
                g_up(zz).wait_send()
            if zz:
                g_down(zz).wait_send()


    @pl.when(t == src_t)
    def _():
        copies = wo_ref.at[pl.ds(0, (ntp - 1) * rank)]
        send(copies, copies, bd_s, bd_r, (d, mate)).wait_send()


def finish_kernel(*refs):
    n = len(refs) // 2
    copies = [pltpu.make_async_copy(refs[i], refs[n + i], refs[-1].at[i]) for i in range(n)]
    for cp in copies:
        cp.start()
    for cp in copies:
        cp.wait()


def fused_shards(
    ndp,
    ntp,
    hidden,
    attention_norm_gain,
    query_key_value_weight,
    key_value_cache,
    cache_fill_lengths,
    output_weight_frozen,
    adapter_down_transposed,
    adapter_up_matrix,
    attention_rows,
    upstream,
    rewards,
    prompt_group_index,
    completion_live_lengths,
):
    rolls, model = hidden.shape
    slots = key_value_cache.shape[1]
    width = model // ndp
    rank, _, piece = adapter_down_transposed.shape
    rows, shard = attention_rows.shape
    qkvw = query_key_value_weight.shape[2]
    feats = output_weight_frozen.shape[1]
    chunks = width // CHUNK
    vm = pl.BlockSpec(memory_space=pltpu.VMEM)
    hbm = pl.BlockSpec(memory_space=pltpu.HBM)
    dma = pltpu.SemaphoreType.DMA
    V = pltpu.VMEM
    dec, out, ga, gb = pl.pallas_call(
        lambda *refs: fused_kernel(ndp, ntp, *refs),
        out_shape=(
            pltpu.VMEM((rolls, model), F32),
            pltpu.VMEM((rows, shard), F32),
            pltpu.VMEM((rank, piece), F32),
            pltpu.VMEM((rank, piece), F32),
        ),
        in_specs=[hbm] * 13,
        out_specs=(vm,) * 4,
        scratch_shapes=[
            V((ndp, rolls, width), BF16),
            V((2, 128), F32),
            V((ndp, rolls, width), BF16),
            V((2, ndp // 2, 2, rank, piece), BF16),
            V((width // piece, rank, piece), BF16),
            V((ndp, 2, 128), F32),
            V((2, 2, ndp // 2, rolls, qkvw + 128), F32),
            V((2, ndp // 2, rolls, qkvw + 128), F32),
            V((2, ndp // 2, rolls, qkvw + 128), F32),
            V((2, ndp // 2, rolls, qkvw + 128), F32),
            V((2, rolls, feats), BF16),
            V((2, 2, ndp // 2, rolls, feats), BF16),
            V((2, ndp * rolls, width + 128), F32),
            V((2, ntp, ndp * rolls, width + 128), F32),
            V((ndp, rolls, width), F32),
            V((ndp, rolls, width), F32),
            V((2, 2, rank, rows // 2), F32),
            V((3, 2, rank, rows // 2), F32),
            V((2, 2, rank, rows // 2), BF16),
            V((2, ndp // 2, 2, rank, piece), F32),
            V((ndp // 2, 2, rank, piece), F32),
            V((ndp // 2, 2, rank, piece), BF16),
            V((ndp // 2, 2, rank, piece), BF16),
            V((ndp // 2, 2, rank, piece), BF16),
            V((ndp // 2, 2, rank, piece), BF16),
            V((rows, shard), BF16),
            V((2, 2, rows, shard), BF16),
            V((2, 2, chunks, feats, CHUNK), BF16),
            V((4, chunks, rows, CHUNK), BF16),
            V((4, chunks, rows, CHUNK), BF16),
            dma((3,)),
            dma((3,)),
            dma((2,)),
            dma((2,)),
            dma,
            dma,
            dma((3,)),
            dma((3,)),
            dma((5,)),
            dma((2, 2, chunks * SEGS)),
            dma,
            dma((chunks - 1 + CHUNK // 128,)),
            dma,
            dma,
            dma,
            dma,
            dma,
            dma,
            dma((3,)),
            dma((3,)),
            dma((2,)),
            dma((2,)),
            V((feats, width), BF16),
            V((rows, shard), BF16),
            V((width, qkvw), BF16),
            V((rolls, slots, 2 * HD), BF16),
            V((rows, shard), BF16),
            dma((13,)),
            V((2, rows, 128), F32),
        ]
        + [dma((2,))] * 8
        + [V((rolls, model), BF16), V((model // 128, 128), BF16)]
        + [V((rank, piece), BF16)] * 2
        + [pltpu.SMEM((rolls,), t) for t in (jnp.int32, F32, jnp.int32, jnp.int32)],
        compiler_params=pltpu.CompilerParams(
            collective_id=0, has_side_effects=True, vmem_limit_bytes=64815104
        ),
    )(
        hidden,
        attention_norm_gain.reshape(model // 128, 128),
        query_key_value_weight[:, 0, :],
        key_value_cache[:, :, 0, :],
        cache_fill_lengths,
        output_weight_frozen[0],
        adapter_down_transposed[:, 0, :],
        adapter_up_matrix[:, 0, :],
        attention_rows,
        upstream,
        rewards,
        prompt_group_index,
        completion_live_lengths,
    )
    parts = (dec, out, ga[:, None, :], gb[:, None, :])
    anywhere = (pl.BlockSpec(memory_space=pl.ANY),) * len(parts)
    return pl.pallas_call(
        finish_kernel,
        out_shape=tuple(jax.ShapeDtypeStruct(p.shape, F32) for p in parts),
        in_specs=[vm] * len(parts),
        out_specs=anywhere,
        scratch_shapes=[dma((len(parts),))],
        compiler_params=pltpu.CompilerParams(vmem_limit_bytes=2**20),
    )(*[pltpu.with_memory_space_constraint(p, pltpu.VMEM) for p in parts])


def shards(
    hidden,
    attention_norm_gain,
    query_key_value_weight,
    key_value_cache,
    cache_fill_lengths,
    output_weight_frozen,
    adapter_down_transposed,
    adapter_up_matrix,
    attention_rows,
    upstream,
    rewards,
    prompt_group_index,
    completion_live_lengths,
):
    a_piece, b_piece = (
        lax.all_gather(adapter_down_transposed, "dp", axis=2, tiled=True),
        lax.all_gather(adapter_up_matrix, "dp", axis=2, tiled=True),
    )
    b_whole = lax.all_gather(b_piece, "tp", axis=1, tiled=True)
    up_matrix_flat = b_whole.reshape(b_whole.shape[0], -1).astype(jnp.float32)
    a_local = a_piece[:, 0, :]
    up_matrix_columns = b_piece[:, 0, :]
    w_rows = query_key_value_weight[:, 0, :].astype(jnp.float32)
    w_cols = output_weight_frozen[0]
    query_width = HEADS_TP * HD
    local_rolls = hidden.shape[0]
    decode_state = hidden.astype(jnp.float32)
    keys_new = []
    values_new = []
    for step in range(2):
        normed = rms_norm(decode_state, attention_norm_gain)
        spread = lax.all_to_all(normed, "dp", split_axis=1, concat_axis=0, tiled=True)
        partial_value = jnp.dot(spread, w_rows, precision=lax.Precision.HIGHEST)
        qkv = lax.psum_scatter(partial_value, "dp", scatter_dimension=0, tiled=True)
        query = qkv[:, :query_width].reshape(local_rolls, HEADS_TP, HD)
        keys_new.append(qkv[:, query_width : query_width + HD])
        values_new.append(qkv[:, query_width + HD :])
        attended = attend(
            query,
            key_value_cache[:, :, 0, :],
            cache_fill_lengths,
            jnp.stack(keys_new, axis=1),
            jnp.stack(values_new, axis=1),
        )
        columns = jnp.dot(
            lax.all_gather(attended, "dp", axis=0, tiled=True),
            w_cols,
            preferred_element_type=jnp.float32,
        )
        returned_values = lax.all_to_all(columns, "dp", split_axis=0, concat_axis=1, tiled=True)
        low_rank_decode = jnp.dot(attended, a_local.T, preferred_element_type=jnp.float32)
        state_update = returned_values + adapter_scale * jnp.dot(
            low_rank_decode, up_matrix_flat, precision=lax.Precision.HIGHEST
        )
        decode_state = decode_state + lax.psum(state_update, "tp")
    groups = local_rolls * lax.axis_size("dp") // GROUP
    onehot = (prompt_group_index[:, None] == jnp.arange(groups, dtype=jnp.int32)[None, :]).astype(
        jnp.float32
    )
    totals, squares = lax.psum(
        (
            jnp.sum(onehot * rewards[:, None], axis=0),
            jnp.sum(onehot * (rewards * rewards)[:, None], axis=0),
        ),
        "dp",
    )
    mean = totals / GROUP
    std = jnp.sqrt(jnp.maximum(squares / GROUP - mean * mean, 0.09))
    advantage = (rewards - jnp.sum(onehot * mean[None, :], axis=1)) / jnp.sum(
        onehot * std[None, :], axis=1
    )
    per_roll = advantage / completion_live_lengths.astype(jnp.float32)
    rows = attention_rows.shape[0]
    slot = jnp.arange(rows, dtype=jnp.int32) % COMP
    limit = jnp.repeat(completion_live_lengths, COMP)
    row_w = jnp.where(slot < limit, jnp.repeat(per_roll, COMP), 0.0)
    whole_rows = jnp.dot(
        attention_rows,
        lax.all_gather(output_weight_frozen, "dp", axis=2, tiled=True)[0],
        preferred_element_type=jnp.float32,
    )
    frozen_output_rows = lax.psum_scatter(whole_rows, "tp", scatter_dimension=1, tiled=True)
    low_sum = lax.psum(jnp.dot(attention_rows, a_local.T, preferred_element_type=jnp.float32), "tp")
    low_rank_rows = low_sum.astype(jnp.bfloat16)
    adapted_output_rows = frozen_output_rows + adapter_scale * jnp.dot(
        low_rank_rows, up_matrix_columns, preferred_element_type=jnp.float32
    )
    advantage_weighted = (row_w[:, None] * upstream.astype(jnp.float32)).astype(jnp.bfloat16)
    backward_result = lax.psum(
        jnp.dot(advantage_weighted, up_matrix_columns.T, preferred_element_type=jnp.float32), "tp"
    ).astype(jnp.bfloat16)
    down_gradient = adapter_scale * lax.dot_general(
        backward_result,
        attention_rows,
        (((0,), (0,)), ((), ())),
        preferred_element_type=jnp.float32,
    )
    up_gradient = adapter_scale * lax.dot_general(
        low_rank_rows,
        advantage_weighted,
        (((0,), (0,)), ((), ())),
        preferred_element_type=jnp.float32,
    )
    grad_a_part, grad_b_part = (
        lax.psum_scatter(down_gradient[:, None, :], "dp", scatter_dimension=2, tiled=True),
        lax.psum_scatter(up_gradient[:, None, :], "dp", scatter_dimension=2, tiled=True),
    )
    return (decode_state, adapted_output_rows, grad_a_part, grad_b_part)


def solution(mesh):
    placed = (
        P("dp", None),
        P(),
        P("dp", "tp", None),
        P("dp", None, "tp", None),
        P("dp"),
        P("tp", None, "dp"),
        P(None, "tp", "dp"),
        P(None, "tp", "dp"),
        P("dp", "tp"),
        P("dp", "tp"),
        P("dp"),
        P("dp"),
        P("dp"),
    )
    ndp, ntp = mesh.shape["dp"], mesh.shape["tp"]

    def body(*args):
        width = args[5].shape[2]
        piece = args[6].shape[2]
        if ntp == 4 and ndp == 8 and piece % 128 == 0 and width % CHUNK == 0:
            return fused_shards(ndp, ntp, *args)
        return shards(*args)

    return jax.shard_map(
        body,
        mesh=mesh,
        in_specs=placed,
        out_specs=(P("dp", None), P("dp", "tp"), P(None, "tp", "dp"), P(None, "tp", "dp")),
        check_vma=False,
    )
```

```python
import math

import jax
import jax.numpy as jnp
from jax import lax
from jax.experimental import pallas as pl
from jax.experimental.pallas import tpu as pltpu
from jax.sharding import PartitionSpec as P

HD = 128
HEADS_TP = 8
GROUP = 4
COMP = 256


adapter_scale = 2.0


def rms_norm(decode_state, gain):
    scale = lax.rsqrt(jnp.mean(decode_state * decode_state, axis=-1, keepdims=True) + 1e-05)
    return decode_state * scale * gain.astype(jnp.float32)


def attend(query, cache, lengths, new_keys, new_values):
    head = query.shape[-1]
    slots = cache.shape[1]
    factor = 1.0 / math.sqrt(head)
    keys = cache[:, :, :head].astype(jnp.float32)
    values = cache[:, :, head:]
    scores = jnp.einsum("bhd,bcd->bhc", query, keys, precision=lax.Precision.HIGHEST) * factor
    valid = jnp.arange(slots, dtype=jnp.int32)[None, None, :] < lengths[:, None, None]
    scores = jnp.where(valid, scores, -1e30)
    extra = jnp.einsum("bhd,bed->bhe", query, new_keys, precision=lax.Precision.HIGHEST) * factor
    joined = jnp.concatenate([scores, extra], axis=-1)
    top = jnp.max(joined, axis=-1, keepdims=True)
    expo = jnp.exp(joined - top)
    probs = (expo / jnp.sum(expo, axis=-1, keepdims=True)).astype(jnp.bfloat16)
    out = jnp.einsum("bhc,bcd->bhd", probs[..., :slots], values, preferred_element_type=jnp.float32)
    out = out + jnp.einsum(
        "bhe,bed->bhd",
        probs[..., slots:].astype(jnp.float32),
        new_values,
        precision=lax.Precision.HIGHEST,
    )
    return out.astype(jnp.bfloat16).reshape(query.shape[0], -1)


MESH = pl.DeviceIdType.MESH
F32 = jnp.float32
BF16 = jnp.bfloat16
NT = (((1,), (1,)), ((), ()))
TN = (((0,), (0,)), ((), ()))
CHUNK = 256
SEGS = 4
ROW_PARTS = 8


def split3(v):
    hi = v.astype(BF16)
    rest = v - hi.astype(F32)
    mid = rest.astype(BF16)
    lo = (rest - mid.astype(F32)).astype(BF16)
    return jnp.concatenate([hi, mid, lo], axis=0)


def exact_dot(v, w, dims=(((1,), (0,)), ((), ()))):
    n = v.shape[0]
    r = lax.dot_general(split3(v), w, dims, preferred_element_type=F32)
    return r[:n] + r[n : 2 * n] + r[2 * n :]


def rows_of(ref, n):
    return jnp.concatenate([ref[i] for i in range(n)], axis=0)


def lanes_of(ref, n):
    return jnp.concatenate([ref[i] for i in range(n)], axis=1)


def fused_kernel(
    ndp,
    ntp,
    h_in,
    gain_in,
    wqkv_in,
    cache_in,
    lens_in,
    wo_in,
    a_in,
    b_in,
    x_in,
    up_in,
    rew_in,
    idx_in,
    live_in,
    dec_ref,
    out_ref,
    ga_ref,
    gb_ref,
    hsend,
    stats_ref,
    hbuf,
    abuf,
    bdbuf,
    statbuf,
    qsend,
    qside,
    qline,
    qrecv,
    asend,
    arecv,
    usend,
    urecv,
    fsend,
    frecv,
    lbsend,
    lbhalf,
    lbfull,
    gown,
    grecv,
    gus,
    gur,
    gds,
    gdr,
    wt_ref,
    xbuf,
    wbuf,
    pbuf,
    prcv,
    ds_s,
    ds_r,
    ts_s,
    ts_r,
    bd_s,
    bd_r,
    xs_s,
    xs_r,
    wl_s,
    wl_r,
    ps_s,
    ps_r,
    gy_s,
    gy_r,
    gu_s,
    gu_r,
    gd_s,
    gd_r,
    lb_s,
    lb_r,
    ab_s,
    ab_r,
    wo_ref,
    x_ref,
    wqkv_ref,
    cache_ref,
    up_ref,
    in_s,
    acc,
    qy_s,
    qy_r,
    qz_s,
    qz_r,
    ay_s,
    ay_r,
    az_s,
    az_r,
    h_ref,
    gain_ref,
    a_ref,
    b_ref,
    lens_ref,
    rew_ref,
    idx_ref,
    live_ref,
):
    d = lax.axis_index("dp")
    t = lax.axis_index("tp")
    z, y = d // 2, d % 2
    x, c = t // 2, t % 2
    nz = ndp // 2
    rolls, model = h_ref.shape
    width = model // ndp
    rank = a_ref.shape[0]
    piece = a_ref.shape[1]
    chunks = wo_ref.shape[1] // CHUNK
    qkvw = wqkv_ref.shape[1]
    rows = x_ref.shape[0]
    mate = 2 * x + (1 - c)
    other_y = 2 * z + (1 - y)

    def fetch(k):
        src, dst = (
            (wo_in, wo_ref),
            (x_in, x_ref),
            (wqkv_in, wqkv_ref),
            (cache_in, cache_ref),
            (up_in, up_ref),
            (h_in, h_ref),
            (a_in, a_ref),
            (b_in, b_ref),
            (idx_in, idx_ref),
            (rew_in, rew_ref),
            (gain_in, gain_ref),
            (live_in, live_ref),
            (lens_in, lens_ref),
        )[k]
        return pltpu.make_async_copy(src, dst, in_s.at[k])

    barrier = pltpu.get_barrier_semaphore()
    for i in range(ndp):
        for j in range(ntp):
            if i or j:
                pl.semaphore_signal(
                    barrier,
                    inc=1,
                    device_id=((d + i) % ndp, (t + j) % ntp),
                    device_id_type=MESH,
                )
    for k in (5, 6, 7, 8, 9, 0, 1, 2, 3, 4, 10, 11, 12):
        fetch(k).start()
    pl.semaphore_wait(barrier, ndp * ntp - 1)
    for k in (5, 6, 7, 8, 9, 10, 11, 12):
        fetch(k).wait()

    sent = []

    def send(src, dst, s, r, dev):
        cp = pltpu.make_async_remote_copy(
            src_ref=src, dst_ref=dst, send_sem=s, recv_sem=r, device_id=dev, device_id_type=MESH
        )
        return cp

    def dp_start(e, src, dst):
        for off in range(1, ndp):
            peer = (d + off) % ndp
            send(src(peer), dst.at[d], ds_s.at[e], ds_r.at[e], (peer, t)).start()
        whole = dst.at[pl.ds(0, ndp - 1)]
        sent.append(send(whole, whole, ds_s.at[e], ds_r.at[e], (d, (t + 1) % ntp)))

    def dp_wait(e, dst):
        whole = dst.at[pl.ds(0, ndp - 1)]
        send(whole, whole, ds_s.at[e], ds_r.at[e], (d, (t + 1) % ntp)).wait_recv()

    def tp_start(e, src, dst):
        for off in range(1, ntp):
            peer = (t + off) % ntp
            send(src, dst.at[t], ts_s.at[e], ts_r.at[e], (d, peer)).start()
        whole = dst.at[pl.ds(0, ntp - 1)]
        sent.append(send(whole, whole, ts_s.at[e], ts_r.at[e], (d, (t + 1) % ntp)))

    def tp_wait(e, dst):
        whole = dst.at[pl.ds(0, ntp - 1)]
        send(whole, whole, ts_s.at[e], ts_r.at[e], (d, (t + 1) % ntp)).wait_recv()

    for i in range(ndp):
        hsend[i] = h_ref[:, i * width : (i + 1) * width]
    lane = lax.broadcasted_iota(jnp.int32, (1, 128), 1)
    ones = [jnp.where(lane == idx_ref[r], 1.0, 0.0) for r in range(rolls)]
    stats_ref[...] = jnp.zeros_like(stats_ref)
    for r in range(rolls):
        stats_ref[0:1] += ones[r] * rew_ref[r]
        stats_ref[1:2] += ones[r] * (rew_ref[r] * rew_ref[r])

    dp_start(0, lambda p: hsend.at[p], hbuf)
    hbuf[d] = hsend[d]
    abuf[y, z, 0] = a_ref[...]
    abuf[y, z, 1] = b_ref[...]
    for k, ref in enumerate((a_ref, b_ref)):
        for off in range(1, nz):
            peer = 2 * ((z + off) % nz) + y
            send(ref, abuf.at[y, z, k], ab_s.at[0], ab_r.at[0], (peer, t)).start()
    others = abuf.at[0, pl.ds(0, nz - 1)]
    sent.append(send(others, others, ab_s.at[0], ab_r.at[0], (other_y, t)))
    dp_start(1, lambda p: stats_ref, statbuf)
    statbuf[d] = stats_ref[...]
    per = width // piece
    half = ndp // per
    src_t = d // half

    def up_block(tj):
        return send(bdbuf, bdbuf, bd_s, bd_r, (d, tj))

    fetch(0).wait()
    fetch(1).wait()
    xcp = send(x_ref, xbuf.at[y, c], xs_s.at[0], xs_r.at[0], (d, mate))
    xcp.start()
    sent.append(xcp)
    xbuf[y, c] = x_ref[...]

    def row_send(k):
        part = rows // ROW_PARTS
        if k >= ROW_PARTS:
            return
        seg = pl.ds(k * part, part)
        send(
            x_ref.at[seg], xbuf.at[y, c, seg], xs_s.at[1], xs_r.at[1], (other_y, t)
        ).start()

    def rows_whole():
        return send(x_ref, xbuf.at[1 - y, c], xs_s.at[1], xs_r.at[1], (other_y, t))

    def relay(dst_core):
        return send(
            xbuf.at[1 - y, c], xbuf.at[1 - y, dst_core], xs_s.at[2], xs_r.at[2], (d, mate)
        )

    feats = wo_ref.shape[0]
    pieces = chunks * SEGS
    near, far = z // 2, 1 - z // 2
    end = jnp.logical_or(z == 0, z == nz - 1)
    role_m = jnp.logical_and(jnp.logical_not(end), c == z // 2)
    role_2 = jnp.logical_and(jnp.logical_not(end), c != z // 2)
    lead = jnp.where(c == near, far, near)
    trail = 1 - lead
    z_up, z_dn = jnp.minimum(z + 1, nz - 1), jnp.maximum(z - 1, 0)
    z_in = jnp.where(z < 2, z_up, z_dn)
    z_out = jnp.where(z < 2, z_dn, z_up)

    cuts = [(ch, 0, CHUNK) for ch in range(chunks - 1)]
    cuts += [(chunks - 1, h * 128, 128) for h in range(CHUNK // 128)]

    def seg_of(k):
        ch, part = k // SEGS, k % SEGS
        if ch < chunks - 1:
            size = feats // SEGS
            return ch, pl.ds(part * size, size), 0, CHUNK
        halves = CHUNK // 128
        size = feats * halves // SEGS
        per_half = SEGS // halves
        return ch, pl.ds((part % per_half) * size, size), (part // per_half) * 128, 128

    def own(k, which, zt):
        ch, seg, off, num = seg_of(k)
        return send(
            wo_ref.at[seg, pl.ds(ch * CHUNK + off, num)],
            wbuf.at[z // 2, c, ch, seg, pl.ds(off, num)],
            wl_s.at[which],
            wl_r.at[z // 2, c, k],
            (2 * zt + y, 2 * x + z % 2),
        )

    def hop(blk, j, which, zt):
        k, cc = j // 2, j % 2
        ch, seg, off, num = seg_of(k)
        ref = wbuf.at[blk, cc, ch, seg, pl.ds(off, num)]
        return send(ref, ref, wl_s.at[which], wl_r.at[blk, cc, k], (2 * zt + y, t))

    def own_tick(k):
        @pl.when(z < nz - 1)
        def _():
            own(k, 0, z_up).start()

        @pl.when(z > 0)
        def _():
            own(k, 1, z_dn).start()

        @pl.when(z % 2 != c)
        def _():
            own(k, 2, z).start()

    waited = {"near": 0, "far_m": 0, "far_2": 0}

    def arrive(name, blk, upto):
        for j in range(waited[name], upto):
            hop(blk, j, 3, z_in).wait_recv()
        waited[name] = max(waited[name], upto)

    def relay_tick(name, blk, lo, hi, which, zt):
        hi = min(hi, 2 * pieces)
        arrive(name, blk, hi)
        for j in range(lo, hi):
            hop(blk, j, which, zt).start()

    clock = [0]
    ticks = 3 * pieces - 2

    def tick():
        n = clock[0]
        if n >= ticks:
            return
        clock[0] += 1
        if n < pieces:
            own_tick(n)
            row_send(n)
            return
        m = n - pieces

        @pl.when(role_m)
        def _():
            if m < pieces:
                relay_tick("near", near, 2 * m, 2 * m + 2, 3, z_in)
                relay_tick("far_m", far, 2 * m, 2 * m + 2, 4, z_out)

        if m >= pieces - 2:

            @pl.when(role_2)
            def _():
                relay_tick("far_2", far, 2 * (m - pieces + 2), 2 * (m - pieces + 2) + 2, 4, z_out)

    def pump(n):
        for _ in range(n):
            tick()

    pump(2)

    @pl.when(z % 2 == c)
    def _():
        for ch in range(chunks):
            wbuf[z // 2, c, ch] = wo_ref[:, ch * CHUNK : (ch + 1) * CHUNK]

    def q_side(step):
        return send(qsend.at[step, 1 - y], qside.at[step], qy_s.at[step], qy_r.at[step], (other_y, t))

    def q_lines(step):
        whole = qrecv.at[step, pl.ds(0, nz - 1)]
        return send(whole, whole, qz_s.at[step], qz_r.at[step], (other_y, t))

    def a_side(step, yy):
        ref = arecv.at[step, yy]
        return send(ref, ref, ay_s.at[step], ay_r.at[step], (other_y, t))

    def a_lines(step):
        whole = arecv.at[step, 0, pl.ds(0, nz - 1)]
        return send(whole, whole, az_s.at[step], az_r.at[step], (other_y, t))

    def ab_side(yy):
        return send(abuf.at[yy], abuf.at[yy], ab_s.at[1], ab_r.at[1], (other_y, t))

    def lb_core():
        return send(lbsend.at[1 - c], lbhalf.at[2], lb_s.at[0], lb_r.at[0], (d, mate))

    def lb_chip():
        return send(lbhalf.at[0], lbhalf.at[1], lb_s.at[1], lb_r.at[1], (d, 2 * (1 - x) + c))

    def lb_back(core):
        return send(lbfull.at[core], lbfull.at[core], lb_s.at[2], lb_r.at[2], (d, mate))

    def g_side():
        return send(gown.at[1 - y], grecv, gy_s, gy_r, (other_y, t))

    def g_own(i):
        return gown[y, i] + grecv[i]

    def g_up(zz):
        part = pl.ds(zz + 1, nz - 1 - zz)
        return send(gus.at[part], gur.at[part], gu_s, gu_r, (2 * (zz + 1) + y, t))

    def g_down(zz):
        part = pl.ds(0, zz)
        return send(gds.at[part], gdr.at[part], gd_s, gd_r, (2 * (zz - 1) + y, t))

    def g_step(ph):
        @pl.when(z == ph)
        def _():
            if ph:
                g_up(ph - 1).wait_recv()
            for i in range(ph + 1, nz):
                gus[i] = (g_own(i) + gur[i].astype(F32) if ph else g_own(i)).astype(BF16)
            g_up(ph).start()

        top = nz - 1 - ph

        @pl.when(z == top)
        def _():
            if ph:
                g_down(top + 1).wait_recv()
            for i in range(top):
                gds[i] = (g_own(i) + gdr[i].astype(F32) if ph else g_own(i)).astype(BF16)
            g_down(top).start()

    def share(dx, dy, u):
        zz = jnp.where(dx == 1, 1 - x, x)
        yy = jnp.where(dy == 1, 1 - y, y)
        ch, off, num = cuts[u]
        cols = pl.ds(off, num)
        return send(
            pbuf.at[2 * dx + dy, ch, :, cols],
            prcv.at[2 * dx + dy, ch, :, cols],
            ps_s,
            ps_r.at[u],
            (2 * z + yy, 2 * zz + c),
        )

    def rows_in():
        rows_whole().wait_recv()
        relay(c).start()

    def rows_ready():
        send(x_ref, xbuf.at[y, 1 - c], xs_s.at[0], xs_r.at[0], (d, mate)).wait_recv()
        relay(1 - c).wait_recv()

    def columns(yy, u):
        ch, off, num = cuts[u]
        return pl.ds(pl.multiple_of((yy * chunks + ch) * CHUNK + off, 128), num)

    def unit(blk, u):
        ch, off, num = cuts[u]
        cols = pl.ds(off, num)
        own_ks = [k for k in range(pieces) if seg_of(k)[0] == ch and seg_of(k)[2] == off]
        upto = 2 * (max(own_ks) + 1)
        leads = blk is lead

        @pl.when(role_m)
        def _():
            arrive("far_m" if leads else "near", blk, upto)

        if not leads:

            @pl.when(role_2)
            def _():
                arrive("far_2", blk, upto)

        others = jnp.logical_not(role_m) if leads else end
        parts = [(k, cc) for k in own_ks for cc in range(2)]

        def landed(todo):
            for cc in range(2):
                mine = jnp.logical_and(c + 2 * blk == z, c == cc)
                ks = [k for k, core in todo if core == cc]

                if ks:

                    @pl.when(jnp.logical_and(others, jnp.logical_not(mine)))
                    def _():
                        for k in ks:
                            hop(blk, 2 * k + cc, 3, z_in).wait_recv()

        dx = jnp.where(blk == x, 0, 1)

        def put(dy, p):
            if dy == 1:
                pbuf[2 * dx + 1, ch, :, cols] = p.astype(BF16)
                share(dx, 1, u).start()
            else:

                @pl.when(dx == 1)
                def _():
                    pbuf[2, ch, :, cols] = p.astype(BF16)
                    share(1, 0, u).start()

                @pl.when(dx == 0)
                def _():
                    out_ref[:, columns(y, u)] += p

        if leads or u < len(cuts) - 1:
            landed(parts)
            for dy in (1, 0):
                yy = (y + dy) % 2
                p = jnp.dot(xbuf[yy, 0], wbuf[blk, 0, ch, :, cols], preferred_element_type=F32)
                p = p + jnp.dot(xbuf[yy, 1], wbuf[blk, 1, ch, :, cols], preferred_element_type=F32)
                put(dy, p)
            return
        for i, (k, cc) in enumerate(parts):
            landed([(k, cc)])
            seg = seg_of(k)[1]
            for dy in (1, 0):
                yy = (y + dy) % 2
                p = jnp.dot(
                    xbuf[yy, cc, :, seg], wbuf[blk, cc, ch, seg, cols], preferred_element_type=F32
                )
                if i:
                    p = p + acc[dy]
                if i < len(parts) - 1:
                    acc[dy] = p
                else:
                    put(dy, p)

    dp_wait(0, hbuf)
    state = jnp.concatenate([hbuf[i].astype(F32) for i in range(ndp)], axis=0)
    gains = gain_ref[...].astype(F32)
    line = lax.broadcasted_iota(jnp.int32, gains.shape, 0)
    gain = jnp.concatenate(
        [
            jnp.sum(jnp.where(line == d * (width // 128) + i, gains, 0.0), axis=0, keepdims=True)
            for i in range(width // 128)
        ],
        axis=1,
    )
    fetch(2).wait()
    new_k, new_v = [], []
    factor = 1.0 / math.sqrt(HD)

    for step in range(2):
        squares = jnp.sum(state * state, axis=-1, keepdims=True)
        part = exact_dot(state * gain, wqkv_ref[...])
        both = jnp.concatenate([part, jnp.broadcast_to(squares, (ndp * rolls, 128))], axis=1)
        for i in range(ndp):
            qsend[step, i % 2, i // 2] = both[i * rolls : (i + 1) * rolls]
        q_side(step).start()
        pump(1)
        if step == 1:
            lb_chip().wait_recv()
            lbfull[c] = (lbhalf[0] + lbhalf[1]).astype(BF16)
            lb_back(c).start()
        if step == 0:
            send(others, others, ab_s.at[0], ab_r.at[0], (other_y, t)).wait_recv()
            ab_side(y).start()
            dp_wait(1, statbuf)
            tot = statbuf[0]
            for i in range(1, ndp):
                tot = tot + statbuf[i]
            mean = tot[0:1] / GROUP
            std = jnp.sqrt(jnp.maximum(tot[1:2] / GROUP - mean * mean, 0.09))
            fetch(4).wait()
            for r in range(rolls):
                one, rew = ones[r], rew_ref[r]
                live = live_ref[r].astype(F32)
                adv = (rew - jnp.sum(one * mean, axis=1, keepdims=True)) / jnp.sum(
                    one * std, axis=1, keepdims=True
                )
                slot = lax.broadcasted_iota(jnp.int32, (COMP, 1), 0).astype(F32)
                row_w = jnp.where(slot < live, adv / live, 0.0)
                seg = pl.ds(r * COMP, COMP)
                wt_ref[seg, :] = (row_w * up_ref[seg, :].astype(F32)).astype(BF16)
        q_side(step).wait_recv()
        for i in range(nz):
            qline[step, i] = qsend[step, y, i] + qside[step, i]
        for off in range(1, nz):
            zt = (z + off) % nz
            src, dst = qline.at[step, zt], qrecv.at[step, z]
            send(src, dst, qz_s.at[step], qz_r.at[step], (2 * zt + y, t)).start()
        pump(2)
        q_lines(step).wait_recv()
        total = qline[step, z]
        for off in range(1, nz):
            total = total + qrecv[step, (z + off) % nz]
        qkv = total[:, :qkvw] * lax.rsqrt(total[:, qkvw : qkvw + 1] / model + 1e-05)
        new_k.append(qkv[:, HEADS_TP * HD : HEADS_TP * HD + HD])
        new_v.append(qkv[:, HEADS_TP * HD + HD :])
        if step == 0:
            fetch(3).wait()
        heads = []
        for b in range(rolls):
            q = jnp.concatenate(
                [qkv[b : b + 1, h * HD : (h + 1) * HD] for h in range(HEADS_TP)], axis=0
            )
            scores = exact_dot(q, cache_ref[b, :, :HD], NT) * factor
            pos = lax.broadcasted_iota(jnp.int32, scores.shape, 1)
            scores = jnp.where(pos < lens_ref[b], scores, -1e30)
            extra = [
                jnp.sum(q * k[b : b + 1], axis=-1, keepdims=True) * factor for k in new_k
            ]
            top = jnp.max(scores, axis=-1, keepdims=True)
            for e in extra:
                top = jnp.maximum(top, e)
            expo = jnp.exp(scores - top)
            ee = [jnp.exp(e - top) for e in extra]
            den = jnp.sum(expo, axis=-1, keepdims=True)
            for e in ee:
                den = den + e
            att = jnp.dot(
                (expo / den).astype(BF16), cache_ref[b, :, HD:], preferred_element_type=F32
            )
            for e, v in zip(ee, new_v):
                att = att + (e / den).astype(BF16).astype(F32) * v[b : b + 1]
            heads.append(jnp.concatenate([att[h : h + 1] for h in range(HEADS_TP)], axis=1))
        asend[step] = jnp.concatenate(heads, axis=0).astype(BF16)
        for off in range(1, nz):
            zt = (z + off) % nz
            send(
                asend.at[step], arecv.at[step, y, z], az_s.at[step], az_r.at[step], (2 * zt + y, t)
            ).start()
        pump(1)
        arecv[step, y, z] = asend[step]
        if step == 0:
            ab_side(1 - y).wait_recv()
            at, bt = (
                jnp.concatenate([abuf[i % 2, i // 2, k] for i in range(ndp)], axis=1)
                for k in range(2)
            )

            @pl.when(t == src_t)
            def _():
                for j in range(per):
                    bdbuf[j] = abuf[j % 2, (d % half) * (per // 2) + j // 2, 1]
                for off in range(1, ntp):
                    up_block((t + off) % ntp).start()

            for k, (m, v) in enumerate(((at, x_ref), (bt, wt_ref))):
                lb = lax.dot_general(m, v[...], NT, preferred_element_type=F32)
                for i in range(2):
                    lbsend[i, k] = lb[:, i * (rows // 2) : (i + 1) * (rows // 2)]
            lb_core().start()
        else:
            lb_back(c).wait_send()
            lb_back(1 - c).wait_recv()
            low_t, back_t = lanes_of(lbfull.at[:, 0], 2), lanes_of(lbfull.at[:, 1], 2)
            ga = adapter_scale * jnp.dot(back_t, x_ref[...], preferred_element_type=F32)
            gb = adapter_scale * jnp.dot(low_t, wt_ref[...], preferred_element_type=F32)
            for i in range(ndp):
                for k, g in enumerate((ga, gb)):
                    gown[i % 2, i // 2, k] = g[:, i * piece : (i + 1) * piece]
            out_ref[...] = adapter_scale * lax.dot_general(
                low_t, bt, TN, preferred_element_type=F32
            )
        a_lines(step).wait_recv()
        a_side(step, y).start()
        if step == 1:
            g_side().start()
        pump(1)
        a_side(step, 1 - y).wait_recv()
        attended = jnp.concatenate(
            [arecv[step, i % 2, i // 2].astype(F32) for i in range(ndp)], axis=0
        ).astype(BF16)
        usend[step, :, :width] = jnp.dot(attended, wo_ref[...], preferred_element_type=F32)
        usend[step, :, width:] = jnp.concatenate(
            [
                lax.dot_general(attended, at, NT, preferred_element_type=F32),
                jnp.zeros((ndp * rolls, 128 - rank), F32),
            ],
            axis=1,
        )
        tp_start(step, usend.at[step], urecv.at[step])
        pump(2)
        urecv[step, t] = usend[step]
        if step == 0:
            lb_core().wait_recv()
            lbhalf[0] = lbsend[c] + lbhalf[2]
            lb_chip().start()

            @pl.when(t != src_t)
            def _():
                up_block(src_t).wait_recv()

            bd = lanes_of(bdbuf, per)
        tp_wait(step, urecv.at[step])
        upd = urecv[step, 0]
        for i in range(1, ntp):
            upd = upd + urecv[step, i]
        state = state + (
            upd[:, :width] + adapter_scale * exact_dot(upd[:, width : width + rank], bd)
        )

    for i in range(ndp):
        fsend[i] = state[i * rolls : (i + 1) * rolls]
    dp_start(2, lambda p: fsend.at[p], frecv)
    frecv[d] = fsend[d]
    rows_in()
    g_side().wait_recv()
    g_step(0)
    pump(2)
    rows_ready()
    for u in range(len(cuts)):
        unit(lead, u)
        if 0 < u < nz - 1:
            g_step(u)
        pump(2)
    dp_wait(2, frecv)
    for i in range(ndp):
        dec_ref[:, i * width : (i + 1) * width] = frecv[i]
    for cp in sent:
        cp.wait_send()
    while clock[0] < 2 * pieces + pieces // 2 - 2:
        pump(1)
    unit(trail, 0)
    pump(ticks)
    unit(trail, 1)
    for u in range(2, len(cuts)):
        unit(trail, u)
    for u in range(len(cuts)):
        ch, off, num = cuts[u]
        three = prcv.at[pl.ds(1, 3), ch, :, pl.ds(off, num)]
        send(three, three, ps_s, ps_r.at[u], (d, mate)).wait_recv()
        for dx, dy in ((1, 0), (0, 1), (1, 1)):
            got = prcv[2 * dx + dy, ch, :, pl.ds(off, num)].astype(F32)
            out_ref[:, columns((y + dy) % 2, u)] += got

    @pl.when(z == 0)
    def _():
        g_down(1).wait_recv()
        gur[0] = jnp.zeros_like(gur[0])

    @pl.when(z == nz - 1)
    def _():
        g_up(nz - 2).wait_recv()
        gdr[nz - 1] = jnp.zeros_like(gdr[0])

    g = g_own(z) + gur[z].astype(F32) + gdr[z].astype(F32)
    ga_ref[...] = g[0]
    gb_ref[...] = g[1]

    def drain(which, full):
        send(full, full, wl_s.at[which], wl_r.at[0, 0, 0], (d, mate)).wait_send()

    @pl.when(z < nz - 1)
    def _():
        drain(0, wbuf.at[0, 0])

    @pl.when(z > 0)
    def _():
        drain(1, wbuf.at[0, 0])

    @pl.when(z % 2 != c)
    def _():
        drain(2, wbuf.at[0, 0])

    @pl.when(role_m)
    def _():
        drain(3, wbuf.at[0])

    @pl.when(jnp.logical_not(end))
    def _():
        drain(4, wbuf.at[0])

    three = pbuf.at[pl.ds(1, 3)]
    send(three, three, ps_s, ps_r.at[0], (d, mate)).wait_send()
    rows_whole().wait_send()
    relay(c).wait_send()
    g_side().wait_send()
    for step in range(2):
        q_side(step).wait_send()
        q_lines(step).wait_send()
        a_side(step, y).wait_send()
        a_lines(step).wait_send()
    lb_core().wait_send()
    lb_chip().wait_send()
    ab_side(y).wait_send()
    for zz in range(nz):

        @pl.when(z == zz)
        def _():
            if zz < nz - 1:
                g_up(zz).wait_send()
            if zz:
                g_down(zz).wait_send()


    @pl.when(t == src_t)
    def _():
        copies = wo_ref.at[pl.ds(0, (ntp - 1) * rank)]
        send(copies, copies, bd_s, bd_r, (d, mate)).wait_send()


def finish_kernel(*refs):
    n = len(refs) // 2
    copies = [pltpu.make_async_copy(refs[i], refs[n + i], refs[-1].at[i]) for i in range(n)]
    for cp in copies:
        cp.start()
    for cp in copies:
        cp.wait()


def fused_shards(
    ndp,
    ntp,
    hidden,
    attention_norm_gain,
    query_key_value_weight,
    key_value_cache,
    cache_fill_lengths,
    output_weight_frozen,
    adapter_down_transposed,
    adapter_up_matrix,
    attention_rows,
    upstream,
    rewards,
    prompt_group_index,
    completion_live_lengths,
):
    rolls, model = hidden.shape
    slots = key_value_cache.shape[1]
    width = model // ndp
    rank, _, piece = adapter_down_transposed.shape
    rows, shard = attention_rows.shape
    qkvw = query_key_value_weight.shape[2]
    feats = output_weight_frozen.shape[1]
    chunks = width // CHUNK
    vm = pl.BlockSpec(memory_space=pltpu.VMEM)
    hbm = pl.BlockSpec(memory_space=pltpu.HBM)
    dma = pltpu.SemaphoreType.DMA
    V = pltpu.VMEM
    dec, out, ga, gb = pl.pallas_call(
        lambda *refs: fused_kernel(ndp, ntp, *refs),
        out_shape=(
            pltpu.VMEM((rolls, model), F32),
            pltpu.VMEM((rows, shard), F32),
            pltpu.VMEM((rank, piece), F32),
            pltpu.VMEM((rank, piece), F32),
        ),
        in_specs=[hbm] * 13,
        out_specs=(vm,) * 4,
        scratch_shapes=[
            V((ndp, rolls, width), BF16),
            V((2, 128), F32),
            V((ndp, rolls, width), BF16),
            V((2, ndp // 2, 2, rank, piece), BF16),
            V((width // piece, rank, piece), BF16),
            V((ndp, 2, 128), F32),
            V((2, 2, ndp // 2, rolls, qkvw + 128), F32),
            V((2, ndp // 2, rolls, qkvw + 128), F32),
            V((2, ndp // 2, rolls, qkvw + 128), F32),
            V((2, ndp // 2, rolls, qkvw + 128), F32),
            V((2, rolls, feats), BF16),
            V((2, 2, ndp // 2, rolls, feats), BF16),
            V((2, ndp * rolls, width + 128), F32),
            V((2, ntp, ndp * rolls, width + 128), F32),
            V((ndp, rolls, width), F32),
            V((ndp, rolls, width), F32),
            V((2, 2, rank, rows // 2), F32),
            V((3, 2, rank, rows // 2), F32),
            V((2, 2, rank, rows // 2), BF16),
            V((2, ndp // 2, 2, rank, piece), F32),
            V((ndp // 2, 2, rank, piece), F32),
            V((ndp // 2, 2, rank, piece), BF16),
            V((ndp // 2, 2, rank, piece), BF16),
            V((ndp // 2, 2, rank, piece), BF16),
            V((ndp // 2, 2, rank, piece), BF16),
            V((rows, shard), BF16),
            V((2, 2, rows, shard), BF16),
            V((2, 2, chunks, feats, CHUNK), BF16),
            V((4, chunks, rows, CHUNK), BF16),
            V((4, chunks, rows, CHUNK), BF16),
            dma((3,)),
            dma((3,)),
            dma((2,)),
            dma((2,)),
            dma,
            dma,
            dma((3,)),
            dma((3,)),
            dma((5,)),
            dma((2, 2, chunks * SEGS)),
            dma,
            dma((chunks - 1 + CHUNK // 128,)),
            dma,
            dma,
            dma,
            dma,
            dma,
            dma,
            dma((3,)),
            dma((3,)),
            dma((2,)),
            dma((2,)),
            V((feats, width), BF16),
            V((rows, shard), BF16),
            V((width, qkvw), BF16),
            V((rolls, slots, 2 * HD), BF16),
            V((rows, shard), BF16),
            dma((13,)),
            V((2, rows, 128), F32),
        ]
        + [dma((2,))] * 8
        + [V((rolls, model), BF16), V((model // 128, 128), BF16)]
        + [V((rank, piece), BF16)] * 2
        + [pltpu.SMEM((rolls,), t) for t in (jnp.int32, F32, jnp.int32, jnp.int32)],
        compiler_params=pltpu.CompilerParams(
            collective_id=0, has_side_effects=True, vmem_limit_bytes=64815104
        ),
    )(
        hidden,
        attention_norm_gain.reshape(model // 128, 128),
        query_key_value_weight[:, 0, :],
        key_value_cache[:, :, 0, :],
        cache_fill_lengths,
        output_weight_frozen[0],
        adapter_down_transposed[:, 0, :],
        adapter_up_matrix[:, 0, :],
        attention_rows,
        upstream,
        rewards,
        prompt_group_index,
        completion_live_lengths,
    )
    parts = (dec, out, ga[:, None, :], gb[:, None, :])
    anywhere = (pl.BlockSpec(memory_space=pl.ANY),) * len(parts)
    return pl.pallas_call(
        finish_kernel,
        out_shape=tuple(jax.ShapeDtypeStruct(p.shape, F32) for p in parts),
        in_specs=[vm] * len(parts),
        out_specs=anywhere,
        scratch_shapes=[dma((len(parts),))],
        compiler_params=pltpu.CompilerParams(vmem_limit_bytes=2**20),
    )(*[pltpu.with_memory_space_constraint(p, pltpu.VMEM) for p in parts])


def shards(
    hidden,
    attention_norm_gain,
    query_key_value_weight,
    key_value_cache,
    cache_fill_lengths,
    output_weight_frozen,
    adapter_down_transposed,
    adapter_up_matrix,
    attention_rows,
    upstream,
    rewards,
    prompt_group_index,
    completion_live_lengths,
):
    a_piece, b_piece = (
        lax.all_gather(adapter_down_transposed, "dp", axis=2, tiled=True),
        lax.all_gather(adapter_up_matrix, "dp", axis=2, tiled=True),
    )
    b_whole = lax.all_gather(b_piece, "tp", axis=1, tiled=True)
    up_matrix_flat = b_whole.reshape(b_whole.shape[0], -1).astype(jnp.float32)
    a_local = a_piece[:, 0, :]
    up_matrix_columns = b_piece[:, 0, :]
    w_rows = query_key_value_weight[:, 0, :].astype(jnp.float32)
    w_cols = output_weight_frozen[0]
    query_width = HEADS_TP * HD
    local_rolls = hidden.shape[0]
    decode_state = hidden.astype(jnp.float32)
    keys_new = []
    values_new = []
    for step in range(2):
        normed = rms_norm(decode_state, attention_norm_gain)
        spread = lax.all_to_all(normed, "dp", split_axis=1, concat_axis=0, tiled=True)
        partial_value = jnp.dot(spread, w_rows, precision=lax.Precision.HIGHEST)
        qkv = lax.psum_scatter(partial_value, "dp", scatter_dimension=0, tiled=True)
        query = qkv[:, :query_width].reshape(local_rolls, HEADS_TP, HD)
        keys_new.append(qkv[:, query_width : query_width + HD])
        values_new.append(qkv[:, query_width + HD :])
        attended = attend(
            query,
            key_value_cache[:, :, 0, :],
            cache_fill_lengths,
            jnp.stack(keys_new, axis=1),
            jnp.stack(values_new, axis=1),
        )
        columns = jnp.dot(
            lax.all_gather(attended, "dp", axis=0, tiled=True),
            w_cols,
            preferred_element_type=jnp.float32,
        )
        returned_values = lax.all_to_all(columns, "dp", split_axis=0, concat_axis=1, tiled=True)
        low_rank_decode = jnp.dot(attended, a_local.T, preferred_element_type=jnp.float32)
        state_update = returned_values + adapter_scale * jnp.dot(
            low_rank_decode, up_matrix_flat, precision=lax.Precision.HIGHEST
        )
        decode_state = decode_state + lax.psum(state_update, "tp")
    groups = local_rolls * lax.axis_size("dp") // GROUP
    onehot = (prompt_group_index[:, None] == jnp.arange(groups, dtype=jnp.int32)[None, :]).astype(
        jnp.float32
    )
    totals, squares = lax.psum(
        (
            jnp.sum(onehot * rewards[:, None], axis=0),
            jnp.sum(onehot * (rewards * rewards)[:, None], axis=0),
        ),
        "dp",
    )
    mean = totals / GROUP
    std = jnp.sqrt(jnp.maximum(squares / GROUP - mean * mean, 0.09))
    advantage = (rewards - jnp.sum(onehot * mean[None, :], axis=1)) / jnp.sum(
        onehot * std[None, :], axis=1
    )
    per_roll = advantage / completion_live_lengths.astype(jnp.float32)
    rows = attention_rows.shape[0]
    slot = jnp.arange(rows, dtype=jnp.int32) % COMP
    limit = jnp.repeat(completion_live_lengths, COMP)
    row_w = jnp.where(slot < limit, jnp.repeat(per_roll, COMP), 0.0)
    whole_rows = jnp.dot(
        attention_rows,
        lax.all_gather(output_weight_frozen, "dp", axis=2, tiled=True)[0],
        preferred_element_type=jnp.float32,
    )
    frozen_output_rows = lax.psum_scatter(whole_rows, "tp", scatter_dimension=1, tiled=True)
    low_sum = lax.psum(jnp.dot(attention_rows, a_local.T, preferred_element_type=jnp.float32), "tp")
    low_rank_rows = low_sum.astype(jnp.bfloat16)
    adapted_output_rows = frozen_output_rows + adapter_scale * jnp.dot(
        low_rank_rows, up_matrix_columns, preferred_element_type=jnp.float32
    )
    advantage_weighted = (row_w[:, None] * upstream.astype(jnp.float32)).astype(jnp.bfloat16)
    backward_result = lax.psum(
        jnp.dot(advantage_weighted, up_matrix_columns.T, preferred_element_type=jnp.float32), "tp"
    ).astype(jnp.bfloat16)
    down_gradient = adapter_scale * lax.dot_general(
        backward_result,
        attention_rows,
        (((0,), (0,)), ((), ())),
        preferred_element_type=jnp.float32,
    )
    up_gradient = adapter_scale * lax.dot_general(
        low_rank_rows,
        advantage_weighted,
        (((0,), (0,)), ((), ())),
        preferred_element_type=jnp.float32,
    )
    grad_a_part, grad_b_part = (
        lax.psum_scatter(down_gradient[:, None, :], "dp", scatter_dimension=2, tiled=True),
        lax.psum_scatter(up_gradient[:, None, :], "dp", scatter_dimension=2, tiled=True),
    )
    return (decode_state, adapted_output_rows, grad_a_part, grad_b_part)


def solution(mesh):
    placed = (
        P("dp", None),
        P(),
        P("dp", "tp", None),
        P("dp", None, "tp", None),
        P("dp"),
        P("tp", None, "dp"),
        P(None, "tp", "dp"),
        P(None, "tp", "dp"),
        P("dp", "tp"),
        P("dp", "tp"),
        P("dp"),
        P("dp"),
        P("dp"),
    )
    ndp, ntp = mesh.shape["dp"], mesh.shape["tp"]

    def body(*args):
        width = args[5].shape[2]
        piece = args[6].shape[2]
        if ntp == 4 and ndp == 8 and piece % 128 == 0 and width % CHUNK == 0:
            return fused_shards(ndp, ntp, *args)
        return shards(*args)

    return jax.shard_map(
        body,
        mesh=mesh,
        in_specs=placed,
        out_specs=(P("dp", None), P("dp", "tp"), P(None, "tp", "dp"), P(None, "tp", "dp")),
        check_vma=False,
    )
```
